512 devices in a mesh: ctx: 32 (over z, y_hi), heads: 16 (over y_lo, x, core).
Axes of the slice: x: 4, y: 8 (y_hi: 4, y_lo: 2; y = y_hi * 2 + y_lo), z: 8, core: 2. Of those that a mesh axis runs over, the one named last changes fastest.
Arguments:
- resid_in: bfloat16 [4096, 5376], P('ctx', 'heads'), may hold values from -6 to 6
- first_layer_queries: bfloat16 [4096, 4096], P('ctx', 'heads'), may hold values from -270 to 270
- first_layer_keys: bfloat16 [4096, 2048], P('ctx', 'heads'), may hold values from -7 to 7
- first_layer_values: bfloat16 [4096, 2048], P('ctx', 'heads'), may hold values from -6 to 6
- out_one: bfloat16 [4096, 5376], P('heads'), may hold values from -6 to 6
- post_gain: float32 [5376], replicated, may hold values from 0.1 to 1.9
- pre_gain: float32 [5376], replicated, may hold values from 0.1 to 1.9
- proj_query: bfloat16 [5376, 4096], P('ctx', 'heads'), may hold values from -30 to 30
- key_projection: bfloat16 [5376, 2048], P('ctx', 'heads'), may hold values from -1 to 1
- value_projection: bfloat16 [5376, 2048], P('ctx', 'heads'), may hold values from -0.078125 to 0.078125
- window: int32 [32], P('heads'), may hold values from 512 to 1024, as said below
- positions: int32 [4096], replicated, may hold values from 0 to 2047, as said below
Outputs:
- resid_out: bfloat16 [4096, 5376], P('ctx', 'heads')
- attended: bfloat16 [4096, 4096], P('ctx', 'heads')
The draws below stay inside these ranges and needn't reach their ends.
Inputs may be any that keep to these rules, and one draw needn't show every extreme that they name: Each query head's window counts back from and includes its own token; some head's window is exactly 1024. `positions`: tokens form three packed documents: a position is 0 at a document's first token and one more than the previous token's otherwise; one document has exactly 2048 tokens and none has more.
All inputs are finite; a program needn't handle non-finite values.
Results may differ from the reference program's by a relative error of at most 0.03.
Values may be sent and summed in bfloat16 or wider, within the bound.
No kernel may reach another device: no remote copies, remote signals or barrier semaphores. Data moves between devices by JAX's collectives and lax.ppermute only.
A program may use at most 64 MiB of HBM per device.

```python
import math
import jax
import jax.numpy as jnp
from jax import lax

MODEL_WIDTH = 5376
QUERY_HEAD_COUNT = 32
KEY_VALUE_HEADS = 16
HEAD_SIZE = 128
LONGEST_WINDOW = 1024
TOK_DEV = 128
SEQUENCE_TOKENS = 4096
N_CTX = 32
N_HEADS = 16


def clipped_normal(key, shape):
    return jax.random.truncated_normal(key, -6.0, 6.0, shape, jnp.float32)


def first_keys_full(key):
    base_value = clipped_normal(jax.random.fold_in(key, 101), (SEQUENCE_TOKENS, KEY_VALUE_HEADS * HEAD_SIZE))
    return base_value


def second_keys_full(key):
    return clipped_normal(jax.random.fold_in(key, 201), (MODEL_WIDTH, KEY_VALUE_HEADS * HEAD_SIZE)) / jnp.sqrt(jnp.float32(MODEL_WIDTH))


def draw_first_layer_keys(key, part):
    return first_keys_full(key).astype(jnp.bfloat16)


def draw_first_layer_queries(key, part):
    drawn = clipped_normal(jax.random.fold_in(key, 103), (SEQUENCE_TOKENS, QUERY_HEAD_COUNT * HEAD_SIZE))
    return drawn.astype(jnp.bfloat16)


def draw_out_one(key, part):
    drawn = clipped_normal(jax.random.fold_in(key, 105), (QUERY_HEAD_COUNT * HEAD_SIZE, MODEL_WIDTH)) / jnp.sqrt(jnp.float32(QUERY_HEAD_COUNT * HEAD_SIZE))
    column = jnp.arange(MODEL_WIDTH, dtype=jnp.float32) / MODEL_WIDTH
    ramp = jnp.power(3.0, column)
    return (drawn * ramp[None, :]).astype(jnp.bfloat16)


def draw_key_projection(key, part):
    return second_keys_full(key).astype(jnp.bfloat16)


def draw_proj_query(key, part):
    drawn = clipped_normal(jax.random.fold_in(key, 202), (MODEL_WIDTH, QUERY_HEAD_COUNT * HEAD_SIZE)) / jnp.sqrt(jnp.float32(MODEL_WIDTH))
    return drawn.astype(jnp.bfloat16)


def draw_window(key, part):
    widths = jax.random.randint(jax.random.fold_in(key, 301), (QUERY_HEAD_COUNT,), LONGEST_WINDOW // 2, LONGEST_WINDOW + 1)
    chosen = jax.random.randint(jax.random.fold_in(key, 302), (), 0, QUERY_HEAD_COUNT)
    return jnp.where(jnp.arange(QUERY_HEAD_COUNT) == chosen, LONGEST_WINDOW, widths).astype(jnp.int32)


def draw_positions(key, part):
    half_seq = SEQUENCE_TOKENS // 2
    first_cut = jax.random.randint(jax.random.fold_in(key, 401), (), 1, half_seq).astype(jnp.int32)
    cuts = jnp.stack([first_cut, first_cut + half_seq])
    row_ids = jnp.arange(SEQUENCE_TOKENS, dtype=jnp.int32)
    starts = jnp.max(jnp.where(cuts[None, :] <= row_ids[:, None], cuts[None, :], 0), axis=1)
    return (row_ids - starts).astype(jnp.int32)


def block_levels(own_key, extent, shards, least, high):
    def one(dim, blocks):
        draws = jax.random.uniform(jax.random.fold_in(jax.random.fold_in(own_key, 6), dim), (blocks,), jnp.float32, least / len(shards), high / len(shards))
        return jnp.repeat(jnp.exp(draws), extent[dim] // blocks).reshape((-1,) + (1,) * (len(extent) - dim - 1))

    factor_of = one(*shards[0])
    for cut in shards[1:]:
        factor_of = factor_of * one(*cut)
    return factor_of


def noise(rng, extent, scale, reach, shards=(), held_as=jnp.bfloat16):
    values = jax.random.normal(rng, extent, jnp.float32) * scale
    if len(shards) > 0:
        values = block_levels(rng, extent, shards, -0.22, 0.18) * values
    return jnp.clip(values, min=-reach, max=reach).astype(held_as)


def setup_inputs(seed: int = 0) -> dict:
    key_of = jax.random.split(jax.random.key(seed), 13)
    return {
        "resid_in": noise(key_of[0], (SEQUENCE_TOKENS, MODEL_WIDTH), 1.0, 6.0, ((0, 32), (1, 16))),
        "first_layer_queries": draw_first_layer_queries(jax.random.fold_in(key_of[12], 71), 0),
        "first_layer_keys": draw_first_layer_keys(jax.random.fold_in(key_of[12], 71), 0),
        "first_layer_values": noise(key_of[3], (SEQUENCE_TOKENS, KEY_VALUE_HEADS * HEAD_SIZE), 1.0, 6.0, ((0, 32), (1, 16))),
        "out_one": draw_out_one(jax.random.fold_in(key_of[12], 71), 0),
        "post_gain": jnp.clip(1.0 + 0.18 * jax.random.normal(key_of[5], (MODEL_WIDTH,), jnp.float32), 0.1, 1.9),
        "pre_gain": jnp.clip(1.0 + 0.18 * jax.random.normal(key_of[6], (MODEL_WIDTH,), jnp.float32), 0.1, 1.9),
        "proj_query": draw_proj_query(jax.random.fold_in(key_of[12], 71), 0),
        "key_projection": draw_key_projection(jax.random.fold_in(key_of[12], 71), 0),
        "value_projection": noise(key_of[9], (MODEL_WIDTH, KEY_VALUE_HEADS * HEAD_SIZE), MODEL_WIDTH ** -0.5, 0.078125, ((0, 32), (1, 16))),
        "window": draw_window(jax.random.fold_in(key_of[12], 71), 0),
        "positions": draw_positions(jax.random.fold_in(key_of[12], 71), 0),
    }


SCALE = 168.0 ** (-0.5)
EPS = 1e-06
THETA = 1000000.0
POSITION_FACTOR = 0.125

def apply_rotary(values, pos_rows, factor):
    half_dim = values.shape[-1] // 2
    speeds = THETA ** (-(jnp.arange(half_dim, dtype=jnp.float32) * 2.0 / values.shape[-1]))
    angles = (pos_rows.astype(jnp.float32) * factor)[:, None] * speeds[None, :]
    cosine = jnp.cos(angles)[:, None, :]
    sine_part = jnp.sin(angles)[:, None, :]
    front_half = values[..., :half_dim]
    back_half = values[..., half_dim:]
    return jnp.concatenate([front_half * cosine - back_half * sine_part, back_half * cosine + front_half * sine_part], axis=-1)

def masked_attention(query_row_block, key_row_block, value_row_block, query_tok, key_tok, query_pos, key_pos, window_limits):
    scores = jnp.einsum('qagd,kad->qagk', query_row_block.astype(jnp.float32), key_row_block.astype(jnp.float32)) * SCALE
    distance = query_tok[:, None] - key_tok[None, :]
    base_ok = (distance >= 0) & (key_tok[None, :] >= 0) & (query_pos[:, None] - key_pos[None, :] == distance)
    visible = base_ok[:, None, None, :] & (distance[:, None, None, :] < window_limits[None, :, :, None])
    row_peak = lax.optimization_barrier(jnp.max(jnp.where(visible, scores, -1e+30), axis=-1, keepdims=True))
    lifted = jnp.where(visible, jnp.exp(scores - row_peak), 0.0)
    row_total = lax.optimization_barrier(jnp.sum(lifted, axis=-1))
    weights = lifted.astype(jnp.bfloat16)
    mixed = jnp.einsum('qagk,kad->qagd', weights.astype(jnp.float32), value_row_block.astype(jnp.float32))
    return (mixed / row_total[..., None]).astype(jnp.bfloat16)

def reference(resid_in, first_layer_queries, first_layer_keys, first_layer_values, out_one, post_gain, pre_gain, proj_query, key_projection, value_projection, window, positions):
    token_sequence = resid_in.shape[0]
    group_length = QUERY_HEAD_COUNT // KEY_VALUE_HEADS
    tokens_all = jnp.arange(token_sequence, dtype=jnp.int32)
    rows_per_block = math.gcd(token_sequence, 512)
    padded_keys = jnp.concatenate([jnp.zeros((LONGEST_WINDOW, KEY_VALUE_HEADS * HEAD_SIZE), jnp.bfloat16), first_layer_keys], axis=0)
    padded_values = jnp.concatenate([jnp.zeros((LONGEST_WINDOW, KEY_VALUE_HEADS * HEAD_SIZE), jnp.bfloat16), first_layer_values], axis=0)
    tok_pad = jnp.arange(-LONGEST_WINDOW, token_sequence, dtype=jnp.int32)
    pos_pad = jnp.concatenate([jnp.zeros((LONGEST_WINDOW,), jnp.int32), positions], axis=0)
    window_limits = window.reshape(KEY_VALUE_HEADS, group_length)

    def layer_one_block(start_index):
        query_row_block = lax.dynamic_slice_in_dim(first_layer_queries, start_index, rows_per_block, 0).reshape(rows_per_block, KEY_VALUE_HEADS, group_length, HEAD_SIZE)
        key_row_block = lax.dynamic_slice_in_dim(padded_keys, start_index, rows_per_block + LONGEST_WINDOW, 0).reshape(rows_per_block + LONGEST_WINDOW, KEY_VALUE_HEADS, HEAD_SIZE)
        value_row_block = lax.dynamic_slice_in_dim(padded_values, start_index, rows_per_block + LONGEST_WINDOW, 0).reshape(rows_per_block + LONGEST_WINDOW, KEY_VALUE_HEADS, HEAD_SIZE)
        key_tok = lax.dynamic_slice_in_dim(tok_pad, start_index, rows_per_block + LONGEST_WINDOW, 0)
        key_pos = lax.dynamic_slice_in_dim(pos_pad, start_index, rows_per_block + LONGEST_WINDOW, 0)
        query_tok = start_index + jnp.arange(rows_per_block, dtype=jnp.int32)
        query_pos = lax.dynamic_slice_in_dim(positions, start_index, rows_per_block, 0)
        result = masked_attention(query_row_block, key_row_block, value_row_block, query_tok, key_tok, query_pos, key_pos, window_limits)
        return result.reshape(rows_per_block, QUERY_HEAD_COUNT * HEAD_SIZE)
    block_starts = jnp.arange(0, token_sequence, rows_per_block, dtype=jnp.int32)
    attend_one = lax.map(layer_one_block, block_starts).reshape(token_sequence, QUERY_HEAD_COUNT * HEAD_SIZE)
    group_cols = QUERY_HEAD_COUNT * HEAD_SIZE // N_HEADS

    def add_group(index, combined):
        index = jnp.asarray(index).astype(jnp.int32)
        columns = lax.dynamic_slice_in_dim(attend_one, index * group_cols, group_cols, 1)
        rows_out = lax.dynamic_slice_in_dim(out_one, index * group_cols, group_cols, 0)
        term = jnp.dot(columns, rows_out, preferred_element_type=jnp.float32).astype(jnp.bfloat16)
        term = lax.optimization_barrier(term)
        return combined + term.astype(jnp.float32)
    combined = lax.fori_loop(0, N_HEADS, add_group, jnp.zeros((token_sequence, MODEL_WIDTH), jnp.float32))
    post_scaled = combined * lax.rsqrt(lax.optimization_barrier(jnp.mean(combined * combined, axis=1, keepdims=True)) + EPS)
    resid_out = (resid_in.astype(jnp.float32) + post_gain[None, :] * post_scaled).astype(jnp.bfloat16)
    residual_rows = resid_out.astype(jnp.float32)
    normalized_rows = (pre_gain[None, :] * residual_rows * lax.rsqrt(lax.optimization_barrier(jnp.mean(residual_rows * residual_rows, axis=1, keepdims=True)) + EPS)).astype(jnp.bfloat16)
    second_layer_query = jnp.dot(normalized_rows, proj_query, preferred_element_type=jnp.float32).reshape(token_sequence, QUERY_HEAD_COUNT, HEAD_SIZE)
    second_layer_query = apply_rotary(second_layer_query, positions, POSITION_FACTOR).astype(jnp.bfloat16).reshape(token_sequence, KEY_VALUE_HEADS, group_length, HEAD_SIZE)
    second_layer_key = jnp.dot(normalized_rows, key_projection, preferred_element_type=jnp.float32).reshape(token_sequence, KEY_VALUE_HEADS, HEAD_SIZE)
    second_layer_key = apply_rotary(second_layer_key, positions, POSITION_FACTOR).astype(jnp.bfloat16)
    second_layer_value = jnp.dot(normalized_rows, value_projection, preferred_element_type=jnp.float32).astype(jnp.bfloat16).reshape(token_sequence, KEY_VALUE_HEADS, HEAD_SIZE)
    widened_limits = jnp.full((KEY_VALUE_HEADS, group_length), token_sequence + 1, jnp.int32)
    query_block = math.gcd(token_sequence, 128)

    def layer_two_block(start_index):
        query_row_block = lax.dynamic_slice_in_dim(second_layer_query, start_index, query_block, 0)
        query_tok = start_index + jnp.arange(query_block, dtype=jnp.int32)
        query_pos = lax.dynamic_slice_in_dim(positions, start_index, query_block, 0)
        result = masked_attention(query_row_block, second_layer_key, second_layer_value, query_tok, tokens_all, query_pos, positions, widened_limits)
        return result.reshape(query_block, QUERY_HEAD_COUNT * HEAD_SIZE)
    two_starts = jnp.arange(0, token_sequence, query_block, dtype=jnp.int32)
    attended_tok = lax.map(layer_two_block, two_starts).reshape(token_sequence, QUERY_HEAD_COUNT * HEAD_SIZE)
    half_rows = TOK_DEV // 2
    device_of = tokens_all // TOK_DEV
    local_row = tokens_all % TOK_DEV
    order = jnp.where(local_row < half_rows, 2 * device_of * half_rows + local_row, (2 * N_CTX - 1 - 2 * device_of) * half_rows + local_row - half_rows).astype(jnp.int32)
    attended = jnp.take(attended_tok, order, axis=0)
    return (resid_out, attended)
```

```python
from functools import partial

import jax
import jax.numpy as jnp
from jax import lax
from jax.experimental import pallas as pl
from jax.experimental.pallas import tpu as pltpu
from jax.sharding import PartitionSpec as P

HEAD_SIZE = 128
SCALE = 168.0 ** (-0.5)
EPS = 1e-06
THETA = 1000000.0
POSITION_FACTOR = 0.125
N_CTX = 32
N_HEADS = 16
Y_HI = 4
Z = 8
TOK = 128
HALF = 64
WIDTH = 5376
COLS = WIDTH // N_HEADS
SLAB = 5760
ROWS = TOK // N_HEADS
NEG = -1e30
Y_GROUPS = [[z * Y_HI + y for y in range(Y_HI)] for z in range(Z)]
Z_GROUPS = [[z * Y_HI + y for z in range(Z)] for y in range(Y_HI)]
VMEM_LIMIT = 48 * 1024 * 1024


def whole(memory_space=pltpu.VMEM):
    return pl.BlockSpec(memory_space=memory_space)


def fold_max(peak, part):
    for lane in range(0, part.shape[1], 128):
        peak = jnp.maximum(peak, part[:, lane : lane + 128])
    return peak


def fold_sum(total, part):
    for lane in range(0, part.shape[1], 128):
        total = total + part[:, lane : lane + 128]
    return total


def softmax_rows(query, chunks, low, high, scores):
    rows = query.shape[0]
    peak = jnp.full((rows, 128), NEG, jnp.float32)
    offset = 0
    for load, tokens in chunks:
        keys, _ = load()
        part = (
            lax.dot_general(
                query, keys, (((1,), (1,)), ((), ())), preferred_element_type=jnp.float32
            )
            * SCALE
        )
        width = part.shape[1]
        seen = (tokens >= low) & (tokens <= high)
        part = jnp.where(seen, part, NEG)
        scores[:, offset : offset + width] = part
        peak = fold_max(peak, part)
        offset += width
    top = jnp.max(peak, axis=1, keepdims=True)
    total = jnp.zeros((rows, 128), jnp.float32)
    mixed = jnp.zeros((rows, HEAD_SIZE), jnp.float32)
    offset = 0
    for load, tokens in chunks:
        _, values = load()
        width = values.shape[0]
        lifted = jnp.exp(scores[:, offset : offset + width] - top)
        total = fold_sum(total, lifted)
        mixed = mixed + jnp.dot(
            lifted.astype(jnp.bfloat16), values, preferred_element_type=jnp.float32
        )
        offset += width
    return mixed / jnp.sum(total, axis=1, keepdims=True)


def first_kernel(base, query, blocks, last, low, out_one, resid, sent, scores):
    place_z, place_y = base[0], base[1]
    start = (place_z * Y_HI + place_y) * TOK
    stacked = jnp.concatenate([query[:, :HEAD_SIZE], query[:, HEAD_SIZE:]], axis=0)
    lowest = low[...][:, :1]
    row = lax.broadcasted_iota(jnp.int32, (2 * TOK, 1), 0)
    high = start + lax.rem(row, TOK)
    lane = lax.broadcasted_iota(jnp.int32, (1, 2 * TOK), 1)
    pair = jnp.where(lane < TOK, lane, lane - (TOK + Y_HI * TOK))
    chunks = []
    for peer in range(Y_HI):
        newer = (place_z - jnp.where(peer > place_y, 1, 0)) * (Y_HI * TOK) + peer * TOK
        chunks.append(
            (
                lambda peer=peer: (
                    blocks[peer, :, :HEAD_SIZE],
                    blocks[peer, :, HEAD_SIZE:],
                ),
                newer + pair,
            )
        )
    chunks.append(
        (
            lambda: (last[:, :HEAD_SIZE], last[:, HEAD_SIZE:]),
            start - 2 * Y_HI * TOK + lane[:, :TOK],
        )
    )
    mixed = softmax_rows(stacked, chunks, lowest, high, scores).astype(jnp.bfloat16)
    attend = jnp.concatenate([mixed[:TOK], mixed[TOK:]], axis=1)
    step = 768
    for col in range(0, WIDTH, step):
        part = jnp.dot(attend, out_one[:, col : col + step], preferred_element_type=jnp.float32)
        sent[:, :, col : col + step] = part.reshape(N_HEADS, ROWS, step).astype(jnp.bfloat16)
    own = resid[...].astype(jnp.float32).reshape(N_HEADS, ROWS, COLS)
    sent[:, :, WIDTH : WIDTH + COLS] = own.astype(jnp.bfloat16)
    sent[:, :, WIDTH + COLS :] = jnp.zeros((N_HEADS, ROWS, SLAB - WIDTH - COLS), jnp.bfloat16)


def norm_kernel(got, post_gain, pre_gain, sent, rows, wide):
    combined = got[0, :, :WIDTH].astype(jnp.float32)
    for peer in range(1, N_HEADS):
        combined = combined + got[peer, :, :WIDTH].astype(jnp.float32)
    for peer in range(N_HEADS):
        rows[:, peer * COLS : (peer + 1) * COLS] = got[peer, :, WIDTH : WIDTH + COLS].astype(
            jnp.float32
        )
    scale = lax.rsqrt(jnp.mean(combined * combined, axis=1, keepdims=True) + EPS)
    resid = (rows[...] + post_gain[...] * (combined * scale)).astype(jnp.bfloat16)
    widened = resid.astype(jnp.float32)
    scale = lax.rsqrt(jnp.mean(widened * widened, axis=1, keepdims=True) + EPS)
    normed = (pre_gain[...] * widened * scale).astype(jnp.bfloat16)
    wide[...] = widened
    for peer in range(N_HEADS):
        sent[peer, :, :WIDTH] = normed
        sent[peer, :, WIDTH : WIDTH + COLS] = wide[:, peer * COLS : (peer + 1) * COLS].astype(
            jnp.bfloat16
        )
        sent[peer, :, WIDTH + COLS :] = jnp.zeros((ROWS, SLAB - WIDTH - COLS), jnp.bfloat16)


def project_kernel(got, weights, turn_cos, turn_sin, query, pair, total):
    step = pl.program_id(0)

    @pl.when(step == 0)
    def _():
        total[...] = jnp.zeros_like(total)

    rows = got[...].astype(jnp.float32).reshape(TOK, got.shape[2]).astype(jnp.bfloat16)
    total[...] += jnp.dot(rows, weights[...], preferred_element_type=jnp.float32)

    @pl.when(step == pl.num_programs(0) - 1)
    def _():
        for head in range(4):
            values = total[:, head * HEAD_SIZE : (head + 1) * HEAD_SIZE]
            if head < 3:
                values = values * turn_cos[...] + pltpu.roll(values, HALF, 1) * turn_sin[...]
            values = values.astype(jnp.bfloat16)
            if head < 2:
                query[:, head * HEAD_SIZE : (head + 1) * HEAD_SIZE] = values
            else:
                pair[:, (head - 2) * HEAD_SIZE : (head - 1) * HEAD_SIZE] = values


SPAN = 2304
CHUNK = 256


def second_kernel(base, query, pair, low, out, scores):
    for part in range(2):
        first = base[part]
        begin = jnp.clip(lax.div(first, TOK) * TOK + TOK - SPAN, 0, N_CTX * TOK - SPAN)
        begin = pl.multiple_of(begin, TOK)
        block = query[part * HALF : (part + 1) * HALF, :]
        stacked = jnp.concatenate([block[:, :HEAD_SIZE], block[:, HEAD_SIZE:]], axis=0)
        lowest = low[part * TOK : (part + 1) * TOK, :1]
        row = lax.broadcasted_iota(jnp.int32, (TOK, 1), 0)
        high = first + lax.rem(row, HALF)
        lane = lax.broadcasted_iota(jnp.int32, (1, CHUNK), 1)
        chunks = []
        for index in range(SPAN // CHUNK):
            at = pl.multiple_of(begin + index * CHUNK, TOK)
            chunks.append(
                (
                    lambda at=at: (
                        pair[pl.ds(at, CHUNK), :HEAD_SIZE],
                        pair[pl.ds(at, CHUNK), HEAD_SIZE:],
                    ),
                    at + lane,
                )
            )
        mixed = softmax_rows(stacked, chunks, lowest, high, scores).astype(jnp.bfloat16)
        out[part * HALF : (part + 1) * HALF, :] = jnp.concatenate(
            [mixed[:HALF], mixed[HALF:]], axis=1
        )


def exchange_heads(value):
    return lax.all_to_all(value, "heads", 0, 0, tiled=True)


def ctx_shift(value, steps):
    return lax.ppermute(value, "ctx", [(i, (i + steps) % N_CTX) for i in range(N_CTX)])


def shards(
    resid_in,
    first_layer_queries,
    first_layer_keys,
    first_layer_values,
    out_one,
    post_gain,
    pre_gain,
    proj_query,
    key_projection,
    value_projection,
    window,
    positions,
):
    ctx_place = lax.axis_index("ctx").astype(jnp.int32)
    place_z, place_y = ctx_place // Y_HI, ctx_place % Y_HI
    bf16, f32 = jnp.bfloat16, jnp.float32
    params = partial(pltpu.CompilerParams, vmem_limit_bytes=VMEM_LIMIT)

    weights = lax.all_gather(
        jnp.concatenate([proj_query, key_projection, value_projection], axis=1),
        "ctx",
        axis=0,
        tiled=True,
    )

    own = jnp.concatenate([first_layer_keys, first_layer_values], axis=1)
    back_one = ctx_shift(own, Y_HI)
    back_two = ctx_shift(own, 2 * Y_HI)
    later = jnp.concatenate([own, back_one], axis=0)
    earlier = jnp.concatenate([back_one, back_two], axis=0)
    peers = jnp.arange(Y_HI, dtype=jnp.int32)[:, None, None]
    blocks = lax.all_to_all(
        jnp.where(peers >= place_y, later[None], earlier[None]),
        "ctx",
        0,
        0,
        tiled=True,
        axis_index_groups=Y_GROUPS,
    )

    start = ctx_place * TOK
    tokens = start + jnp.arange(TOK, dtype=jnp.int32)
    local_pos = lax.dynamic_slice_in_dim(positions, start, TOK, 0)
    low_one = jnp.maximum((tokens - local_pos)[None, :], tokens[None, :] - window[:, None] + 1)
    low_one = jnp.broadcast_to(low_one.reshape(2 * TOK, 1), (2 * TOK, 128))
    sent = pl.pallas_call(
        first_kernel,
        out_shape=jax.ShapeDtypeStruct((N_HEADS, ROWS, SLAB), bf16),
        in_specs=[whole(pltpu.SMEM)] + [whole()] * 6,
        out_specs=whole(),
        scratch_shapes=[pltpu.VMEM((2 * TOK, 9 * TOK), f32)],
        compiler_params=params(),
        cost_estimate=pl.CostEstimate(
            flops=600_000_000, bytes_accessed=6_000_000, transcendentals=300_000
        ),
        name="first_layer",
    )(
        jnp.stack([place_z, place_y]),
        first_layer_queries,
        blocks,
        back_two,
        low_one,
        out_one,
        resid_in,
    )
    got = exchange_heads(sent)
    sent = pl.pallas_call(
        norm_kernel,
        out_shape=jax.ShapeDtypeStruct((N_HEADS, ROWS, SLAB), bf16),
        in_specs=[whole()] * 3,
        out_specs=whole(),
        scratch_shapes=[pltpu.VMEM((ROWS, WIDTH), f32)] * 2,
        compiler_params=params(),
        name="norms",
    )(got, post_gain[None, :], pre_gain[None, :])
    got = exchange_heads(sent)
    resid_out = got[:, :, WIDTH : WIDTH + COLS].reshape(TOK, COLS)

    speeds = THETA ** (-(jnp.arange(HALF, dtype=f32) * 2.0 / HEAD_SIZE))
    angles = (local_pos.astype(f32) * POSITION_FACTOR)[:, None] * speeds[None, :]
    cosine, sine = jnp.cos(angles), jnp.sin(angles)
    turn_cos = jnp.concatenate([cosine, cosine], axis=1)
    turn_sin = jnp.concatenate([-sine, sine], axis=1)
    depth = 896
    query, pair = pl.pallas_call(
        project_kernel,
        out_shape=(
            jax.ShapeDtypeStruct((TOK, 2 * HEAD_SIZE), bf16),
            jax.ShapeDtypeStruct((TOK, 2 * HEAD_SIZE), bf16),
        ),
        grid=(WIDTH // depth,),
        in_specs=[
            pl.BlockSpec((N_HEADS, ROWS, depth), lambda k: (0, 0, k)),
            pl.BlockSpec((depth, 4 * HEAD_SIZE), lambda k: (k, 0)),
            pl.BlockSpec((TOK, HEAD_SIZE), lambda k: (0, 0)),
            pl.BlockSpec((TOK, HEAD_SIZE), lambda k: (0, 0)),
        ],
        out_specs=(
            pl.BlockSpec((TOK, 2 * HEAD_SIZE), lambda k: (0, 0)),
            pl.BlockSpec((TOK, 2 * HEAD_SIZE), lambda k: (0, 0)),
        ),
        scratch_shapes=[pltpu.VMEM((TOK, 4 * HEAD_SIZE), f32)],
        compiler_params=params(),
        name="project",
    )(got, weights, turn_cos, turn_sin)

    row_pairs = lax.all_to_all(
        jnp.broadcast_to(pair[None], (Y_HI, TOK, 2 * HEAD_SIZE)),
        "ctx",
        0,
        0,
        tiled=True,
        axis_index_groups=Y_GROUPS,
    ).reshape(Y_HI * TOK, 2 * HEAD_SIZE)
    all_pairs = lax.all_gather(row_pairs, "ctx", axis=0, tiled=True, axis_index_groups=Z_GROUPS)
    moved = lax.ppermute(query[HALF:], "ctx", [(i, N_CTX - 1 - i) for i in range(N_CTX)])
    query = jnp.concatenate([query[:HALF], moved], axis=0)

    second = (2 * N_CTX - 1 - 2 * ctx_place) * HALF
    firsts = jnp.stack([start, second])
    both = (firsts[:, None] + jnp.arange(HALF, dtype=jnp.int32)[None, :])
    pos_both = jnp.stack(
        [
            lax.dynamic_slice_in_dim(positions, start, HALF, 0),
            lax.dynamic_slice_in_dim(positions, second, HALF, 0),
        ]
    )
    low_two = jnp.broadcast_to((both - pos_both)[:, None, :], (2, 2, HALF)).reshape(2 * TOK, 1)
    low_two = jnp.broadcast_to(low_two, (2 * TOK, 128))
    attended = pl.pallas_call(
        second_kernel,
        out_shape=jax.ShapeDtypeStruct((TOK, 2 * HEAD_SIZE), bf16),
        in_specs=[whole(pltpu.SMEM)] + [whole()] * 3,
        out_specs=whole(),
        scratch_shapes=[pltpu.VMEM((TOK, SPAN), f32)],
        compiler_params=params(),
        name="second_layer",
    )(firsts, query, all_pairs, low_two)
    return (resid_out, attended)


def solution(mesh):
    placed = (
        P("ctx", "heads"),
        P("ctx", "heads"),
        P("ctx", "heads"),
        P("ctx", "heads"),
        P("heads", None),
        P(),
        P(),
        P("ctx", "heads"),
        P("ctx", "heads"),
        P("ctx", "heads"),
        P("heads"),
        P(),
    )
    return jax.shard_map(
        shards,
        mesh=mesh,
        in_specs=placed,
        out_specs=(P("ctx", "heads"), P("ctx", "heads")),
        check_vma=False,
    )
```

```python
from functools import partial

import jax
import jax.numpy as jnp
from jax import lax
from jax.experimental import pallas as pl
from jax.experimental.pallas import tpu as pltpu
from jax.sharding import PartitionSpec as P


HEAD_SIZE = 128
SCALE = 168.0 ** (-0.5)
EPS = 1e-06
THETA = 1000000.0
POSITION_FACTOR = 0.125
N_CTX = 32
N_HEADS = 16
Y_HI = 4
Z = 8
TOK = 128
HALF = 64
WIDTH = 5376
COLS = WIDTH // N_HEADS
SLAB = 5760
ROWS = TOK // N_HEADS
NEG = -1e30
Y_GROUPS = [[z * Y_HI + y for y in range(Y_HI)] for z in range(Z)]
Z_GROUPS = [[z * Y_HI + y for z in range(Z)] for y in range(Y_HI)]
VMEM_LIMIT = 48 * 1024 * 1024


def whole(memory_space=pltpu.VMEM):
    return pl.BlockSpec(memory_space=memory_space)


def fold_max(peak, part):
    for lane in range(0, part.shape[1], 128):
        peak = jnp.maximum(peak, part[:, lane : lane + 128])
    return peak


def fold_sum(total, part):
    for lane in range(0, part.shape[1], 128):
        total = total + part[:, lane : lane + 128]
    return total


def softmax_rows(query, chunks, low, high, scores):
    rows = query.shape[0]
    peak = jnp.full((rows, 128), NEG, jnp.float32)
    offset = 0
    for load, tokens in chunks:
        keys, _ = load()
        part = (
            lax.dot_general(
                query, keys, (((1,), (1,)), ((), ())), preferred_element_type=jnp.float32
            )
            * SCALE
        )
        width = part.shape[1]
        seen = (tokens >= low) & (tokens <= high)
        part = jnp.where(seen, part, NEG)
        scores[:, offset : offset + width] = part
        peak = fold_max(peak, part)
        offset += width
    top = jnp.max(peak, axis=1, keepdims=True)
    total = jnp.zeros((rows, 128), jnp.float32)
    mixed = jnp.zeros((rows, HEAD_SIZE), jnp.float32)
    offset = 0
    for load, tokens in chunks:
        _, values = load()
        width = values.shape[0]
        lifted = jnp.exp(scores[:, offset : offset + width] - top)
        total = fold_sum(total, lifted)
        mixed = mixed + jnp.dot(
            lifted.astype(jnp.bfloat16), values, preferred_element_type=jnp.float32
        )
        offset += width
    return mixed / jnp.sum(total, axis=1, keepdims=True)


def first_kernel(base, query, blocks, last, low, out_one, resid, sent, scores):
    place_z, place_y = base[0], base[1]
    start = (place_z * Y_HI + place_y) * TOK
    stacked = jnp.concatenate([query[:, :HEAD_SIZE], query[:, HEAD_SIZE:]], axis=0)
    lowest = low[...][:, :1]
    row = lax.broadcasted_iota(jnp.int32, (2 * TOK, 1), 0)
    high = start + lax.rem(row, TOK)
    lane = lax.broadcasted_iota(jnp.int32, (1, 2 * TOK), 1)
    pair = jnp.where(lane < TOK, lane, lane - (TOK + Y_HI * TOK))
    chunks = []
    for peer in range(Y_HI):
        newer = (place_z - jnp.where(peer > place_y, 1, 0)) * (Y_HI * TOK) + peer * TOK
        chunks.append(
            (
                lambda peer=peer: (
                    blocks[peer, :, :HEAD_SIZE],
                    blocks[peer, :, HEAD_SIZE:],
                ),
                newer + pair,
            )
        )
    chunks.append(
        (
            lambda: (last[:, :HEAD_SIZE], last[:, HEAD_SIZE:]),
            start - 2 * Y_HI * TOK + lane[:, :TOK],
        )
    )
    mixed = softmax_rows(stacked, chunks, lowest, high, scores).astype(jnp.bfloat16)
    attend = jnp.concatenate([mixed[:TOK], mixed[TOK:]], axis=1)
    step = 768
    for col in range(0, WIDTH, step):
        part = jnp.dot(attend, out_one[:, col : col + step], preferred_element_type=jnp.float32)
        sent[:, :, col : col + step] = part.reshape(N_HEADS, ROWS, step).astype(jnp.bfloat16)
    own = resid[...].astype(jnp.float32).reshape(N_HEADS, ROWS, COLS)
    sent[:, :, WIDTH : WIDTH + COLS] = own.astype(jnp.bfloat16)
    sent[:, :, WIDTH + COLS :] = jnp.zeros((N_HEADS, ROWS, SLAB - WIDTH - COLS), jnp.bfloat16)


def norm_kernel(got, post_gain, pre_gain, sent, rows, wide):
    combined = got[0, :, :WIDTH].astype(jnp.float32)
    for peer in range(1, N_HEADS):
        combined = combined + got[peer, :, :WIDTH].astype(jnp.float32)
    for peer in range(N_HEADS):
        rows[:, peer * COLS : (peer + 1) * COLS] = got[peer, :, WIDTH : WIDTH + COLS].astype(
            jnp.float32
        )
    scale = lax.rsqrt(jnp.mean(combined * combined, axis=1, keepdims=True) + EPS)
    resid = (rows[...] + post_gain[...] * (combined * scale)).astype(jnp.bfloat16)
    widened = resid.astype(jnp.float32)
    scale = lax.rsqrt(jnp.mean(widened * widened, axis=1, keepdims=True) + EPS)
    normed = (pre_gain[...] * widened * scale).astype(jnp.bfloat16)
    wide[...] = widened
    for peer in range(N_HEADS):
        sent[peer, :, :WIDTH] = normed
        sent[peer, :, WIDTH : WIDTH + COLS] = wide[:, peer * COLS : (peer + 1) * COLS].astype(
            jnp.bfloat16
        )
        sent[peer, :, WIDTH + COLS :] = jnp.zeros((ROWS, SLAB - WIDTH - COLS), jnp.bfloat16)


def project_kernel(got, weights, turn_cos, turn_sin, query, pair, total):
    step = pl.program_id(0)

    @pl.when(step == 0)
    def _():
        total[...] = jnp.zeros_like(total)

    rows = got[...].astype(jnp.float32).reshape(TOK, got.shape[2]).astype(jnp.bfloat16)
    total[...] += jnp.dot(rows, weights[...], preferred_element_type=jnp.float32)

    @pl.when(step == pl.num_programs(0) - 1)
    def _():
        for head in range(4):
            values = total[:, head * HEAD_SIZE : (head + 1) * HEAD_SIZE]
            if head < 3:
                values = values * turn_cos[...] + pltpu.roll(values, HALF, 1) * turn_sin[...]
            values = values.astype(jnp.bfloat16)
            if head < 2:
                query[:, head * HEAD_SIZE : (head + 1) * HEAD_SIZE] = values
            else:
                pair[:, (head - 2) * HEAD_SIZE : (head - 1) * HEAD_SIZE] = values


SPAN = 2304
CHUNK = 256


def second_kernel(base, query, pair, low, out, scores):
    for part in range(2):
        first = base[part]
        begin = jnp.clip(lax.div(first, TOK) * TOK + TOK - SPAN, 0, N_CTX * TOK - SPAN)
        begin = pl.multiple_of(begin, TOK)
        block = query[part * HALF : (part + 1) * HALF, :]
        stacked = jnp.concatenate([block[:, :HEAD_SIZE], block[:, HEAD_SIZE:]], axis=0)
        lowest = low[part * TOK : (part + 1) * TOK, :1]
        row = lax.broadcasted_iota(jnp.int32, (TOK, 1), 0)
        high = first + lax.rem(row, HALF)
        lane = lax.broadcasted_iota(jnp.int32, (1, CHUNK), 1)
        chunks = []
        for index in range(SPAN // CHUNK):
            at = pl.multiple_of(begin + index * CHUNK, TOK)
            chunks.append(
                (
                    lambda at=at: (
                        pair[pl.ds(at, CHUNK), :HEAD_SIZE],
                        pair[pl.ds(at, CHUNK), HEAD_SIZE:],
                    ),
                    at + lane,
                )
            )
        mixed = softmax_rows(stacked, chunks, lowest, high, scores).astype(jnp.bfloat16)
        out[part * HALF : (part + 1) * HALF, :] = jnp.concatenate(
            [mixed[:HALF], mixed[HALF:]], axis=1
        )


def exchange_heads(value):
    return lax.all_to_all(value, "heads", 0, 0, tiled=True)


def spread_rows(value):
    rows, cols = value.shape
    return lax.all_to_all(
        jnp.broadcast_to(value[None], (Y_HI, rows, cols)),
        "ctx",
        0,
        0,
        tiled=True,
        axis_index_groups=Y_GROUPS,
    ).reshape(Y_HI * rows, cols)


def ctx_shift(value, steps):
    return lax.ppermute(value, "ctx", [(i, (i + steps) % N_CTX) for i in range(N_CTX)])


def shards(
    resid_in,
    first_layer_queries,
    first_layer_keys,
    first_layer_values,
    out_one,
    post_gain,
    pre_gain,
    proj_query,
    key_projection,
    value_projection,
    window,
    positions,
):
    ctx_place = lax.axis_index("ctx").astype(jnp.int32)
    place_z, place_y = ctx_place // Y_HI, ctx_place % Y_HI
    bf16, f32 = jnp.bfloat16, jnp.float32
    params = partial(pltpu.CompilerParams, vmem_limit_bytes=VMEM_LIMIT)

    own = jnp.concatenate([first_layer_keys, first_layer_values], axis=1)
    back_one = ctx_shift(own, Y_HI)
    back_two = ctx_shift(own, 2 * Y_HI)
    joined = jnp.concatenate([proj_query, key_projection, value_projection], axis=1)
    weights = spread_rows(joined)
    weights = lax.all_gather(weights, "ctx", axis=0, tiled=True, axis_index_groups=Z_GROUPS)

    later = jnp.concatenate([own, back_one], axis=0)
    earlier = jnp.concatenate([back_one, back_two], axis=0)
    peers = jnp.arange(Y_HI, dtype=jnp.int32)[:, None, None]
    window_blocks = jnp.where(peers >= place_y, later[None], earlier[None])
    blocks = lax.all_to_all(
        window_blocks, "ctx", 0, 0, tiled=True, axis_index_groups=Y_GROUPS
    )

    start = ctx_place * TOK
    tokens = start + jnp.arange(TOK, dtype=jnp.int32)
    local_pos = lax.dynamic_slice_in_dim(positions, start, TOK, 0)
    low_one = jnp.maximum((tokens - local_pos)[None, :], tokens[None, :] - window[:, None] + 1)
    low_one = jnp.broadcast_to(low_one.reshape(2 * TOK, 1), (2 * TOK, 128))
    sent = pl.pallas_call(
        first_kernel,
        out_shape=jax.ShapeDtypeStruct((N_HEADS, ROWS, SLAB), bf16),
        in_specs=[whole(pltpu.SMEM)] + [whole()] * 6,
        out_specs=whole(),
        scratch_shapes=[pltpu.VMEM((2 * TOK, 9 * TOK), f32)],
        compiler_params=params(),
        cost_estimate=pl.CostEstimate(
            flops=600_000_000, bytes_accessed=6_000_000, transcendentals=300_000
        ),
        name="first_layer",
    )(
        jnp.stack([place_z, place_y]),
        first_layer_queries,
        blocks,
        back_two,
        low_one,
        out_one,
        resid_in,
    )
    got = exchange_heads(sent)
    sent = pl.pallas_call(
        norm_kernel,
        out_shape=jax.ShapeDtypeStruct((N_HEADS, ROWS, SLAB), bf16),
        in_specs=[whole()] * 3,
        out_specs=whole(),
        scratch_shapes=[pltpu.VMEM((ROWS, WIDTH), f32)] * 2,
        compiler_params=params(),
        name="norms",
    )(got, post_gain[None, :], pre_gain[None, :])
    got = exchange_heads(sent)
    resid_out = got[:, :, WIDTH : WIDTH + COLS].reshape(TOK, COLS)

    speeds = THETA ** (-(jnp.arange(HALF, dtype=f32) * 2.0 / HEAD_SIZE))
    angles = (local_pos.astype(f32) * POSITION_FACTOR)[:, None] * speeds[None, :]
    cosine, sine = jnp.cos(angles), jnp.sin(angles)
    turn_cos = jnp.concatenate([cosine, cosine], axis=1)
    turn_sin = jnp.concatenate([-sine, sine], axis=1)
    depth = 896
    query, pair = pl.pallas_call(
        project_kernel,
        out_shape=(
            jax.ShapeDtypeStruct((TOK, 2 * HEAD_SIZE), bf16),
            jax.ShapeDtypeStruct((TOK, 2 * HEAD_SIZE), bf16),
        ),
        grid=(WIDTH // depth,),
        in_specs=[
            pl.BlockSpec((N_HEADS, ROWS, depth), lambda k: (0, 0, k)),
            pl.BlockSpec((depth, 4 * HEAD_SIZE), lambda k: (k, 0)),
            pl.BlockSpec((TOK, HEAD_SIZE), lambda k: (0, 0)),
            pl.BlockSpec((TOK, HEAD_SIZE), lambda k: (0, 0)),
        ],
        out_specs=(
            pl.BlockSpec((TOK, 2 * HEAD_SIZE), lambda k: (0, 0)),
            pl.BlockSpec((TOK, 2 * HEAD_SIZE), lambda k: (0, 0)),
        ),
        scratch_shapes=[pltpu.VMEM((TOK, 4 * HEAD_SIZE), f32)],
        compiler_params=params(),
        name="project",
    )(got, weights, turn_cos, turn_sin)

    row_pairs = spread_rows(pair)
    all_pairs = lax.all_gather(row_pairs, "ctx", axis=0, tiled=True, axis_index_groups=Z_GROUPS)
    moved = lax.ppermute(query[HALF:], "ctx", [(i, N_CTX - 1 - i) for i in range(N_CTX)])
    query = jnp.concatenate([query[:HALF], moved], axis=0)

    second = (2 * N_CTX - 1 - 2 * ctx_place) * HALF
    firsts = jnp.stack([start, second])
    both = (firsts[:, None] + jnp.arange(HALF, dtype=jnp.int32)[None, :])
    pos_both = jnp.stack(
        [
            lax.dynamic_slice_in_dim(positions, start, HALF, 0),
            lax.dynamic_slice_in_dim(positions, second, HALF, 0),
        ]
    )
    low_two = jnp.broadcast_to((both - pos_both)[:, None, :], (2, 2, HALF)).reshape(2 * TOK, 1)
    low_two = jnp.broadcast_to(low_two, (2 * TOK, 128))
    attended = pl.pallas_call(
        second_kernel,
        out_shape=jax.ShapeDtypeStruct((TOK, 2 * HEAD_SIZE), bf16),
        in_specs=[whole(pltpu.SMEM)] + [whole()] * 3,
        out_specs=whole(),
        scratch_shapes=[pltpu.VMEM((TOK, SPAN), f32)],
        compiler_params=params(),
        name="second_layer",
    )(firsts, query, all_pairs, low_two)
    return (resid_out, attended)


def solution(mesh):
    placed = (
        P("ctx", "heads"),
        P("ctx", "heads"),
        P("ctx", "heads"),
        P("ctx", "heads"),
        P("heads", None),
        P(),
        P(),
        P("ctx", "heads"),
        P("ctx", "heads"),
        P("ctx", "heads"),
        P("heads"),
        P(),
    )
    return jax.shard_map(
        shards,
        mesh=mesh,
        in_specs=placed,
        out_specs=(P("ctx", "heads"), P("ctx", "heads")),
        check_vma=False,
    )
```

```python
from functools import partial

import jax
import jax.numpy as jnp
from jax import lax
from jax.experimental import pallas as pl
from jax.experimental.pallas import tpu as pltpu
from jax.sharding import PartitionSpec as P


HEAD_SIZE = 128
SCALE = 168.0 ** (-0.5)
EPS = 1e-06
THETA = 1000000.0
POSITION_FACTOR = 0.125
N_CTX = 32
N_HEADS = 16
Y_HI = 4
Z = 8
TOK = 128
HALF = 64
WIDTH = 5376
COLS = WIDTH // N_HEADS
SLAB = 5760
ROWS = TOK // N_HEADS
NEG = -1e30
Y_GROUPS = [[z * Y_HI + y for y in range(Y_HI)] for z in range(Z)]
GROUP = 16
HALF_GROUPS = [list(range(GROUP)), list(range(GROUP, N_CTX))]
Z_GROUPS = [[z * Y_HI + y for z in range(Z)] for y in range(Y_HI)]
VMEM_LIMIT = 24 * 1024 * 1024


def whole(memory_space=pltpu.VMEM):
    return pl.BlockSpec(memory_space=memory_space)


def fold_max(peak, part):
    for lane in range(0, part.shape[1], 128):
        peak = jnp.maximum(peak, part[:, lane : lane + 128])
    return peak


def fold_sum(total, part):
    for lane in range(0, part.shape[1], 128):
        total = total + part[:, lane : lane + 128]
    return total


def softmax_rows(query, chunks, low, high, scores):
    rows = query.shape[0]
    peak = jnp.full((rows, 128), NEG, jnp.float32)
    offset = 0
    for load, tokens in chunks:
        keys, _ = load()
        part = (
            lax.dot_general(
                query, keys, (((1,), (1,)), ((), ())), preferred_element_type=jnp.float32
            )
            * SCALE
        )
        width = part.shape[1]
        seen = (tokens >= low) & (tokens <= high)
        part = jnp.where(seen, part, NEG)
        scores[:, offset : offset + width] = part
        peak = fold_max(peak, part)
        offset += width
    top = jnp.max(peak, axis=1, keepdims=True)
    total = jnp.zeros((rows, 128), jnp.float32)
    mixed = jnp.zeros((rows, HEAD_SIZE), jnp.float32)
    offset = 0
    for load, tokens in chunks:
        _, values = load()
        width = values.shape[0]
        lifted = jnp.exp(scores[:, offset : offset + width] - top)
        total = fold_sum(total, lifted)
        mixed = mixed + jnp.dot(
            lifted.astype(jnp.bfloat16), values, preferred_element_type=jnp.float32
        )
        offset += width
    total = jnp.sum(total, axis=1, keepdims=True)
    return mixed / total, top + jnp.log(total)


def first_kernel(base, query, blocks, last, low, out_one, resid, sent, scores):
    place_z, place_y = base[0], base[1]
    start = (place_z * Y_HI + place_y) * TOK
    stacked = jnp.concatenate([query[:, :HEAD_SIZE], query[:, HEAD_SIZE:]], axis=0)
    lowest = low[...][:, :1]
    row = lax.broadcasted_iota(jnp.int32, (2 * TOK, 1), 0)
    high = start + lax.rem(row, TOK)
    lane = lax.broadcasted_iota(jnp.int32, (1, 2 * TOK), 1)
    pair = jnp.where(lane < TOK, lane, lane - (TOK + Y_HI * TOK))
    chunks = []
    for peer in range(Y_HI):
        newer = (place_z - jnp.where(peer > place_y, 1, 0)) * (Y_HI * TOK) + peer * TOK
        chunks.append(
            (
                lambda peer=peer: (
                    blocks[peer, :, :HEAD_SIZE],
                    blocks[peer, :, HEAD_SIZE:],
                ),
                newer + pair,
            )
        )
    chunks.append(
        (
            lambda: (last[:, :HEAD_SIZE], last[:, HEAD_SIZE:]),
            start - 2 * Y_HI * TOK + lane[:, :TOK],
        )
    )
    mixed, _ = softmax_rows(stacked, chunks, lowest, high, scores)
    mixed = mixed.astype(jnp.bfloat16)
    attend = jnp.concatenate([mixed[:TOK], mixed[TOK:]], axis=1)
    step = 768
    for col in range(0, WIDTH, step):
        part = jnp.dot(attend, out_one[:, col : col + step], preferred_element_type=jnp.float32)
        sent[:, :, col : col + step] = part.reshape(N_HEADS, ROWS, step).astype(jnp.bfloat16)
    own = resid[...].astype(jnp.float32).reshape(N_HEADS, ROWS, COLS)
    sent[:, :, WIDTH : WIDTH + COLS] = own.astype(jnp.bfloat16)
    sent[:, :, WIDTH + COLS :] = jnp.zeros((N_HEADS, ROWS, SLAB - WIDTH - COLS), jnp.bfloat16)


def norm_kernel(got, post_gain, pre_gain, sent, rows, wide):
    combined = got[0, :, :WIDTH].astype(jnp.float32)
    for peer in range(1, N_HEADS):
        combined = combined + got[peer, :, :WIDTH].astype(jnp.float32)
    for peer in range(N_HEADS):
        rows[:, peer * COLS : (peer + 1) * COLS] = got[peer, :, WIDTH : WIDTH + COLS].astype(
            jnp.float32
        )
    scale = lax.rsqrt(jnp.mean(combined * combined, axis=1, keepdims=True) + EPS)
    resid = (rows[...] + post_gain[...] * (combined * scale)).astype(jnp.bfloat16)
    widened = resid.astype(jnp.float32)
    scale = lax.rsqrt(jnp.mean(widened * widened, axis=1, keepdims=True) + EPS)
    normed = (pre_gain[...] * widened * scale).astype(jnp.bfloat16)
    wide[...] = widened
    for peer in range(N_HEADS):
        sent[peer, :, :WIDTH] = normed
        sent[peer, :, WIDTH : WIDTH + COLS] = wide[:, peer * COLS : (peer + 1) * COLS].astype(
            jnp.bfloat16
        )
        sent[peer, :, WIDTH + COLS :] = jnp.zeros((ROWS, SLAB - WIDTH - COLS), jnp.bfloat16)


def prepare_kernel(
    keys, values, proj_query, key_projection, value_projection, own, spread, joined, in_sem, out_sem
):
    width = HEAD_SIZE
    moves = [
        pltpu.make_async_copy(source, target, in_sem.at[index])
        for index, (source, target) in enumerate(
            (
                (proj_query, joined.at[:, : 2 * width]),
                (key_projection, joined.at[:, 2 * width : 3 * width]),
                (value_projection, joined.at[:, 3 * width :]),
                (keys, own.at[:, :width]),
                (values, own.at[:, width:]),
            )
        )
    ]
    for move in moves:
        move.start()
    for move in moves[:3]:
        move.wait()
    copies = [
        pltpu.make_async_copy(joined, spread.at[peer], out_sem.at[peer]) for peer in range(Y_HI)
    ]
    for move in copies:
        move.start()
    for move in moves[3:] + copies:
        move.wait()


def project_kernel(
    got, weights, turn_cos, turn_sin, query, pair, held, block, in_sem, out_sem
):
    depth = WIDTH // PARTS
    spans = [slice(part * depth, (part + 1) * depth) for part in range(PARTS)]
    moves = [
        pltpu.make_async_copy(weights.at[span], held.at[span], in_sem.at[part])
        for part, span in enumerate(spans)
    ]
    for move in moves:
        move.start()
    total = jnp.zeros((TOK, 4 * HEAD_SIZE), jnp.float32)
    for move, span in zip(moves, spans):
        rows = got[:, :, span].astype(jnp.float32).reshape(TOK, depth).astype(jnp.bfloat16)
        move.wait()
        total = total + jnp.dot(rows, held[span, :], preferred_element_type=jnp.float32)
    for head in range(4):
        values = total[:, head * HEAD_SIZE : (head + 1) * HEAD_SIZE]
        if head < 3:
            values = values * turn_cos[...] + pltpu.roll(values, HALF, 1) * turn_sin[...]
        values = values.astype(jnp.bfloat16)
        if head < 2:
            query[:, head * HEAD_SIZE : (head + 1) * HEAD_SIZE] = values
        else:
            block[:, (head - 2) * HEAD_SIZE : (head - 1) * HEAD_SIZE] = values
    moves = [pltpu.make_async_copy(block, pair.at[peer], out_sem.at[peer]) for peer in range(GROUP)]
    for move in moves:
        move.start()
    for move in moves:
        move.wait()


CHUNK = 256
PARTS = 7


def three_terms(values):
    terms = []
    for _ in range(3):
        term = values.astype(jnp.bfloat16).astype(jnp.float32)
        terms.append(term)
        values = values - term
    return terms


def second_kernel(base, own_query, other_query, pair, low, kept, kept_log, sent, scores):
    lane = lax.broadcasted_iota(jnp.int32, (1, CHUNK), 1)
    row = lax.broadcasted_iota(jnp.int32, (2 * TOK, 1), 0)
    slot = lax.broadcasted_iota(jnp.int32, (HALF, HEAD_SIZE), 1)
    for index, query in enumerate((own_query, other_query)):
        stacked = jnp.concatenate([query[:, :HEAD_SIZE], query[:, HEAD_SIZE:]], axis=0)
        lowest = low[index * TOK : (index + 1) * TOK, :1]
        lowest = jnp.concatenate([lowest, lowest], axis=0)
        high = base[1 + index] + lax.rem(row, TOK)
        chunks = []
        for at in range(0, GROUP * TOK, CHUNK):
            chunks.append(
                (
                    lambda at=at: (
                        pair[at : at + CHUNK, :HEAD_SIZE],
                        pair[at : at + CHUNK, HEAD_SIZE:],
                    ),
                    base[0] + at + lane,
                )
            )
        mixed, logs = softmax_rows(stacked, chunks, lowest, high, scores)
        for half in range(2):
            rows = slice(half * HALF, (half + 1) * HALF)
            pieces = [slice(half * HALF + head * TOK, (half + 1) * HALF + head * TOK) for head in range(2)]
            if half == index:
                for head in range(2):
                    kept[rows, head * HEAD_SIZE : (head + 1) * HEAD_SIZE] = mixed[pieces[head]]
                kept_log[rows, :] = jnp.where(slot < 3, logs[pieces[0]], logs[pieces[1]])
            else:
                packed = jnp.zeros((HALF, HEAD_SIZE), jnp.float32)
                for head in range(2):
                    sent[rows, head * HEAD_SIZE : (head + 1) * HEAD_SIZE] = mixed[
                        pieces[head]
                    ].astype(jnp.bfloat16)
                    for place, term in enumerate(three_terms(logs[pieces[head]])):
                        packed = jnp.where(slot == 3 * head + place, term, packed)
                sent[rows, 2 * HEAD_SIZE :] = packed.astype(jnp.bfloat16)


def combine_kernel(kept, kept_log, got, out):
    packed = got[:, 2 * HEAD_SIZE :].astype(jnp.float32)
    for head in range(2):
        cols = slice(head * HEAD_SIZE, (head + 1) * HEAD_SIZE)
        mine = kept_log[:, 3 * head : 3 * head + 1]
        at = 3 * head
        theirs = packed[:, at : at + 1] + packed[:, at + 1 : at + 2] + packed[:, at + 2 : at + 3]
        top = jnp.maximum(mine, theirs)
        mine = jnp.exp(mine - top)
        theirs = jnp.exp(theirs - top)
        mixed = kept[:, cols] * mine + got[:, cols].astype(jnp.float32) * theirs
        out[:, cols] = (mixed / (mine + theirs)).astype(jnp.bfloat16)


def exchange_heads(value):
    return lax.all_to_all(value, "heads", 0, 0, tiled=True)


def exchange_y(value):
    return lax.all_to_all(value, "ctx", 0, 0, tiled=True, axis_index_groups=Y_GROUPS)


def mirror(value):
    return lax.ppermute(value, "ctx", [(i, N_CTX - 1 - i) for i in range(N_CTX)])


def ctx_shift(value, steps):
    return lax.ppermute(value, "ctx", [(i, (i + steps) % N_CTX) for i in range(N_CTX)])


def shards(
    resid_in,
    first_layer_queries,
    first_layer_keys,
    first_layer_values,
    out_one,
    post_gain,
    pre_gain,
    proj_query,
    key_projection,
    value_projection,
    window,
    positions,
):
    ctx_place = lax.axis_index("ctx").astype(jnp.int32)
    place_z, place_y = ctx_place // Y_HI, ctx_place % Y_HI
    bf16, f32 = jnp.bfloat16, jnp.float32
    params = partial(pltpu.CompilerParams, vmem_limit_bytes=VMEM_LIMIT)

    own, spread = pl.pallas_call(
        prepare_kernel,
        out_shape=(
            jax.ShapeDtypeStruct((TOK, 2 * HEAD_SIZE), bf16),
            jax.ShapeDtypeStruct((Y_HI, proj_query.shape[0], 4 * HEAD_SIZE), bf16),
        ),
        in_specs=[whole(pltpu.HBM)] * 5,
        out_specs=(whole(), whole(pltpu.HBM)),
        scratch_shapes=[
            pltpu.VMEM((proj_query.shape[0], 4 * HEAD_SIZE), bf16),
            pltpu.SemaphoreType.DMA((5,)),
            pltpu.SemaphoreType.DMA((Y_HI,)),
        ],
        name="prepare",
    )(first_layer_keys, first_layer_values, proj_query, key_projection, value_projection)
    back_one = ctx_shift(own, Y_HI)
    back_two = ctx_shift(own, 2 * Y_HI)
    weights = exchange_y(spread).reshape(-1, 4 * HEAD_SIZE)
    weights = lax.all_gather(weights, "ctx", axis=0, tiled=True, axis_index_groups=Z_GROUPS)

    later = jnp.concatenate([own, back_one], axis=0)
    earlier = jnp.concatenate([back_one, back_two], axis=0)
    peers = jnp.arange(Y_HI, dtype=jnp.int32)[:, None, None]
    window_blocks = jnp.where(peers >= place_y, later[None], earlier[None])
    blocks = exchange_y(window_blocks)

    start = ctx_place * TOK
    tokens = start + jnp.arange(TOK, dtype=jnp.int32)
    local_pos = lax.dynamic_slice_in_dim(positions, start, TOK, 0)
    low_one = jnp.maximum((tokens - local_pos)[None, :], tokens[None, :] - window[:, None] + 1)
    low_one = jnp.broadcast_to(low_one.reshape(2 * TOK, 1), (2 * TOK, 128))
    sent = pl.pallas_call(
        first_kernel,
        out_shape=jax.ShapeDtypeStruct((N_HEADS, ROWS, SLAB), bf16),
        in_specs=[whole(pltpu.SMEM)] + [whole()] * 6,
        out_specs=whole(),
        scratch_shapes=[pltpu.VMEM((2 * TOK, 9 * TOK), f32)],
        compiler_params=params(),
        cost_estimate=pl.CostEstimate(
            flops=600_000_000, bytes_accessed=6_000_000, transcendentals=300_000
        ),
        name="first_layer",
    )(
        jnp.stack([place_z, place_y]),
        first_layer_queries,
        blocks,
        back_two,
        low_one,
        out_one,
        resid_in,
    )
    got = exchange_heads(sent)
    sent = pl.pallas_call(
        norm_kernel,
        out_shape=jax.ShapeDtypeStruct((N_HEADS, ROWS, SLAB), bf16),
        in_specs=[whole()] * 3,
        out_specs=whole(),
        scratch_shapes=[pltpu.VMEM((ROWS, WIDTH), f32)] * 2,
        compiler_params=params(),
        name="norms",
    )(got, post_gain[None, :], pre_gain[None, :])
    got = exchange_heads(sent)
    resid_out = got[:, :, WIDTH : WIDTH + COLS].reshape(TOK, COLS)

    speeds = THETA ** (-(jnp.arange(HALF, dtype=f32) * 2.0 / HEAD_SIZE))
    angles = (local_pos.astype(f32) * POSITION_FACTOR)[:, None] * speeds[None, :]
    cosine, sine = jnp.cos(angles), jnp.sin(angles)
    turn_cos = jnp.concatenate([cosine, cosine], axis=1)
    turn_sin = jnp.concatenate([-sine, sine], axis=1)
    query, pair = pl.pallas_call(
        project_kernel,
        out_shape=(
            jax.ShapeDtypeStruct((TOK, 2 * HEAD_SIZE), bf16),
            jax.ShapeDtypeStruct((GROUP, TOK, 2 * HEAD_SIZE), bf16),
        ),
        in_specs=[whole(), whole(pltpu.HBM), whole(), whole()],
        out_specs=(whole(), whole(pltpu.HBM)),
        scratch_shapes=[
            pltpu.VMEM((WIDTH, 4 * HEAD_SIZE), bf16),
            pltpu.VMEM((TOK, 2 * HEAD_SIZE), bf16),
            pltpu.SemaphoreType.DMA((PARTS,)),
            pltpu.SemaphoreType.DMA((GROUP,)),
        ],
        compiler_params=pltpu.CompilerParams(vmem_limit_bytes=52 * 1024 * 1024),
        name="project",
    )(got, weights, turn_cos, turn_sin)

    pairs = lax.all_to_all(
        pair, "ctx", 0, 0, tiled=True, axis_index_groups=HALF_GROUPS
    ).reshape(GROUP * TOK, 2 * HEAD_SIZE)
    other_query = mirror(query)

    other_start = (N_CTX - 1 - ctx_place) * TOK
    other_pos = lax.dynamic_slice_in_dim(positions, other_start, TOK, 0)
    other_tokens = other_start + jnp.arange(TOK, dtype=jnp.int32)
    low_two = jnp.concatenate([tokens - local_pos, other_tokens - other_pos])
    low_two = jnp.broadcast_to(low_two[:, None], (2 * TOK, 128))
    bases = jnp.stack([(ctx_place // GROUP) * (GROUP * TOK), start, other_start])
    kept, kept_log, sent = pl.pallas_call(
        second_kernel,
        out_shape=(
            jax.ShapeDtypeStruct((TOK, 2 * HEAD_SIZE), f32),
            jax.ShapeDtypeStruct((TOK, HEAD_SIZE), f32),
            jax.ShapeDtypeStruct((TOK, 3 * HEAD_SIZE), bf16),
        ),
        in_specs=[whole(pltpu.SMEM)] + [whole()] * 4,
        out_specs=(whole(), whole(), whole()),
        scratch_shapes=[pltpu.VMEM((2 * TOK, GROUP * TOK), f32)],
        compiler_params=params(),
        name="second_layer",
    )(bases, query, other_query, pairs, low_two)
    got = mirror(sent)
    attended = pl.pallas_call(
        combine_kernel,
        out_shape=jax.ShapeDtypeStruct((TOK, 2 * HEAD_SIZE), bf16),
        in_specs=[whole()] * 3,
        out_specs=whole(),
        compiler_params=params(),
        name="combine",
    )(kept, kept_log, got)
    return (resid_out, attended)


def solution(mesh):
    placed = (
        P("ctx", "heads"),
        P("ctx", "heads"),
        P("ctx", "heads"),
        P("ctx", "heads"),
        P("heads", None),
        P(),
        P(),
        P("ctx", "heads"),
        P("ctx", "heads"),
        P("ctx", "heads"),
        P("heads"),
        P(),
    )
    return jax.shard_map(
        shards,
        mesh=mesh,
        in_specs=placed,
        out_specs=(P("ctx", "heads"), P("ctx", "heads")),
        check_vma=False,
    )
```

```python
from functools import partial

import jax
import jax.numpy as jnp
from jax import lax
from jax.experimental import pallas as pl
from jax.experimental.pallas import tpu as pltpu
from jax.sharding import PartitionSpec as P


HEAD_SIZE = 128
SCALE = 168.0 ** (-0.5)
EPS = 1e-06
THETA = 1000000.0
POSITION_FACTOR = 0.125
N_CTX = 32
N_HEADS = 16
Y_HI = 4
Z = 8
TOK = 128
HALF = 64
WIDTH = 5376
COLS = WIDTH // N_HEADS
SLAB = 5760
ROWS = TOK // N_HEADS
NEG = -1e30
Y_GROUPS = [[z * Y_HI + y for y in range(Y_HI)] for z in range(Z)]
Z_GROUPS = [[z * Y_HI + y for z in range(Z)] for y in range(Y_HI)]
VMEM_LIMIT = 24 * 1024 * 1024


def whole(memory_space=pltpu.VMEM):
    return pl.BlockSpec(memory_space=memory_space)


def fold_max(peak, part):
    for lane in range(0, part.shape[1], 128):
        peak = jnp.maximum(peak, part[:, lane : lane + 128])
    return peak


def fold_sum(total, part):
    for lane in range(0, part.shape[1], 128):
        total = total + part[:, lane : lane + 128]
    return total


def softmax_rows(query, chunks, low, high, scores):
    rows = query.shape[0]
    peak = jnp.full((rows, 128), NEG, jnp.float32)
    offset = 0
    for load, tokens in chunks:
        keys, _ = load()
        part = (
            lax.dot_general(
                query, keys, (((1,), (1,)), ((), ())), preferred_element_type=jnp.float32
            )
            * SCALE
        )
        width = part.shape[1]
        seen = (tokens >= low) & (tokens <= high)
        part = jnp.where(seen, part, NEG)
        scores[:, offset : offset + width] = part
        peak = fold_max(peak, part)
        offset += width
    top = jnp.max(peak, axis=1, keepdims=True)
    total = jnp.zeros((rows, 128), jnp.float32)
    mixed = jnp.zeros((rows, HEAD_SIZE), jnp.float32)
    offset = 0
    for load, tokens in chunks:
        _, values = load()
        width = values.shape[0]
        lifted = jnp.exp(scores[:, offset : offset + width] - top)
        total = fold_sum(total, lifted)
        mixed = mixed + jnp.dot(
            lifted.astype(jnp.bfloat16), values, preferred_element_type=jnp.float32
        )
        offset += width
    total = jnp.sum(total, axis=1, keepdims=True)
    return mixed / total, top + jnp.log(total)


def select_kernel(base, own, back_one, back_two, *shifted):
    for steps, out in enumerate(shifted, start=1):
        onward = base[1] + steps < Y_HI

        @pl.when(onward)
        def _(out=out):
            out[:TOK] = own[...]
            out[TOK:] = back_one[...]

        @pl.when(jnp.logical_not(onward))
        def _(out=out):
            out[:TOK] = back_one[...]
            out[TOK:] = back_two[...]


def first_kernel(
    base, query, own, back_one, back_two, near, middle, far, low, out_one, resid, sent, scores
):
    place_z, place_y = base[0], base[1]
    start = (place_z * Y_HI + place_y) * TOK
    stacked = jnp.concatenate([query[:, :HEAD_SIZE], query[:, HEAD_SIZE:]], axis=0)
    lowest = low[...][:, :1]
    row = lax.broadcasted_iota(jnp.int32, (2 * TOK, 1), 0)
    high = start + lax.rem(row, TOK)
    lane = lax.broadcasted_iota(jnp.int32, (1, 2 * TOK), 1)
    pair = jnp.where(lane < TOK, lane, lane - (TOK + Y_HI * TOK))
    chunks = []

    def add(block, tokens):
        chunks.append((lambda: (block[:, :HEAD_SIZE], block[:, HEAD_SIZE:]), tokens))

    for steps, block in enumerate((near, middle, far), start=1):
        add(block, start - steps * TOK + pair)
    for level, block in enumerate((own, back_one, back_two)):
        add(block, start - level * Y_HI * TOK + lane[:, :TOK])
    mixed, _ = softmax_rows(stacked, chunks, lowest, high, scores)
    mixed = mixed.astype(jnp.bfloat16)
    attend = jnp.concatenate([mixed[:TOK], mixed[TOK:]], axis=1)
    step = 768
    for col in range(0, WIDTH, step):
        part = jnp.dot(attend, out_one[:, col : col + step], preferred_element_type=jnp.float32)
        sent[:, :, col : col + step] = part.reshape(N_HEADS, ROWS, step).astype(jnp.bfloat16)
    own = resid[...].astype(jnp.float32).reshape(N_HEADS, ROWS, COLS)
    sent[:, :, WIDTH : WIDTH + COLS] = own.astype(jnp.bfloat16)
    sent[:, :, WIDTH + COLS :] = jnp.zeros((N_HEADS, ROWS, SLAB - WIDTH - COLS), jnp.bfloat16)


def norm_kernel(got, post_gain, pre_gain, sent, rows, wide):
    combined = got[0, :, :WIDTH].astype(jnp.float32)
    for peer in range(1, N_HEADS):
        combined = combined + got[peer, :, :WIDTH].astype(jnp.float32)
    for peer in range(N_HEADS):
        rows[:, peer * COLS : (peer + 1) * COLS] = got[peer, :, WIDTH : WIDTH + COLS].astype(
            jnp.float32
        )
    scale = lax.rsqrt(jnp.mean(combined * combined, axis=1, keepdims=True) + EPS)
    resid = (rows[...] + post_gain[...] * (combined * scale)).astype(jnp.bfloat16)
    widened = resid.astype(jnp.float32)
    scale = lax.rsqrt(jnp.mean(widened * widened, axis=1, keepdims=True) + EPS)
    normed = (pre_gain[...] * widened * scale).astype(jnp.bfloat16)
    wide[...] = widened
    for peer in range(N_HEADS):
        sent[peer, :, :WIDTH] = normed
        sent[peer, :, WIDTH : WIDTH + COLS] = wide[:, peer * COLS : (peer + 1) * COLS].astype(
            jnp.bfloat16
        )
        sent[peer, :, WIDTH + COLS :] = jnp.zeros((ROWS, SLAB - WIDTH - COLS), jnp.bfloat16)


def prepare_kernel(
    keys, values, proj_query, key_projection, value_projection, own, spread, joined, in_sem, out_sem
):
    width = HEAD_SIZE
    moves = [
        pltpu.make_async_copy(source, target, in_sem.at[index])
        for index, (source, target) in enumerate(
            (
                (proj_query, joined.at[:, : 2 * width]),
                (key_projection, joined.at[:, 2 * width : 3 * width]),
                (value_projection, joined.at[:, 3 * width :]),
                (keys, own.at[:, :width]),
                (values, own.at[:, width:]),
            )
        )
    ]
    for move in moves:
        move.start()
    for move in moves[:3]:
        move.wait()
    copies = [
        pltpu.make_async_copy(joined, spread.at[peer], out_sem.at[peer]) for peer in range(Y_HI)
    ]
    for move in copies:
        move.start()
    for move in moves[3:] + copies:
        move.wait()


def project_kernel(
    got, weights, turn_cos, turn_sin, front, back, pair, held, block, in_sem, out_sem
):
    depth = WIDTH // PARTS
    spans = [slice(part * depth, (part + 1) * depth) for part in range(PARTS)]
    moves = [
        pltpu.make_async_copy(weights.at[span], held.at[span], in_sem.at[part])
        for part, span in enumerate(spans)
    ]
    for move in moves:
        move.start()
    total = jnp.zeros((TOK, 4 * HEAD_SIZE), jnp.float32)
    for move, span in zip(moves, spans):
        rows = got[:, :, span].astype(jnp.float32).reshape(TOK, depth).astype(jnp.bfloat16)
        move.wait()
        total = total + jnp.dot(rows, held[span, :], preferred_element_type=jnp.float32)
    for head in range(4):
        values = total[:, head * HEAD_SIZE : (head + 1) * HEAD_SIZE]
        if head < 3:
            values = values * turn_cos[...] + pltpu.roll(values, HALF, 1) * turn_sin[...]
        values = values.astype(jnp.bfloat16)
        if head < 2:
            front[:, head * HEAD_SIZE : (head + 1) * HEAD_SIZE] = values[:HALF]
            back[:, head * HEAD_SIZE : (head + 1) * HEAD_SIZE] = values[HALF:]
        else:
            block[:, (head - 2) * HEAD_SIZE : (head - 1) * HEAD_SIZE] = values
    moves = [pltpu.make_async_copy(block, pair.at[member], out_sem.at[member]) for member in range(Z)]
    for move in moves:
        move.start()
    for move in moves:
        move.wait()


CHUNK = 256
PARTS = 7


def three_terms(values):
    terms = []
    for _ in range(3):
        term = values.astype(jnp.bfloat16).astype(jnp.float32)
        terms.append(term)
        values = values - term
    return terms


def second_kernel(base, queries, pair, low, sent, scores):
    place_z, place_y = base[0], base[1]
    lane = lax.broadcasted_iota(jnp.int32, (1, CHUNK), 1)
    lane = jnp.where(lane < TOK, lane, lane + (Y_HI - 1) * TOK)
    row = lax.broadcasted_iota(jnp.int32, (2 * TOK, 1), 0)
    slot = lax.broadcasted_iota(jnp.int32, (TOK, HEAD_SIZE), 1)
    chunks = []
    for at in range(0, Z * TOK, CHUNK):
        chunks.append(
            (
                lambda at=at: (pair[at : at + CHUNK, :HEAD_SIZE], pair[at : at + CHUNK, HEAD_SIZE:]),
                at * Y_HI + place_y * TOK + lane,
            )
        )
    for peer in range(Y_HI):
        block = queries[peer * TOK : (peer + 1) * TOK, :]
        stacked = jnp.concatenate([block[:, :HEAD_SIZE], block[:, HEAD_SIZE:]], axis=0)
        lowest = low[peer * TOK : (peer + 1) * TOK, :1]
        lowest = jnp.concatenate([lowest, lowest], axis=0)
        front_first = (place_z * Y_HI + peer) * TOK
        back_first = ((Z - place_z) * Y_HI - 1 - peer) * TOK
        within = lax.rem(row, TOK)
        high = within + jnp.where(within < HALF, front_first, back_first)
        mixed, logs = softmax_rows(stacked, chunks, lowest, high, scores)
        packed = jnp.zeros((TOK, HEAD_SIZE), jnp.float32)
        for head in range(2):
            rows = slice(head * TOK, (head + 1) * TOK)
            sent[peer, :, head * HEAD_SIZE : (head + 1) * HEAD_SIZE] = mixed[rows].astype(
                jnp.bfloat16
            )
            for place, term in enumerate(three_terms(logs[rows])):
                packed = jnp.where(slot == 3 * head + place, term, packed)
        sent[peer, :, 2 * HEAD_SIZE :] = packed.astype(jnp.bfloat16)


def combine_kernel(got, out):
    for head in range(2):
        logs = []
        for peer in range(Y_HI):
            packed = got[peer, :, 2 * HEAD_SIZE :].astype(jnp.float32)
            at = 3 * head
            logs.append(
                packed[:, at : at + 1] + packed[:, at + 1 : at + 2] + packed[:, at + 2 : at + 3]
            )
        top = jnp.maximum(jnp.maximum(logs[0], logs[1]), jnp.maximum(logs[2], logs[3]))
        cols = slice(head * HEAD_SIZE, (head + 1) * HEAD_SIZE)
        mixed = jnp.zeros((TOK, HEAD_SIZE), jnp.float32)
        total = jnp.zeros((TOK, 1), jnp.float32)
        for peer in range(Y_HI):
            weight = jnp.exp(logs[peer] - top)
            mixed = mixed + weight * got[peer, :, cols].astype(jnp.float32)
            total = total + weight
        out[:, cols] = (mixed / total).astype(jnp.bfloat16)


def exchange_heads(value):
    return lax.all_to_all(value, "heads", 0, 0, tiled=True)


def exchange_y(value):
    return lax.all_to_all(value, "ctx", 0, 0, tiled=True, axis_index_groups=Y_GROUPS)


def y_shift(value, steps):
    pairs = [(z * Y_HI + y, z * Y_HI + (y + steps) % Y_HI) for z in range(Z) for y in range(Y_HI)]
    return lax.ppermute(value, "ctx", pairs)


def mirror(value):
    return lax.ppermute(value, "ctx", [(i, N_CTX - 1 - i) for i in range(N_CTX)])


def ctx_shift(value, steps):
    return lax.ppermute(value, "ctx", [(i, (i + steps) % N_CTX) for i in range(N_CTX)])


def shards(
    resid_in,
    first_layer_queries,
    first_layer_keys,
    first_layer_values,
    out_one,
    post_gain,
    pre_gain,
    proj_query,
    key_projection,
    value_projection,
    window,
    positions,
):
    ctx_place = lax.axis_index("ctx").astype(jnp.int32)
    place_z, place_y = ctx_place // Y_HI, ctx_place % Y_HI
    bf16, f32 = jnp.bfloat16, jnp.float32
    params = partial(pltpu.CompilerParams, vmem_limit_bytes=VMEM_LIMIT)

    own, spread = pl.pallas_call(
        prepare_kernel,
        out_shape=(
            jax.ShapeDtypeStruct((TOK, 2 * HEAD_SIZE), bf16),
            jax.ShapeDtypeStruct((Y_HI, proj_query.shape[0], 4 * HEAD_SIZE), bf16),
        ),
        in_specs=[whole(pltpu.HBM)] * 5,
        out_specs=(whole(), whole(pltpu.HBM)),
        scratch_shapes=[
            pltpu.VMEM((proj_query.shape[0], 4 * HEAD_SIZE), bf16),
            pltpu.SemaphoreType.DMA((5,)),
            pltpu.SemaphoreType.DMA((Y_HI,)),
        ],
        name="prepare",
    )(first_layer_keys, first_layer_values, proj_query, key_projection, value_projection)
    back_one = ctx_shift(own, Y_HI)
    back_two = ctx_shift(own, 2 * Y_HI)
    weights = exchange_y(spread).reshape(-1, 4 * HEAD_SIZE)
    weights = lax.all_gather(weights, "ctx", axis=0, tiled=True, axis_index_groups=Z_GROUPS)

    bases = jnp.stack([place_z, place_y])
    outgoing = pl.pallas_call(
        select_kernel,
        out_shape=[jax.ShapeDtypeStruct((2 * TOK, 2 * HEAD_SIZE), bf16)] * (Y_HI - 1),
        in_specs=[whole(pltpu.SMEM)] + [whole()] * 3,
        out_specs=[whole()] * (Y_HI - 1),
        compiler_params=params(),
        name="window_select",
    )(bases, own, back_one, back_two)
    incoming = []
    for steps, block in enumerate(outgoing, start=1):
        incoming.append(y_shift(block, steps))

    start = ctx_place * TOK
    tokens = start + jnp.arange(TOK, dtype=jnp.int32)
    local_pos = lax.dynamic_slice_in_dim(positions, start, TOK, 0)
    low_one = jnp.maximum((tokens - local_pos)[None, :], tokens[None, :] - window[:, None] + 1)
    low_one = jnp.broadcast_to(low_one.reshape(2 * TOK, 1), (2 * TOK, 128))
    sent = pl.pallas_call(
        first_kernel,
        out_shape=jax.ShapeDtypeStruct((N_HEADS, ROWS, SLAB), bf16),
        in_specs=[whole(pltpu.SMEM)] + [whole()] * 10,
        out_specs=whole(),
        scratch_shapes=[pltpu.VMEM((2 * TOK, 9 * TOK), f32)],
        compiler_params=params(),
        cost_estimate=pl.CostEstimate(
            flops=600_000_000, bytes_accessed=6_000_000, transcendentals=300_000
        ),
        name="first_layer",
    )(
        bases,
        first_layer_queries,
        own,
        back_one,
        back_two,
        *incoming,
        low_one,
        out_one,
        resid_in,
    )
    got = exchange_heads(sent)
    sent = pl.pallas_call(
        norm_kernel,
        out_shape=jax.ShapeDtypeStruct((N_HEADS, ROWS, SLAB), bf16),
        in_specs=[whole()] * 3,
        out_specs=whole(),
        scratch_shapes=[pltpu.VMEM((ROWS, WIDTH), f32)] * 2,
        compiler_params=params(),
        name="norms",
    )(got, post_gain[None, :], pre_gain[None, :])
    got = exchange_heads(sent)
    resid_out = got[:, :, WIDTH : WIDTH + COLS].reshape(TOK, COLS)

    speeds = THETA ** (-(jnp.arange(HALF, dtype=f32) * 2.0 / HEAD_SIZE))
    angles = (local_pos.astype(f32) * POSITION_FACTOR)[:, None] * speeds[None, :]
    cosine, sine = jnp.cos(angles), jnp.sin(angles)
    turn_cos = jnp.concatenate([cosine, cosine], axis=1)
    turn_sin = jnp.concatenate([-sine, sine], axis=1)
    front, back, pair = pl.pallas_call(
        project_kernel,
        out_shape=(
            jax.ShapeDtypeStruct((HALF, 2 * HEAD_SIZE), bf16),
            jax.ShapeDtypeStruct((HALF, 2 * HEAD_SIZE), bf16),
            jax.ShapeDtypeStruct((Z, TOK, 2 * HEAD_SIZE), bf16),
        ),
        in_specs=[whole(), whole(pltpu.HBM), whole(), whole()],
        out_specs=(whole(), whole(), whole(pltpu.HBM)),
        scratch_shapes=[
            pltpu.VMEM((WIDTH, 4 * HEAD_SIZE), bf16),
            pltpu.VMEM((TOK, 2 * HEAD_SIZE), bf16),
            pltpu.SemaphoreType.DMA((PARTS,)),
            pltpu.SemaphoreType.DMA((Z,)),
        ],
        compiler_params=pltpu.CompilerParams(vmem_limit_bytes=50 * 1024 * 1024),
        name="project",
    )(got, weights, turn_cos, turn_sin)

    pairs = lax.all_to_all(pair, "ctx", 0, 0, tiled=True, axis_index_groups=Z_GROUPS)
    pairs = pairs.reshape(Z * TOK, 2 * HEAD_SIZE)
    back = mirror(back)
    queries = lax.all_gather(
        jnp.concatenate([front, back], axis=0),
        "ctx",
        axis=0,
        tiled=True,
        axis_index_groups=Y_GROUPS,
    )

    level = Y_HI * TOK
    halves = (Y_HI, 2, HALF)
    order = jnp.arange(level, dtype=jnp.int32).reshape(halves)
    near, far = place_z * level, (Z - 1 - place_z) * level
    near_low = near + order - lax.dynamic_slice_in_dim(positions, near, level, 0).reshape(halves)
    far_low = far + order - lax.dynamic_slice_in_dim(positions, far, level, 0).reshape(halves)
    low_two = jnp.stack([near_low[:, 0], far_low[::-1, 1]], axis=1).reshape(level, 1)
    low_two = jnp.broadcast_to(low_two, (level, 128))
    sent = pl.pallas_call(
        second_kernel,
        out_shape=jax.ShapeDtypeStruct((Y_HI, TOK, 3 * HEAD_SIZE), bf16),
        in_specs=[whole(pltpu.SMEM)] + [whole()] * 3,
        out_specs=whole(),
        scratch_shapes=[pltpu.VMEM((2 * TOK, Z * TOK), f32)],
        compiler_params=params(),
        name="second_layer",
    )(bases, queries, pairs, low_two)
    got = exchange_y(sent)
    attended = pl.pallas_call(
        combine_kernel,
        out_shape=jax.ShapeDtypeStruct((TOK, 2 * HEAD_SIZE), bf16),
        in_specs=[whole()],
        out_specs=whole(),
        compiler_params=params(),
        name="combine",
    )(got)
    return (resid_out, attended)


def solution(mesh):
    placed = (
        P("ctx", "heads"),
        P("ctx", "heads"),
        P("ctx", "heads"),
        P("ctx", "heads"),
        P("heads", None),
        P(),
        P(),
        P("ctx", "heads"),
        P("ctx", "heads"),
        P("ctx", "heads"),
        P("heads"),
        P(),
    )
    return jax.shard_map(
        shards,
        mesh=mesh,
        in_specs=placed,
        out_specs=(P("ctx", "heads"), P("ctx", "heads")),
        check_vma=False,
    )
```

```python
from functools import partial

import jax
import jax.numpy as jnp
from jax import lax
from jax.experimental import pallas as pl
from jax.experimental.pallas import tpu as pltpu
from jax.sharding import PartitionSpec as P


HEAD_SIZE = 128
SCALE = 168.0 ** (-0.5)
EPS = 1e-06
THETA = 1000000.0
POSITION_FACTOR = 0.125
N_CTX = 32
N_HEADS = 16
Y_HI = 4
Z = 8
TOK = 128
HALF = 64
WIDTH = 5376
COLS = WIDTH // N_HEADS
SLAB = 5760
ROWS = TOK // N_HEADS
NEG = -1e30
Y_GROUPS = [[z * Y_HI + y for y in range(Y_HI)] for z in range(Z)]
LEVEL_PAIRS = [
    [z * Y_HI + y for y in range(Y_HI)] + [(Z - 1 - z) * Y_HI + y for y in range(Y_HI)]
    for z in range(Z // 2)
]
Z_GROUPS = [[z * Y_HI + y for z in range(Z)] for y in range(Y_HI)]
VMEM_LIMIT = 24 * 1024 * 1024


def whole(memory_space=pltpu.VMEM):
    return pl.BlockSpec(memory_space=memory_space)


def fold_max(peak, part):
    for lane in range(0, part.shape[1], 128):
        peak = jnp.maximum(peak, part[:, lane : lane + 128])
    return peak


def fold_sum(total, part):
    for lane in range(0, part.shape[1], 128):
        total = total + part[:, lane : lane + 128]
    return total


def softmax_rows(query, chunks, low, high, scores):
    rows = query.shape[0]
    peak = jnp.full((rows, 128), NEG, jnp.float32)
    offset = 0
    for load, tokens in chunks:
        keys, _ = load()
        part = (
            lax.dot_general(
                query, keys, (((1,), (1,)), ((), ())), preferred_element_type=jnp.float32
            )
            * SCALE
        )
        width = part.shape[1]
        seen = (tokens >= low) & (tokens <= high)
        part = jnp.where(seen, part, NEG)
        scores[:, offset : offset + width] = part
        peak = fold_max(peak, part)
        offset += width
    top = jnp.max(peak, axis=1, keepdims=True)
    total = jnp.zeros((rows, 128), jnp.float32)
    mixed = jnp.zeros((rows, HEAD_SIZE), jnp.float32)
    offset = 0
    for load, tokens in chunks:
        _, values = load()
        width = values.shape[0]
        lifted = jnp.exp(scores[:, offset : offset + width] - top)
        total = fold_sum(total, lifted)
        mixed = mixed + jnp.dot(
            lifted.astype(jnp.bfloat16), values, preferred_element_type=jnp.float32
        )
        offset += width
    total = jnp.sum(total, axis=1, keepdims=True)
    return mixed / total, top + jnp.log(total)


def first_kernel(base, query, blocks, last, low, out_one, resid, sent, scores):
    place_z, place_y = base[0], base[1]
    start = (place_z * Y_HI + place_y) * TOK
    stacked = jnp.concatenate([query[:, :HEAD_SIZE], query[:, HEAD_SIZE:]], axis=0)
    lowest = low[...][:, :1]
    row = lax.broadcasted_iota(jnp.int32, (2 * TOK, 1), 0)
    high = start + lax.rem(row, TOK)
    lane = lax.broadcasted_iota(jnp.int32, (1, 2 * TOK), 1)
    pair = jnp.where(lane < TOK, lane, lane - (TOK + Y_HI * TOK))
    chunks = []
    for peer in range(Y_HI):
        newer = (place_z - jnp.where(peer > place_y, 1, 0)) * (Y_HI * TOK) + peer * TOK
        chunks.append(
            (
                lambda peer=peer: (
                    blocks[peer, :, :HEAD_SIZE],
                    blocks[peer, :, HEAD_SIZE:],
                ),
                newer + pair,
            )
        )
    chunks.append(
        (
            lambda: (last[:, :HEAD_SIZE], last[:, HEAD_SIZE:]),
            start - 2 * Y_HI * TOK + lane[:, :TOK],
        )
    )
    mixed, _ = softmax_rows(stacked, chunks, lowest, high, scores)
    mixed = mixed.astype(jnp.bfloat16)
    attend = jnp.concatenate([mixed[:TOK], mixed[TOK:]], axis=1)
    step = 768
    for col in range(0, WIDTH, step):
        part = jnp.dot(attend, out_one[:, col : col + step], preferred_element_type=jnp.float32)
        sent[:, :, col : col + step] = part.reshape(N_HEADS, ROWS, step).astype(jnp.bfloat16)
    own = resid[...].astype(jnp.float32).reshape(N_HEADS, ROWS, COLS)
    sent[:, :, WIDTH : WIDTH + COLS] = own.astype(jnp.bfloat16)
    sent[:, :, WIDTH + COLS :] = jnp.zeros((N_HEADS, ROWS, SLAB - WIDTH - COLS), jnp.bfloat16)


def norm_kernel(got, post_gain, pre_gain, sent, rows, wide):
    combined = got[0, :, :WIDTH].astype(jnp.float32)
    for peer in range(1, N_HEADS):
        combined = combined + got[peer, :, :WIDTH].astype(jnp.float32)
    for peer in range(N_HEADS):
        rows[:, peer * COLS : (peer + 1) * COLS] = got[peer, :, WIDTH : WIDTH + COLS].astype(
            jnp.float32
        )
    scale = lax.rsqrt(jnp.mean(combined * combined, axis=1, keepdims=True) + EPS)
    resid = (rows[...] + post_gain[...] * (combined * scale)).astype(jnp.bfloat16)
    widened = resid.astype(jnp.float32)
    scale = lax.rsqrt(jnp.mean(widened * widened, axis=1, keepdims=True) + EPS)
    normed = (pre_gain[...] * widened * scale).astype(jnp.bfloat16)
    wide[...] = widened
    for peer in range(N_HEADS):
        sent[peer, :, :WIDTH] = normed
        sent[peer, :, WIDTH : WIDTH + COLS] = wide[:, peer * COLS : (peer + 1) * COLS].astype(
            jnp.bfloat16
        )
        sent[peer, :, WIDTH + COLS :] = jnp.zeros((ROWS, SLAB - WIDTH - COLS), jnp.bfloat16)


def prepare_kernel(
    keys, values, proj_query, key_projection, value_projection, own, spread, joined, in_sem, out_sem
):
    width = HEAD_SIZE
    moves = [
        pltpu.make_async_copy(source, target, in_sem.at[index])
        for index, (source, target) in enumerate(
            (
                (proj_query, joined.at[:, : 2 * width]),
                (key_projection, joined.at[:, 2 * width : 3 * width]),
                (value_projection, joined.at[:, 3 * width :]),
                (keys, own.at[:, :width]),
                (values, own.at[:, width:]),
            )
        )
    ]
    for move in moves:
        move.start()
    for move in moves[:3]:
        move.wait()
    copies = [
        pltpu.make_async_copy(joined, spread.at[peer], out_sem.at[peer]) for peer in range(Y_HI)
    ]
    for move in copies:
        move.start()
    for move in moves[3:] + copies:
        move.wait()


def project_kernel(
    got, weights, turn_cos, turn_sin, query, pair, held, block, in_sem, out_sem
):
    depth = WIDTH // PARTS
    spans = [slice(part * depth, (part + 1) * depth) for part in range(PARTS)]
    moves = [
        pltpu.make_async_copy(weights.at[span], held.at[span], in_sem.at[part])
        for part, span in enumerate(spans)
    ]
    for move in moves:
        move.start()
    total = jnp.zeros((TOK, 4 * HEAD_SIZE), jnp.float32)
    for move, span in zip(moves, spans):
        rows = got[:, :, span].astype(jnp.float32).reshape(TOK, depth).astype(jnp.bfloat16)
        move.wait()
        total = total + jnp.dot(rows, held[span, :], preferred_element_type=jnp.float32)
    for head in range(4):
        values = total[:, head * HEAD_SIZE : (head + 1) * HEAD_SIZE]
        if head < 3:
            values = values * turn_cos[...] + pltpu.roll(values, HALF, 1) * turn_sin[...]
        values = values.astype(jnp.bfloat16)
        if head < 2:
            query[:, head * HEAD_SIZE : (head + 1) * HEAD_SIZE] = values
        else:
            block[:, (head - 2) * HEAD_SIZE : (head - 1) * HEAD_SIZE] = values
    moves = [pltpu.make_async_copy(block, pair.at[member], out_sem.at[member]) for member in range(Z)]
    for move in moves:
        move.start()
    for move in moves:
        move.wait()


CHUNK = 256
PARTS = 7


def three_terms(values):
    terms = []
    for _ in range(3):
        term = values.astype(jnp.bfloat16).astype(jnp.float32)
        terms.append(term)
        values = values - term
    return terms


def second_kernel(base, queries, pair, low, sent, scores):
    place_z, place_y, upper = base[0], base[1], base[2]
    lane = lax.broadcasted_iota(jnp.int32, (1, CHUNK), 1)
    lane = jnp.where(lane < TOK, lane, lane + (Y_HI - 1) * TOK)
    row = lax.broadcasted_iota(jnp.int32, (2 * TOK, 1), 0)
    slot = lax.broadcasted_iota(jnp.int32, (TOK, HEAD_SIZE), 1)
    chunks = []
    for at in range(0, Z * TOK, CHUNK):
        chunks.append(
            (
                lambda at=at: (pair[at : at + CHUNK, :HEAD_SIZE], pair[at : at + CHUNK, HEAD_SIZE:]),
                at * Y_HI + place_y * TOK + lane,
            )
        )
    for peer in range(Y_HI):
        block = queries[peer * TOK : (peer + 1) * TOK, :]
        stacked = jnp.concatenate([block[:, :HEAD_SIZE], block[:, HEAD_SIZE:]], axis=0)
        lowest = low[peer * TOK : (peer + 1) * TOK, :1]
        lowest = jnp.concatenate([lowest, lowest], axis=0)
        high = (place_z * Y_HI + peer) * TOK + lax.rem(row, TOK)
        mixed, logs = softmax_rows(stacked, chunks, lowest, high, scores)
        packed = jnp.zeros((TOK, HEAD_SIZE), jnp.float32)
        pieces = []
        for head in range(2):
            rows = slice(head * TOK, (head + 1) * TOK)
            pieces.append(mixed[rows])
            for place, term in enumerate(three_terms(logs[rows])):
                packed = jnp.where(slot == 3 * head + place, term, packed)
        whole_rows = jnp.concatenate(pieces + [packed], axis=1).astype(jnp.bfloat16)
        sent[peer + Y_HI * upper] = whole_rows[:HALF]
        sent[Y_HI - 1 - peer + Y_HI * (1 - upper)] = whole_rows[HALF:]


def combine_kernel(base, got, out):
    for half in range(2):
        upper = base[2] if half == 0 else 1 - base[2]
        parts = [got[peer + Y_HI * upper].astype(jnp.float32) for peer in range(Y_HI)]
        for head in range(2):
            at = 2 * HEAD_SIZE + 3 * head
            logs = [
                part[:, at : at + 1] + part[:, at + 1 : at + 2] + part[:, at + 2 : at + 3]
                for part in parts
            ]
            top = jnp.maximum(jnp.maximum(logs[0], logs[1]), jnp.maximum(logs[2], logs[3]))
            cols = slice(head * HEAD_SIZE, (head + 1) * HEAD_SIZE)
            mixed = jnp.zeros((HALF, HEAD_SIZE), jnp.float32)
            total = jnp.zeros((HALF, 1), jnp.float32)
            for part, log in zip(parts, logs):
                weight = jnp.exp(log - top)
                mixed = mixed + weight * part[:, cols]
                total = total + weight
            out[half * HALF : (half + 1) * HALF, cols] = (mixed / total).astype(jnp.bfloat16)


def exchange_heads(value):
    return lax.all_to_all(value, "heads", 0, 0, tiled=True)


def exchange_y(value):
    return lax.all_to_all(value, "ctx", 0, 0, tiled=True, axis_index_groups=Y_GROUPS)


def ctx_shift(value, steps):
    return lax.ppermute(value, "ctx", [(i, (i + steps) % N_CTX) for i in range(N_CTX)])


def shards(
    resid_in,
    first_layer_queries,
    first_layer_keys,
    first_layer_values,
    out_one,
    post_gain,
    pre_gain,
    proj_query,
    key_projection,
    value_projection,
    window,
    positions,
):
    ctx_place = lax.axis_index("ctx").astype(jnp.int32)
    place_z, place_y = ctx_place // Y_HI, ctx_place % Y_HI
    bf16, f32 = jnp.bfloat16, jnp.float32
    params = partial(pltpu.CompilerParams, vmem_limit_bytes=VMEM_LIMIT)

    own, spread = pl.pallas_call(
        prepare_kernel,
        out_shape=(
            jax.ShapeDtypeStruct((TOK, 2 * HEAD_SIZE), bf16),
            jax.ShapeDtypeStruct((Y_HI, proj_query.shape[0], 4 * HEAD_SIZE), bf16),
        ),
        in_specs=[whole(pltpu.HBM)] * 5,
        out_specs=(whole(), whole(pltpu.HBM)),
        scratch_shapes=[
            pltpu.VMEM((proj_query.shape[0], 4 * HEAD_SIZE), bf16),
            pltpu.SemaphoreType.DMA((5,)),
            pltpu.SemaphoreType.DMA((Y_HI,)),
        ],
        name="prepare",
    )(first_layer_keys, first_layer_values, proj_query, key_projection, value_projection)
    back_one = ctx_shift(own, Y_HI)
    back_two = ctx_shift(own, 2 * Y_HI)
    weights = exchange_y(spread).reshape(-1, 4 * HEAD_SIZE)
    weights = lax.all_gather(weights, "ctx", axis=0, tiled=True, axis_index_groups=Z_GROUPS)

    bases = jnp.stack([place_z, place_y, place_z // (Z // 2)])
    later = jnp.concatenate([own, back_one], axis=0)
    earlier = jnp.concatenate([back_one, back_two], axis=0)
    peers = jnp.arange(Y_HI, dtype=jnp.int32)[:, None, None]
    window_blocks = jnp.where(peers >= place_y, later[None], earlier[None])
    blocks = exchange_y(window_blocks)

    start = ctx_place * TOK
    tokens = start + jnp.arange(TOK, dtype=jnp.int32)
    local_pos = lax.dynamic_slice_in_dim(positions, start, TOK, 0)
    low_one = jnp.maximum((tokens - local_pos)[None, :], tokens[None, :] - window[:, None] + 1)
    low_one = jnp.broadcast_to(low_one.reshape(2 * TOK, 1), (2 * TOK, 128))
    sent = pl.pallas_call(
        first_kernel,
        out_shape=jax.ShapeDtypeStruct((N_HEADS, ROWS, SLAB), bf16),
        in_specs=[whole(pltpu.SMEM)] + [whole()] * 6,
        out_specs=whole(),
        scratch_shapes=[pltpu.VMEM((2 * TOK, 9 * TOK), f32)],
        compiler_params=params(),
        cost_estimate=pl.CostEstimate(
            flops=600_000_000, bytes_accessed=6_000_000, transcendentals=300_000
        ),
        name="first_layer",
    )(
        bases,
        first_layer_queries,
        blocks,
        back_two,
        low_one,
        out_one,
        resid_in,
    )
    got = exchange_heads(sent)
    sent = pl.pallas_call(
        norm_kernel,
        out_shape=jax.ShapeDtypeStruct((N_HEADS, ROWS, SLAB), bf16),
        in_specs=[whole()] * 3,
        out_specs=whole(),
        scratch_shapes=[pltpu.VMEM((ROWS, WIDTH), f32)] * 2,
        compiler_params=params(),
        name="norms",
    )(got, post_gain[None, :], pre_gain[None, :])
    got = exchange_heads(sent)
    resid_out = got[:, :, WIDTH : WIDTH + COLS].reshape(TOK, COLS)

    speeds = THETA ** (-(jnp.arange(HALF, dtype=f32) * 2.0 / HEAD_SIZE))
    angles = (local_pos.astype(f32) * POSITION_FACTOR)[:, None] * speeds[None, :]
    cosine, sine = jnp.cos(angles), jnp.sin(angles)
    turn_cos = jnp.concatenate([cosine, cosine], axis=1)
    turn_sin = jnp.concatenate([-sine, sine], axis=1)
    query, pair = pl.pallas_call(
        project_kernel,
        out_shape=(
            jax.ShapeDtypeStruct((TOK, 2 * HEAD_SIZE), bf16),
            jax.ShapeDtypeStruct((Z, TOK, 2 * HEAD_SIZE), bf16),
        ),
        in_specs=[whole(), whole(pltpu.HBM), whole(), whole()],
        out_specs=(whole(), whole(pltpu.HBM)),
        scratch_shapes=[
            pltpu.VMEM((WIDTH, 4 * HEAD_SIZE), bf16),
            pltpu.VMEM((TOK, 2 * HEAD_SIZE), bf16),
            pltpu.SemaphoreType.DMA((PARTS,)),
            pltpu.SemaphoreType.DMA((Z,)),
        ],
        compiler_params=pltpu.CompilerParams(vmem_limit_bytes=50 * 1024 * 1024),
        name="project",
    )(got, weights, turn_cos, turn_sin)

    pairs = lax.all_to_all(pair, "ctx", 0, 0, tiled=True, axis_index_groups=Z_GROUPS)
    pairs = pairs.reshape(Z * TOK, 2 * HEAD_SIZE)
    queries = lax.all_gather(
        query, "ctx", axis=0, tiled=True, axis_index_groups=Y_GROUPS
    )

    level = Y_HI * TOK
    first = place_z * level
    low_two = first + jnp.arange(level, dtype=jnp.int32)
    low_two = low_two - lax.dynamic_slice_in_dim(positions, first, level, 0)
    low_two = jnp.broadcast_to(low_two[:, None], (level, 128))
    sent = pl.pallas_call(
        second_kernel,
        out_shape=jax.ShapeDtypeStruct((2 * Y_HI, HALF, 3 * HEAD_SIZE), bf16),
        in_specs=[whole(pltpu.SMEM)] + [whole()] * 3,
        out_specs=whole(),
        scratch_shapes=[pltpu.VMEM((2 * TOK, Z * TOK), f32)],
        compiler_params=params(),
        name="second_layer",
    )(bases, queries, pairs, low_two)
    got = lax.all_to_all(sent, "ctx", 0, 0, tiled=True, axis_index_groups=LEVEL_PAIRS)
    attended = pl.pallas_call(
        combine_kernel,
        out_shape=jax.ShapeDtypeStruct((TOK, 2 * HEAD_SIZE), bf16),
        in_specs=[whole(pltpu.SMEM), whole()],
        out_specs=whole(),
        compiler_params=params(),
        name="combine",
    )(bases, got)
    return (resid_out, attended)


def solution(mesh):
    placed = (
        P("ctx", "heads"),
        P("ctx", "heads"),
        P("ctx", "heads"),
        P("ctx", "heads"),
        P("heads", None),
        P(),
        P(),
        P("ctx", "heads"),
        P("ctx", "heads"),
        P("ctx", "heads"),
        P("heads"),
        P(),
    )
    return jax.shard_map(
        shards,
        mesh=mesh,
        in_specs=placed,
        out_specs=(P("ctx", "heads"), P("ctx", "heads")),
        check_vma=False,
    )
```

```python
from functools import partial

import jax
import jax.numpy as jnp
from jax import lax
from jax.experimental import pallas as pl
from jax.experimental.pallas import tpu as pltpu
from jax.sharding import PartitionSpec as P


HEAD_SIZE = 128
SCALE = 168.0 ** (-0.5)
EPS = 1e-06
THETA = 1000000.0
POSITION_FACTOR = 0.125
N_CTX = 32
N_HEADS = 16
Y_HI = 4
Z = 8
TOK = 128
HALF = 64
WIDTH = 5376
COLS = WIDTH // N_HEADS
SLAB = 5760
ROWS = TOK // N_HEADS
NEG = -1e30
Y_GROUPS = [[z * Y_HI + y for y in range(Y_HI)] for z in range(Z)]
LEVEL_PAIRS = [
    [z * Y_HI + y for y in range(Y_HI)] + [(Z - 1 - z) * Y_HI + y for y in range(Y_HI)]
    for z in range(Z // 2)
]
Z_GROUPS = [[z * Y_HI + y for z in range(Z)] for y in range(Y_HI)]
VMEM_LIMIT = 24 * 1024 * 1024


def whole(memory_space=pltpu.VMEM):
    return pl.BlockSpec(memory_space=memory_space)


def fold_max(peak, part):
    for lane in range(0, part.shape[1], 128):
        peak = jnp.maximum(peak, part[:, lane : lane + 128])
    return peak


def fold_sum(total, part):
    for lane in range(0, part.shape[1], 128):
        total = total + part[:, lane : lane + 128]
    return total


def softmax_rows(query, chunks, low, high, scores):
    rows = query.shape[0]
    peak = jnp.full((rows, 128), NEG, jnp.float32)
    offset = 0
    for load, tokens in chunks:
        keys, _ = load()
        part = (
            lax.dot_general(
                query, keys, (((1,), (1,)), ((), ())), preferred_element_type=jnp.float32
            )
            * SCALE
        )
        width = part.shape[1]
        seen = (tokens >= low) & (tokens <= high)
        part = jnp.where(seen, part, NEG)
        scores[:, offset : offset + width] = part
        peak = fold_max(peak, part)
        offset += width
    top = jnp.max(peak, axis=1, keepdims=True)
    total = jnp.zeros((rows, 128), jnp.float32)
    mixed = jnp.zeros((rows, HEAD_SIZE), jnp.float32)
    offset = 0
    for load, tokens in chunks:
        _, values = load()
        width = values.shape[0]
        lifted = jnp.exp(scores[:, offset : offset + width] - top)
        total = fold_sum(total, lifted)
        mixed = mixed + jnp.dot(
            lifted.astype(jnp.bfloat16), values, preferred_element_type=jnp.float32
        )
        offset += width
    total = jnp.sum(total, axis=1, keepdims=True)
    return mixed / total, top + jnp.log(total)


def first_kernel(base, query, blocks, last, low, out_one, resid, sent, scores):
    place_z, place_y = base[0], base[1]
    start = (place_z * Y_HI + place_y) * TOK
    stacked = jnp.concatenate([query[:, :HEAD_SIZE], query[:, HEAD_SIZE:]], axis=0)
    lowest = low[...][:, :1]
    row = lax.broadcasted_iota(jnp.int32, (2 * TOK, 1), 0)
    high = start + lax.rem(row, TOK)
    lane = lax.broadcasted_iota(jnp.int32, (1, 2 * TOK), 1)
    pair = jnp.where(lane < TOK, lane, lane - (TOK + Y_HI * TOK))
    chunks = []
    for peer in range(Y_HI):
        newer = (place_z - jnp.where(peer > place_y, 1, 0)) * (Y_HI * TOK) + peer * TOK
        chunks.append(
            (
                lambda peer=peer: (
                    blocks[peer, :, :HEAD_SIZE],
                    blocks[peer, :, HEAD_SIZE:],
                ),
                newer + pair,
            )
        )
    chunks.append(
        (
            lambda: (last[:, :HEAD_SIZE], last[:, HEAD_SIZE:]),
            start - 2 * Y_HI * TOK + lane[:, :TOK],
        )
    )
    mixed, _ = softmax_rows(stacked, chunks, lowest, high, scores)
    mixed = mixed.astype(jnp.bfloat16)
    attend = jnp.concatenate([mixed[:TOK], mixed[TOK:]], axis=1)
    step = 768
    for col in range(0, WIDTH, step):
        part = jnp.dot(attend, out_one[:, col : col + step], preferred_element_type=jnp.float32)
        sent[:, :, col : col + step] = part.reshape(N_HEADS, ROWS, step).astype(jnp.bfloat16)
    own = resid[...].astype(jnp.float32).reshape(N_HEADS, ROWS, COLS)
    sent[:, :, WIDTH : WIDTH + COLS] = own.astype(jnp.bfloat16)
    sent[:, :, WIDTH + COLS :] = jnp.zeros((N_HEADS, ROWS, SLAB - WIDTH - COLS), jnp.bfloat16)


def norm_kernel(got, post_gain, pre_gain, sent, rows, wide):
    combined = got[0, :, :WIDTH].astype(jnp.float32)
    for peer in range(1, N_HEADS):
        combined = combined + got[peer, :, :WIDTH].astype(jnp.float32)
    for peer in range(N_HEADS):
        rows[:, peer * COLS : (peer + 1) * COLS] = got[peer, :, WIDTH : WIDTH + COLS].astype(
            jnp.float32
        )
    scale = lax.rsqrt(jnp.mean(combined * combined, axis=1, keepdims=True) + EPS)
    resid = (rows[...] + post_gain[...] * (combined * scale)).astype(jnp.bfloat16)
    widened = resid.astype(jnp.float32)
    scale = lax.rsqrt(jnp.mean(widened * widened, axis=1, keepdims=True) + EPS)
    normed = (pre_gain[...] * widened * scale).astype(jnp.bfloat16)
    wide[...] = widened
    for peer in range(N_HEADS):
        sent[peer, :, :WIDTH] = normed
        sent[peer, :, WIDTH : WIDTH + COLS] = wide[:, peer * COLS : (peer + 1) * COLS].astype(
            jnp.bfloat16
        )
        sent[peer, :, WIDTH + COLS :] = jnp.zeros((ROWS, SLAB - WIDTH - COLS), jnp.bfloat16)


def prepare_kernel(
    keys, values, proj_query, key_projection, value_projection, own, spread, joined, in_sem, out_sem
):
    width = HEAD_SIZE
    moves = [
        pltpu.make_async_copy(source, target, in_sem.at[index])
        for index, (source, target) in enumerate(
            (
                (proj_query, joined.at[:, : 2 * width]),
                (key_projection, joined.at[:, 2 * width : 3 * width]),
                (value_projection, joined.at[:, 3 * width :]),
                (keys, own.at[:, :width]),
                (values, own.at[:, width:]),
            )
        )
    ]
    for move in moves:
        move.start()
    for move in moves[:3]:
        move.wait()
    copies = [
        pltpu.make_async_copy(joined, spread.at[peer], out_sem.at[peer]) for peer in range(Y_HI)
    ]
    for move in copies:
        move.start()
    for move in moves[3:] + copies:
        move.wait()


def project_kernel(base, got, *refs):
    pieces, refs = refs[: Z + 1], refs[Z + 1 :]
    turn_cos, turn_sin, query, pair, held, block, in_sem, out_sem = refs
    level_rows = WIDTH // Z
    offsets = [0, -1, 1, -2, 2, -3, 3, 4, 4]
    for index, (piece, offset) in enumerate(zip(pieces, offsets)):
        level = lax.rem(base[0] + (offset + Z), Z)
        at = level * level_rows + (level_rows // 2 if index == Z else 0)
        target = held.at[pl.ds(pl.multiple_of(at, 16), piece.shape[0])]
        pltpu.make_async_copy(piece, target, in_sem.at[level]).start()
    depth = WIDTH // PARTS
    total = jnp.zeros((TOK, 4 * HEAD_SIZE), jnp.float32)
    arrived = 0
    for part in range(PARTS):
        span = slice(part * depth, (part + 1) * depth)
        rows = got[:, :, span].astype(jnp.float32).reshape(TOK, depth).astype(jnp.bfloat16)
        while arrived * level_rows < (part + 1) * depth:
            rows_of = slice(arrived * level_rows, (arrived + 1) * level_rows)
            pltpu.make_async_copy(pieces[0], held.at[rows_of], in_sem.at[arrived]).wait()
            arrived += 1
        total = total + jnp.dot(rows, held[span, :], preferred_element_type=jnp.float32)
    for head in range(4):
        values = total[:, head * HEAD_SIZE : (head + 1) * HEAD_SIZE]
        if head < 3:
            values = values * turn_cos[...] + pltpu.roll(values, HALF, 1) * turn_sin[...]
        values = values.astype(jnp.bfloat16)
        if head < 2:
            query[:, head * HEAD_SIZE : (head + 1) * HEAD_SIZE] = values
        else:
            block[:, (head - 2) * HEAD_SIZE : (head - 1) * HEAD_SIZE] = values
    moves = [pltpu.make_async_copy(block, pair.at[member], out_sem.at[member]) for member in range(Z)]
    for move in moves:
        move.start()
    for move in moves:
        move.wait()


CHUNK = 256
PARTS = 7


def three_terms(values):
    terms = []
    for _ in range(3):
        term = values.astype(jnp.bfloat16).astype(jnp.float32)
        terms.append(term)
        values = values - term
    return terms


def second_kernel(base, queries, pair, low, sent, scores):
    place_z, place_y, upper = base[0], base[1], base[2]
    lane = lax.broadcasted_iota(jnp.int32, (1, CHUNK), 1)
    lane = jnp.where(lane < TOK, lane, lane + (Y_HI - 1) * TOK)
    row = lax.broadcasted_iota(jnp.int32, (2 * TOK, 1), 0)
    slot = lax.broadcasted_iota(jnp.int32, (TOK, HEAD_SIZE), 1)
    chunks = []
    for at in range(0, Z * TOK, CHUNK):
        chunks.append(
            (
                lambda at=at: (pair[at : at + CHUNK, :HEAD_SIZE], pair[at : at + CHUNK, HEAD_SIZE:]),
                at * Y_HI + place_y * TOK + lane,
            )
        )
    for peer in range(Y_HI):
        block = queries[peer * TOK : (peer + 1) * TOK, :]
        stacked = jnp.concatenate([block[:, :HEAD_SIZE], block[:, HEAD_SIZE:]], axis=0)
        lowest = low[peer * TOK : (peer + 1) * TOK, :1]
        lowest = jnp.concatenate([lowest, lowest], axis=0)
        high = (place_z * Y_HI + peer) * TOK + lax.rem(row, TOK)
        mixed, logs = softmax_rows(stacked, chunks, lowest, high, scores)
        packed = jnp.zeros((TOK, HEAD_SIZE), jnp.float32)
        pieces = []
        for head in range(2):
            rows = slice(head * TOK, (head + 1) * TOK)
            pieces.append(mixed[rows])
            for place, term in enumerate(three_terms(logs[rows])):
                packed = jnp.where(slot == 3 * head + place, term, packed)
        whole_rows = jnp.concatenate(pieces + [packed], axis=1).astype(jnp.bfloat16)
        sent[peer + Y_HI * upper] = whole_rows[:HALF]
        sent[Y_HI - 1 - peer + Y_HI * (1 - upper)] = whole_rows[HALF:]


def combine_kernel(base, got, out):
    for half in range(2):
        upper = base[2] if half == 0 else 1 - base[2]
        parts = [got[peer + Y_HI * upper].astype(jnp.float32) for peer in range(Y_HI)]
        for head in range(2):
            at = 2 * HEAD_SIZE + 3 * head
            logs = [
                part[:, at : at + 1] + part[:, at + 1 : at + 2] + part[:, at + 2 : at + 3]
                for part in parts
            ]
            top = jnp.maximum(jnp.maximum(logs[0], logs[1]), jnp.maximum(logs[2], logs[3]))
            cols = slice(head * HEAD_SIZE, (head + 1) * HEAD_SIZE)
            mixed = jnp.zeros((HALF, HEAD_SIZE), jnp.float32)
            total = jnp.zeros((HALF, 1), jnp.float32)
            for part, log in zip(parts, logs):
                weight = jnp.exp(log - top)
                mixed = mixed + weight * part[:, cols]
                total = total + weight
            out[half * HALF : (half + 1) * HALF, cols] = (mixed / total).astype(jnp.bfloat16)


def exchange_heads(value):
    return lax.all_to_all(value, "heads", 0, 0, tiled=True)


def exchange_y(value):
    return lax.all_to_all(value, "ctx", 0, 0, tiled=True, axis_index_groups=Y_GROUPS)


def ctx_shift(value, steps):
    return lax.ppermute(value, "ctx", [(i, (i + steps) % N_CTX) for i in range(N_CTX)])


def shards(
    resid_in,
    first_layer_queries,
    first_layer_keys,
    first_layer_values,
    out_one,
    post_gain,
    pre_gain,
    proj_query,
    key_projection,
    value_projection,
    window,
    positions,
):
    ctx_place = lax.axis_index("ctx").astype(jnp.int32)
    place_z, place_y = ctx_place // Y_HI, ctx_place % Y_HI
    bf16, f32 = jnp.bfloat16, jnp.float32
    params = partial(pltpu.CompilerParams, vmem_limit_bytes=VMEM_LIMIT)

    own, spread = pl.pallas_call(
        prepare_kernel,
        out_shape=(
            jax.ShapeDtypeStruct((TOK, 2 * HEAD_SIZE), bf16),
            jax.ShapeDtypeStruct((Y_HI, proj_query.shape[0], 4 * HEAD_SIZE), bf16),
        ),
        in_specs=[whole(pltpu.HBM)] * 5,
        out_specs=(whole(), whole(pltpu.HBM)),
        scratch_shapes=[
            pltpu.VMEM((proj_query.shape[0], 4 * HEAD_SIZE), bf16),
            pltpu.SemaphoreType.DMA((5,)),
            pltpu.SemaphoreType.DMA((Y_HI,)),
        ],
        name="prepare",
    )(first_layer_keys, first_layer_values, proj_query, key_projection, value_projection)
    back_one = ctx_shift(own, Y_HI)
    back_two = ctx_shift(own, 2 * Y_HI)
    weights = exchange_y(spread).reshape(-1, 4 * HEAD_SIZE)
    bases = jnp.stack([place_z, place_y, place_z // (Z // 2)])
    pieces = [weights]
    upward, downward = weights, weights
    for _ in range(1, Z // 2):
        upward = ctx_shift(upward, Y_HI)
        downward = ctx_shift(downward, -Y_HI)
        pieces += [upward, downward]
    half_rows = weights.shape[0] // 2
    upward, downward = upward[:half_rows], downward[half_rows:]
    upward = ctx_shift(upward, Y_HI)
    downward = ctx_shift(downward, -Y_HI)
    pieces += [upward, downward]

    later = jnp.concatenate([own, back_one], axis=0)
    earlier = jnp.concatenate([back_one, back_two], axis=0)
    peers = jnp.arange(Y_HI, dtype=jnp.int32)[:, None, None]
    window_blocks = jnp.where(peers >= place_y, later[None], earlier[None])
    blocks = exchange_y(window_blocks)

    start = ctx_place * TOK
    tokens = start + jnp.arange(TOK, dtype=jnp.int32)
    local_pos = lax.dynamic_slice_in_dim(positions, start, TOK, 0)
    low_one = jnp.maximum((tokens - local_pos)[None, :], tokens[None, :] - window[:, None] + 1)
    low_one = jnp.broadcast_to(low_one.reshape(2 * TOK, 1), (2 * TOK, 128))
    sent = pl.pallas_call(
        first_kernel,
        out_shape=jax.ShapeDtypeStruct((N_HEADS, ROWS, SLAB), bf16),
        in_specs=[whole(pltpu.SMEM)] + [whole()] * 6,
        out_specs=whole(),
        scratch_shapes=[pltpu.VMEM((2 * TOK, 9 * TOK), f32)],
        compiler_params=params(),
        cost_estimate=pl.CostEstimate(
            flops=600_000_000, bytes_accessed=6_000_000, transcendentals=300_000
        ),
        name="first_layer",
    )(
        bases,
        first_layer_queries,
        blocks,
        back_two,
        low_one,
        out_one,
        resid_in,
    )
    got = exchange_heads(sent)
    sent = pl.pallas_call(
        norm_kernel,
        out_shape=jax.ShapeDtypeStruct((N_HEADS, ROWS, SLAB), bf16),
        in_specs=[whole()] * 3,
        out_specs=whole(),
        scratch_shapes=[pltpu.VMEM((ROWS, WIDTH), f32)] * 2,
        compiler_params=params(),
        name="norms",
    )(got, post_gain[None, :], pre_gain[None, :])
    got = exchange_heads(sent)
    resid_out = got[:, :, WIDTH : WIDTH + COLS].reshape(TOK, COLS)

    speeds = THETA ** (-(jnp.arange(HALF, dtype=f32) * 2.0 / HEAD_SIZE))
    angles = (local_pos.astype(f32) * POSITION_FACTOR)[:, None] * speeds[None, :]
    cosine, sine = jnp.cos(angles), jnp.sin(angles)
    turn_cos = jnp.concatenate([cosine, cosine], axis=1)
    turn_sin = jnp.concatenate([-sine, sine], axis=1)
    query, pair = pl.pallas_call(
        project_kernel,
        out_shape=(
            jax.ShapeDtypeStruct((TOK, 2 * HEAD_SIZE), bf16),
            jax.ShapeDtypeStruct((Z, TOK, 2 * HEAD_SIZE), bf16),
        ),
        in_specs=[whole(pltpu.SMEM), whole()] + [whole(pltpu.HBM)] * (Z + 1) + [whole(), whole()],
        out_specs=(whole(), whole(pltpu.HBM)),
        scratch_shapes=[
            pltpu.VMEM((WIDTH, 4 * HEAD_SIZE), bf16),
            pltpu.VMEM((TOK, 2 * HEAD_SIZE), bf16),
            pltpu.SemaphoreType.DMA((Z,)),
            pltpu.SemaphoreType.DMA((Z,)),
        ],
        compiler_params=pltpu.CompilerParams(vmem_limit_bytes=50 * 1024 * 1024),
        name="project",
    )(bases, got, *pieces, turn_cos, turn_sin)

    pairs = lax.all_to_all(pair, "ctx", 0, 0, tiled=True, axis_index_groups=Z_GROUPS)
    pairs = pairs.reshape(Z * TOK, 2 * HEAD_SIZE)
    queries = lax.all_gather(
        query, "ctx", axis=0, tiled=True, axis_index_groups=Y_GROUPS
    )

    level = Y_HI * TOK
    first = place_z * level
    low_two = first + jnp.arange(level, dtype=jnp.int32)
    low_two = low_two - lax.dynamic_slice_in_dim(positions, first, level, 0)
    low_two = jnp.broadcast_to(low_two[:, None], (level, 128))
    sent = pl.pallas_call(
        second_kernel,
        out_shape=jax.ShapeDtypeStruct((2 * Y_HI, HALF, 3 * HEAD_SIZE), bf16),
        in_specs=[whole(pltpu.SMEM)] + [whole()] * 3,
        out_specs=whole(),
        scratch_shapes=[pltpu.VMEM((2 * TOK, Z * TOK), f32)],
        compiler_params=params(),
        name="second_layer",
    )(bases, queries, pairs, low_two)
    got = lax.all_to_all(sent, "ctx", 0, 0, tiled=True, axis_index_groups=LEVEL_PAIRS)
    attended = pl.pallas_call(
        combine_kernel,
        out_shape=jax.ShapeDtypeStruct((TOK, 2 * HEAD_SIZE), bf16),
        in_specs=[whole(pltpu.SMEM), whole()],
        out_specs=whole(),
        compiler_params=params(),
        name="combine",
    )(bases, got)
    return (resid_out, attended)


def solution(mesh):
    placed = (
        P("ctx", "heads"),
        P("ctx", "heads"),
        P("ctx", "heads"),
        P("ctx", "heads"),
        P("heads", None),
        P(),
        P(),
        P("ctx", "heads"),
        P("ctx", "heads"),
        P("ctx", "heads"),
        P("heads"),
        P(),
    )
    return jax.shard_map(
        shards,
        mesh=mesh,
        in_specs=placed,
        out_specs=(P("ctx", "heads"), P("ctx", "heads")),
        check_vma=False,
    )
```

```python
from functools import partial

import jax
import jax.numpy as jnp
from jax import lax
from jax.experimental import pallas as pl
from jax.experimental.pallas import tpu as pltpu
from jax.sharding import PartitionSpec as P


HEAD_SIZE = 128
SCALE = 168.0 ** (-0.5)
EPS = 1e-06
THETA = 1000000.0
POSITION_FACTOR = 0.125
N_CTX = 32
N_HEADS = 16
Y_HI = 4
Z = 8
TOK = 128
HALF = 64
WIDTH = 5376
COLS = WIDTH // N_HEADS
SLAB = 5760
ROWS = TOK // N_HEADS
NEG = -1e30
Y_GROUPS = [[z * Y_HI + y for y in range(Y_HI)] for z in range(Z)]
LEVEL_PAIRS = [
    [z * Y_HI + y for y in range(Y_HI)] + [(Z - 1 - z) * Y_HI + y for y in range(Y_HI)]
    for z in range(Z // 2)
]
Z_GROUPS = [[z * Y_HI + y for z in range(Z)] for y in range(Y_HI)]
VMEM_LIMIT = 24 * 1024 * 1024
FIRST_LIMIT = 24 * 1024 * 1024
NORM_LIMIT = 24 * 1024 * 1024
PROJECT_LIMIT = 56 * 1024 * 1024


def whole(memory_space=pltpu.VMEM):
    return pl.BlockSpec(memory_space=memory_space)


def fold_max(peak, part):
    for lane in range(0, part.shape[1], 128):
        peak = jnp.maximum(peak, part[:, lane : lane + 128])
    return peak


def fold_sum(total, part):
    for lane in range(0, part.shape[1], 128):
        total = total + part[:, lane : lane + 128]
    return total


def softmax_rows(query, chunks, low, high, scores):
    rows = query.shape[0]
    peak = jnp.full((rows, 128), NEG, jnp.float32)
    offset = 0
    for load, tokens in chunks:
        keys, _ = load()
        part = (
            lax.dot_general(
                query, keys, (((1,), (1,)), ((), ())), preferred_element_type=jnp.float32
            )
            * SCALE
        )
        width = part.shape[1]
        seen = (tokens >= low) & (tokens <= high)
        part = jnp.where(seen, part, NEG)
        scores[:, offset : offset + width] = part
        peak = fold_max(peak, part)
        offset += width
    top = jnp.max(peak, axis=1, keepdims=True)
    total = jnp.zeros((rows, 128), jnp.float32)
    mixed = jnp.zeros((rows, HEAD_SIZE), jnp.float32)
    offset = 0
    for load, tokens in chunks:
        _, values = load()
        width = values.shape[0]
        lifted = jnp.exp(scores[:, offset : offset + width] - top)
        total = fold_sum(total, lifted)
        mixed = mixed + jnp.dot(
            lifted.astype(jnp.bfloat16), values, preferred_element_type=jnp.float32
        )
        offset += width
    total = jnp.sum(total, axis=1, keepdims=True)
    return mixed / total, top + jnp.log(total)


def first_kernel(base, query, blocks, last, low, out_one, resid, sent, scores):
    place_z, place_y = base[0], base[1]
    start = (place_z * Y_HI + place_y) * TOK
    stacked = jnp.concatenate([query[:, :HEAD_SIZE], query[:, HEAD_SIZE:]], axis=0)
    lowest = low[...][:, :1]
    row = lax.broadcasted_iota(jnp.int32, (2 * TOK, 1), 0)
    high = start + lax.rem(row, TOK)
    lane = lax.broadcasted_iota(jnp.int32, (1, 2 * TOK), 1)
    pair = jnp.where(lane < TOK, lane, lane - (TOK + Y_HI * TOK))
    chunks = []
    for peer in range(Y_HI):
        newer = (place_z - jnp.where(peer > place_y, 1, 0)) * (Y_HI * TOK) + peer * TOK
        chunks.append(
            (
                lambda peer=peer: (
                    blocks[peer, :, :HEAD_SIZE],
                    blocks[peer, :, HEAD_SIZE:],
                ),
                newer + pair,
            )
        )
    chunks.append(
        (
            lambda: (last[:, :HEAD_SIZE], last[:, HEAD_SIZE:]),
            start - 2 * Y_HI * TOK + lane[:, :TOK],
        )
    )
    mixed, _ = softmax_rows(stacked, chunks, lowest, high, scores)
    mixed = mixed.astype(jnp.bfloat16)
    attend = jnp.concatenate([mixed[:TOK], mixed[TOK:]], axis=1)
    step = 768
    for col in range(0, WIDTH, step):
        part = jnp.dot(attend, out_one[:, col : col + step], preferred_element_type=jnp.float32)
        sent[:, :, col : col + step] = part.reshape(N_HEADS, ROWS, step).astype(jnp.bfloat16)
    own = resid[...].astype(jnp.float32).reshape(N_HEADS, ROWS, COLS)
    sent[:, :, WIDTH : WIDTH + COLS] = own.astype(jnp.bfloat16)
    sent[:, :, WIDTH + COLS :] = jnp.zeros((N_HEADS, ROWS, SLAB - WIDTH - COLS), jnp.bfloat16)


def norm_kernel(got, post_gain, pre_gain, sent, rows, wide):
    combined = got[0, :, :WIDTH].astype(jnp.float32)
    for peer in range(1, N_HEADS):
        combined = combined + got[peer, :, :WIDTH].astype(jnp.float32)
    for peer in range(N_HEADS):
        rows[:, peer * COLS : (peer + 1) * COLS] = got[peer, :, WIDTH : WIDTH + COLS].astype(
            jnp.float32
        )
    scale = lax.rsqrt(jnp.mean(combined * combined, axis=1, keepdims=True) + EPS)
    resid = (rows[...] + post_gain[...] * (combined * scale)).astype(jnp.bfloat16)
    widened = resid.astype(jnp.float32)
    scale = lax.rsqrt(jnp.mean(widened * widened, axis=1, keepdims=True) + EPS)
    normed = (pre_gain[...] * widened * scale).astype(jnp.bfloat16)
    wide[...] = widened
    for peer in range(N_HEADS):
        sent[peer, :, :WIDTH] = normed
        sent[peer, :, WIDTH : WIDTH + COLS] = wide[:, peer * COLS : (peer + 1) * COLS].astype(
            jnp.bfloat16
        )
        sent[peer, :, WIDTH + COLS :] = jnp.zeros((ROWS, SLAB - WIDTH - COLS), jnp.bfloat16)


def prepare_kernel(
    keys, values, proj_query, key_projection, value_projection, own, spread, joined, in_sem, out_sem
):
    width = HEAD_SIZE
    moves = [
        pltpu.make_async_copy(source, target, in_sem.at[index])
        for index, (source, target) in enumerate(
            (
                (proj_query, joined.at[:, : 2 * width]),
                (key_projection, joined.at[:, 2 * width : 3 * width]),
                (value_projection, joined.at[:, 3 * width :]),
                (keys, own.at[:, :width]),
                (values, own.at[:, width:]),
            )
        )
    ]
    for move in moves:
        move.start()
    for move in moves[:3]:
        move.wait()
    copies = [
        pltpu.make_async_copy(joined, spread.at[peer], out_sem.at[peer]) for peer in range(Y_HI)
    ]
    for move in copies:
        move.start()
    for move in moves[3:] + copies:
        move.wait()


def project_kernel(base, got, *refs):
    pieces, refs = refs[:Z], refs[Z:]
    turn_cos, turn_sin, query, pair, held, block, in_sem, out_sem = refs
    level_rows = WIDTH // Z
    offsets = [0, -1, -2, -3, -4, 1, 2, 3]
    for piece, offset in zip(pieces, offsets):
        level = lax.rem(base[0] + (offset + Z), Z)
        target = held.at[pl.ds(pl.multiple_of(level * level_rows, 16), level_rows)]
        pltpu.make_async_copy(piece, target, in_sem.at[level]).start()
    depth = WIDTH // PARTS
    total = jnp.zeros((TOK, 4 * HEAD_SIZE), jnp.float32)
    arrived = 0
    for part in range(PARTS):
        span = slice(part * depth, (part + 1) * depth)
        rows = got[:, :, span].astype(jnp.float32).reshape(TOK, depth).astype(jnp.bfloat16)
        while arrived * level_rows < (part + 1) * depth:
            rows_of = slice(arrived * level_rows, (arrived + 1) * level_rows)
            pltpu.make_async_copy(pieces[0], held.at[rows_of], in_sem.at[arrived]).wait()
            arrived += 1
        total = total + jnp.dot(rows, held[span, :], preferred_element_type=jnp.float32)
    for head in range(4):
        values = total[:, head * HEAD_SIZE : (head + 1) * HEAD_SIZE]
        if head < 3:
            values = values * turn_cos[...] + pltpu.roll(values, HALF, 1) * turn_sin[...]
        values = values.astype(jnp.bfloat16)
        if head < 2:
            query[:, head * HEAD_SIZE : (head + 1) * HEAD_SIZE] = values
        else:
            block[:, (head - 2) * HEAD_SIZE : (head - 1) * HEAD_SIZE] = values
    moves = [pltpu.make_async_copy(block, pair.at[member], out_sem.at[member]) for member in range(Z)]
    for move in moves:
        move.start()
    for move in moves:
        move.wait()


CHUNK = 256
PARTS = 7


def three_terms(values):
    terms = []
    for _ in range(3):
        term = values.astype(jnp.bfloat16).astype(jnp.float32)
        terms.append(term)
        values = values - term
    return terms


def second_kernel(base, queries, pair, low, sent, scores):
    place_z, place_y, upper = base[0], base[1], base[2]
    lane = lax.broadcasted_iota(jnp.int32, (1, CHUNK), 1)
    lane = jnp.where(lane < TOK, lane, lane + (Y_HI - 1) * TOK)
    row = lax.broadcasted_iota(jnp.int32, (2 * TOK, 1), 0)
    slot = lax.broadcasted_iota(jnp.int32, (TOK, HEAD_SIZE), 1)
    chunks = []
    for at in range(0, Z * TOK, CHUNK):
        chunks.append(
            (
                lambda at=at: (pair[at : at + CHUNK, :HEAD_SIZE], pair[at : at + CHUNK, HEAD_SIZE:]),
                at * Y_HI + place_y * TOK + lane,
            )
        )
    for peer in range(Y_HI):
        block = queries[peer * TOK : (peer + 1) * TOK, :]
        stacked = jnp.concatenate([block[:, :HEAD_SIZE], block[:, HEAD_SIZE:]], axis=0)
        lowest = low[peer * TOK : (peer + 1) * TOK, :1]
        lowest = jnp.concatenate([lowest, lowest], axis=0)
        high = (place_z * Y_HI + peer) * TOK + lax.rem(row, TOK)
        mixed, logs = softmax_rows(stacked, chunks, lowest, high, scores)
        packed = jnp.zeros((TOK, HEAD_SIZE), jnp.float32)
        pieces = []
        for head in range(2):
            rows = slice(head * TOK, (head + 1) * TOK)
            pieces.append(mixed[rows])
            for place, term in enumerate(three_terms(logs[rows])):
                packed = jnp.where(slot == 3 * head + place, term, packed)
        whole_rows = jnp.concatenate(pieces + [packed], axis=1).astype(jnp.bfloat16)
        sent[peer + Y_HI * upper] = whole_rows[:HALF]
        sent[Y_HI - 1 - peer + Y_HI * (1 - upper)] = whole_rows[HALF:]


def combine_kernel(base, got, out):
    for half in range(2):
        upper = base[2] if half == 0 else 1 - base[2]
        parts = [got[peer + Y_HI * upper].astype(jnp.float32) for peer in range(Y_HI)]
        for head in range(2):
            at = 2 * HEAD_SIZE + 3 * head
            logs = [
                part[:, at : at + 1] + part[:, at + 1 : at + 2] + part[:, at + 2 : at + 3]
                for part in parts
            ]
            top = jnp.maximum(jnp.maximum(logs[0], logs[1]), jnp.maximum(logs[2], logs[3]))
            cols = slice(head * HEAD_SIZE, (head + 1) * HEAD_SIZE)
            mixed = jnp.zeros((HALF, HEAD_SIZE), jnp.float32)
            total = jnp.zeros((HALF, 1), jnp.float32)
            for part, log in zip(parts, logs):
                weight = jnp.exp(log - top)
                mixed = mixed + weight * part[:, cols]
                total = total + weight
            out[half * HALF : (half + 1) * HALF, cols] = (mixed / total).astype(jnp.bfloat16)


def exchange_heads(value):
    return lax.all_to_all(value, "heads", 0, 0, tiled=True)


def exchange_y(value):
    return lax.all_to_all(value, "ctx", 0, 0, tiled=True, axis_index_groups=Y_GROUPS)


def ctx_shift(value, steps):
    return lax.ppermute(value, "ctx", [(i, (i + steps) % N_CTX) for i in range(N_CTX)])


def shards(
    resid_in,
    first_layer_queries,
    first_layer_keys,
    first_layer_values,
    out_one,
    post_gain,
    pre_gain,
    proj_query,
    key_projection,
    value_projection,
    window,
    positions,
):
    ctx_place = lax.axis_index("ctx").astype(jnp.int32)
    place_z, place_y = ctx_place // Y_HI, ctx_place % Y_HI
    bf16, f32 = jnp.bfloat16, jnp.float32
    params = partial(pltpu.CompilerParams, vmem_limit_bytes=VMEM_LIMIT)
    first_params = pltpu.CompilerParams(vmem_limit_bytes=FIRST_LIMIT)
    norm_params = pltpu.CompilerParams(vmem_limit_bytes=NORM_LIMIT)
    project_params = pltpu.CompilerParams(vmem_limit_bytes=PROJECT_LIMIT)

    own, spread = pl.pallas_call(
        prepare_kernel,
        out_shape=(
            jax.ShapeDtypeStruct((TOK, 2 * HEAD_SIZE), bf16),
            jax.ShapeDtypeStruct((Y_HI, proj_query.shape[0], 4 * HEAD_SIZE), bf16),
        ),
        in_specs=[whole(pltpu.HBM)] * 5,
        out_specs=(whole(), whole(pltpu.HBM)),
        scratch_shapes=[
            pltpu.VMEM((proj_query.shape[0], 4 * HEAD_SIZE), bf16),
            pltpu.SemaphoreType.DMA((5,)),
            pltpu.SemaphoreType.DMA((Y_HI,)),
        ],
        name="prepare",
    )(first_layer_keys, first_layer_values, proj_query, key_projection, value_projection)
    back_one = ctx_shift(own, Y_HI)
    back_two = ctx_shift(own, 2 * Y_HI)
    weights = exchange_y(spread).reshape(-1, 4 * HEAD_SIZE)
    bases = jnp.stack([place_z, place_y, place_z // (Z // 2)])
    pieces = [weights]
    for count, sign in ((Z // 2, 1), (Z // 2 - 1, -1)):
        piece = weights
        for _ in range(1, count + 1):
            piece = ctx_shift(piece, sign * Y_HI)
            pieces.append(piece)

    later = jnp.concatenate([own, back_one], axis=0)
    earlier = jnp.concatenate([back_one, back_two], axis=0)
    peers = jnp.arange(Y_HI, dtype=jnp.int32)[:, None, None]
    window_blocks = jnp.where(peers >= place_y, later[None], earlier[None])
    blocks = exchange_y(window_blocks)

    start = ctx_place * TOK
    tokens = start + jnp.arange(TOK, dtype=jnp.int32)
    local_pos = lax.dynamic_slice_in_dim(positions, start, TOK, 0)
    low_one = jnp.maximum((tokens - local_pos)[None, :], tokens[None, :] - window[:, None] + 1)
    low_one = jnp.broadcast_to(low_one.reshape(2 * TOK, 1), (2 * TOK, 128))
    sent = pl.pallas_call(
        first_kernel,
        out_shape=jax.ShapeDtypeStruct((N_HEADS, ROWS, SLAB), bf16),
        in_specs=[whole(pltpu.SMEM)] + [whole()] * 6,
        out_specs=whole(),
        scratch_shapes=[pltpu.VMEM((2 * TOK, 9 * TOK), f32)],
        compiler_params=first_params,
        cost_estimate=pl.CostEstimate(
            flops=600_000_000, bytes_accessed=6_000_000, transcendentals=300_000
        ),
        name="first_layer",
    )(
        bases,
        first_layer_queries,
        blocks,
        back_two,
        low_one,
        out_one,
        resid_in,
    )
    got = exchange_heads(sent)
    sent = pl.pallas_call(
        norm_kernel,
        out_shape=jax.ShapeDtypeStruct((N_HEADS, ROWS, SLAB), bf16),
        in_specs=[whole()] * 3,
        out_specs=whole(),
        scratch_shapes=[pltpu.VMEM((ROWS, WIDTH), f32)] * 2,
        compiler_params=norm_params,
        name="norms",
    )(got, post_gain[None, :], pre_gain[None, :])
    got = exchange_heads(sent)
    resid_out = got[:, :, WIDTH : WIDTH + COLS].reshape(TOK, COLS)

    speeds = THETA ** (-(jnp.arange(HALF, dtype=f32) * 2.0 / HEAD_SIZE))
    angles = (local_pos.astype(f32) * POSITION_FACTOR)[:, None] * speeds[None, :]
    cosine, sine = jnp.cos(angles), jnp.sin(angles)
    turn_cos = jnp.concatenate([cosine, cosine], axis=1)
    turn_sin = jnp.concatenate([-sine, sine], axis=1)
    query, pair = pl.pallas_call(
        project_kernel,
        out_shape=(
            jax.ShapeDtypeStruct((TOK, 2 * HEAD_SIZE), bf16),
            jax.ShapeDtypeStruct((Z, TOK, 2 * HEAD_SIZE), bf16),
        ),
        in_specs=[whole(pltpu.SMEM), whole()] + [whole(pltpu.HBM)] * Z + [whole(), whole()],
        out_specs=(whole(), whole(pltpu.HBM)),
        scratch_shapes=[
            pltpu.VMEM((WIDTH, 4 * HEAD_SIZE), bf16),
            pltpu.VMEM((TOK, 2 * HEAD_SIZE), bf16),
            pltpu.SemaphoreType.DMA((Z,)),
            pltpu.SemaphoreType.DMA((Z,)),
        ],
        compiler_params=project_params,
        name="project",
    )(bases, got, *pieces, turn_cos, turn_sin)

    pairs = lax.all_to_all(pair, "ctx", 0, 0, tiled=True, axis_index_groups=Z_GROUPS)
    pairs = pairs.reshape(Z * TOK, 2 * HEAD_SIZE)
    queries = lax.all_gather(
        query, "ctx", axis=0, tiled=True, axis_index_groups=Y_GROUPS
    )

    level = Y_HI * TOK
    first = place_z * level
    low_two = first + jnp.arange(level, dtype=jnp.int32)
    low_two = low_two - lax.dynamic_slice_in_dim(positions, first, level, 0)
    low_two = jnp.broadcast_to(low_two[:, None], (level, 128))
    sent = pl.pallas_call(
        second_kernel,
        out_shape=jax.ShapeDtypeStruct((2 * Y_HI, HALF, 3 * HEAD_SIZE), bf16),
        in_specs=[whole(pltpu.SMEM)] + [whole()] * 3,
        out_specs=whole(),
        scratch_shapes=[pltpu.VMEM((2 * TOK, Z * TOK), f32)],
        compiler_params=params(),
        name="second_layer",
    )(bases, queries, pairs, low_two)
    got = lax.all_to_all(sent, "ctx", 0, 0, tiled=True, axis_index_groups=LEVEL_PAIRS)
    attended = pl.pallas_call(
        combine_kernel,
        out_shape=jax.ShapeDtypeStruct((TOK, 2 * HEAD_SIZE), bf16),
        in_specs=[whole(pltpu.SMEM), whole()],
        out_specs=whole(),
        compiler_params=params(),
        name="combine",
    )(bases, got)
    return (resid_out, attended)


def solution(mesh):
    placed = (
        P("ctx", "heads"),
        P("ctx", "heads"),
        P("ctx", "heads"),
        P("ctx", "heads"),
        P("heads", None),
        P(),
        P(),
        P("ctx", "heads"),
        P("ctx", "heads"),
        P("ctx", "heads"),
        P("heads"),
        P(),
    )
    return jax.shard_map(
        shards,
        mesh=mesh,
        in_specs=placed,
        out_specs=(P("ctx", "heads"), P("ctx", "heads")),
        check_vma=False,
    )
```

```python
from functools import partial

import jax
import jax.numpy as jnp
from jax import lax
from jax.experimental import pallas as pl
from jax.experimental.pallas import tpu as pltpu
from jax.sharding import PartitionSpec as P


HEAD_SIZE = 128
SCALE = 168.0 ** (-0.5)
EPS = 1e-06
THETA = 1000000.0
POSITION_FACTOR = 0.125
N_CTX = 32
N_HEADS = 16
Y_HI = 4
Z = 8
TOK = 128
HALF = 64
WIDTH = 5376
COLS = WIDTH // N_HEADS
SLAB = 5760
ROWS = TOK // N_HEADS
NEG = -1e30
Y_GROUPS = [[z * Y_HI + y for y in range(Y_HI)] for z in range(Z)]
LEVEL_PAIRS = [
    [z * Y_HI + y for y in range(Y_HI)] + [(Z - 1 - z) * Y_HI + y for y in range(Y_HI)]
    for z in range(Z // 2)
]
Z_GROUPS = [[z * Y_HI + y for z in range(Z)] for y in range(Y_HI)]
VMEM_LIMIT = 24 * 1024 * 1024
FIRST_LIMIT = 24 * 1024 * 1024
NORM_LIMIT = 24 * 1024 * 1024
PROJECT_LIMIT = 56 * 1024 * 1024


def whole(memory_space=pltpu.VMEM):
    return pl.BlockSpec(memory_space=memory_space)


def fold_max(peak, part):
    for lane in range(0, part.shape[1], 128):
        peak = jnp.maximum(peak, part[:, lane : lane + 128])
    return peak


def fold_sum(total, part):
    for lane in range(0, part.shape[1], 128):
        total = total + part[:, lane : lane + 128]
    return total


def softmax_rows(query, chunks, low, high, scores):
    rows = query.shape[0]
    peak = jnp.full((rows, 128), NEG, jnp.float32)
    offset = 0
    for load, tokens in chunks:
        keys, _ = load()
        part = (
            lax.dot_general(
                query, keys, (((1,), (1,)), ((), ())), preferred_element_type=jnp.float32
            )
            * SCALE
        )
        width = part.shape[1]
        seen = (tokens >= low) & (tokens <= high)
        part = jnp.where(seen, part, NEG)
        scores[:, offset : offset + width] = part
        peak = fold_max(peak, part)
        offset += width
    top = jnp.max(peak, axis=1, keepdims=True)
    total = jnp.zeros((rows, 128), jnp.float32)
    mixed = jnp.zeros((rows, HEAD_SIZE), jnp.float32)
    offset = 0
    for load, tokens in chunks:
        _, values = load()
        width = values.shape[0]
        lifted = jnp.exp(scores[:, offset : offset + width] - top)
        total = fold_sum(total, lifted)
        mixed = mixed + jnp.dot(
            lifted.astype(jnp.bfloat16), values, preferred_element_type=jnp.float32
        )
        offset += width
    total = jnp.sum(total, axis=1, keepdims=True)
    return mixed / total, top + jnp.log(total)


def first_kernel(base, query, blocks, last, low, out_one, resid, sent, scores):
    place_z, place_y = base[0], base[1]
    start = (place_z * Y_HI + place_y) * TOK
    stacked = jnp.concatenate([query[:, :HEAD_SIZE], query[:, HEAD_SIZE:]], axis=0)
    lowest = low[...][:, :1]
    row = lax.broadcasted_iota(jnp.int32, (2 * TOK, 1), 0)
    high = start + lax.rem(row, TOK)
    lane = lax.broadcasted_iota(jnp.int32, (1, 2 * TOK), 1)
    pair = jnp.where(lane < TOK, lane, lane - (TOK + Y_HI * TOK))
    chunks = []
    for peer in range(Y_HI):
        newer = (place_z - jnp.where(peer > place_y, 1, 0)) * (Y_HI * TOK) + peer * TOK
        chunks.append(
            (
                lambda peer=peer: (
                    blocks[peer, :, :HEAD_SIZE],
                    blocks[peer, :, HEAD_SIZE:],
                ),
                newer + pair,
            )
        )
    chunks.append(
        (
            lambda: (last[:, :HEAD_SIZE], last[:, HEAD_SIZE:]),
            start - 2 * Y_HI * TOK + lane[:, :TOK],
        )
    )
    mixed, _ = softmax_rows(stacked, chunks, lowest, high, scores)
    mixed = mixed.astype(jnp.bfloat16)
    attend = jnp.concatenate([mixed[:TOK], mixed[TOK:]], axis=1)
    step = 768
    for col in range(0, WIDTH, step):
        part = jnp.dot(attend, out_one[:, col : col + step], preferred_element_type=jnp.float32)
        sent[:, :, col : col + step] = part.reshape(N_HEADS, ROWS, step).astype(jnp.bfloat16)
    own = resid[...].astype(jnp.float32).reshape(N_HEADS, ROWS, COLS)
    sent[:, :, WIDTH : WIDTH + COLS] = own.astype(jnp.bfloat16)
    sent[:, :, WIDTH + COLS :] = jnp.zeros((N_HEADS, ROWS, SLAB - WIDTH - COLS), jnp.bfloat16)


def norm_kernel(got, post_gain, pre_gain, sent, rows, wide):
    combined = got[0, :, :WIDTH].astype(jnp.float32)
    for peer in range(1, N_HEADS):
        combined = combined + got[peer, :, :WIDTH].astype(jnp.float32)
    for peer in range(N_HEADS):
        rows[:, peer * COLS : (peer + 1) * COLS] = got[peer, :, WIDTH : WIDTH + COLS].astype(
            jnp.float32
        )
    scale = lax.rsqrt(jnp.mean(combined * combined, axis=1, keepdims=True) + EPS)
    resid = (rows[...] + post_gain[...] * (combined * scale)).astype(jnp.bfloat16)
    widened = resid.astype(jnp.float32)
    scale = lax.rsqrt(jnp.mean(widened * widened, axis=1, keepdims=True) + EPS)
    normed = (pre_gain[...] * widened * scale).astype(jnp.bfloat16)
    wide[...] = widened
    for peer in range(N_HEADS):
        sent[peer, :, :WIDTH] = normed
        sent[peer, :, WIDTH : WIDTH + COLS] = wide[:, peer * COLS : (peer + 1) * COLS].astype(
            jnp.bfloat16
        )
        sent[peer, :, WIDTH + COLS :] = jnp.zeros((ROWS, SLAB - WIDTH - COLS), jnp.bfloat16)


def prepare_kernel(
    keys, values, proj_query, key_projection, value_projection, own, spread, joined, in_sem, out_sem
):
    width = HEAD_SIZE
    moves = [
        pltpu.make_async_copy(source, target, in_sem.at[index])
        for index, (source, target) in enumerate(
            (
                (proj_query, joined.at[:, : 2 * width]),
                (key_projection, joined.at[:, 2 * width : 3 * width]),
                (value_projection, joined.at[:, 3 * width :]),
                (keys, own.at[:, :width]),
                (values, own.at[:, width:]),
            )
        )
    ]
    for move in moves:
        move.start()
    for move in moves[:3]:
        move.wait()
    copies = [
        pltpu.make_async_copy(joined, spread.at[peer], out_sem.at[peer]) for peer in range(Y_HI)
    ]
    for move in copies:
        move.start()
    for move in moves[3:] + copies:
        move.wait()


def project_kernel(base, got, *refs):
    pieces, refs = refs[:Z], refs[Z:]
    turn_cos, turn_sin, query, pair, held, normed, block, in_sem, row_sem, out_sem = refs
    level_rows = WIDTH // Z
    depth = WIDTH // PARTS
    offsets = [0, -1, -2, -3, -4, 1, 2, 3]

    def row_move(part):
        span = pl.ds(part * depth, depth)
        return pltpu.make_async_copy(got.at[:, :, span], normed.at[:, :, span], row_sem.at[part])

    for level in range(Z):
        if level < PARTS:
            row_move(level).start()
        target = held.at[level * level_rows : (level + 1) * level_rows]
        for piece, offset in zip(pieces, offsets):

            @pl.when(lax.rem(base[0] + (offset + Z), Z) == level)
            def _(piece=piece):
                pltpu.make_async_copy(piece, target, in_sem.at[level]).start()

    total = jnp.zeros((TOK, 4 * HEAD_SIZE), jnp.float32)
    arrived = 0
    for part in range(PARTS):
        span = slice(part * depth, (part + 1) * depth)
        row_move(part).wait()
        rows = normed[:, :, span].astype(jnp.float32).reshape(TOK, depth).astype(jnp.bfloat16)
        while arrived * level_rows < (part + 1) * depth:
            rows_of = slice(arrived * level_rows, (arrived + 1) * level_rows)
            pltpu.make_async_copy(pieces[0], held.at[rows_of], in_sem.at[arrived]).wait()
            arrived += 1
        total = total + jnp.dot(rows, held[span, :], preferred_element_type=jnp.float32)
    for head in range(4):
        values = total[:, head * HEAD_SIZE : (head + 1) * HEAD_SIZE]
        if head < 3:
            values = values * turn_cos[...] + pltpu.roll(values, HALF, 1) * turn_sin[...]
        values = values.astype(jnp.bfloat16)
        if head < 2:
            query[:, head * HEAD_SIZE : (head + 1) * HEAD_SIZE] = values
        else:
            block[:, (head - 2) * HEAD_SIZE : (head - 1) * HEAD_SIZE] = values
    moves = [pltpu.make_async_copy(block, pair.at[member], out_sem.at[member]) for member in range(Z)]
    for move in moves:
        move.start()
    for move in moves:
        move.wait()


CHUNK = 256
PARTS = 7


def three_terms(values):
    terms = []
    for _ in range(3):
        term = values.astype(jnp.bfloat16).astype(jnp.float32)
        terms.append(term)
        values = values - term
    return terms


def second_kernel(base, queries, pair, low, sent, scores):
    place_z, place_y, upper = base[0], base[1], base[2]
    lane = lax.broadcasted_iota(jnp.int32, (1, CHUNK), 1)
    lane = jnp.where(lane < TOK, lane, lane + (Y_HI - 1) * TOK)
    row = lax.broadcasted_iota(jnp.int32, (2 * TOK, 1), 0)
    slot = lax.broadcasted_iota(jnp.int32, (TOK, HEAD_SIZE), 1)
    chunks = []
    for at in range(0, Z * TOK, CHUNK):
        chunks.append(
            (
                lambda at=at: (pair[at : at + CHUNK, :HEAD_SIZE], pair[at : at + CHUNK, HEAD_SIZE:]),
                at * Y_HI + place_y * TOK + lane,
            )
        )
    for peer in range(Y_HI):
        block = queries[peer * TOK : (peer + 1) * TOK, :]
        stacked = jnp.concatenate([block[:, :HEAD_SIZE], block[:, HEAD_SIZE:]], axis=0)
        lowest = low[peer * TOK : (peer + 1) * TOK, :1]
        lowest = jnp.concatenate([lowest, lowest], axis=0)
        high = (place_z * Y_HI + peer) * TOK + lax.rem(row, TOK)
        mixed, logs = softmax_rows(stacked, chunks, lowest, high, scores)
        packed = jnp.zeros((TOK, HEAD_SIZE), jnp.float32)
        pieces = []
        for head in range(2):
            rows = slice(head * TOK, (head + 1) * TOK)
            pieces.append(mixed[rows])
            for place, term in enumerate(three_terms(logs[rows])):
                packed = jnp.where(slot == 3 * head + place, term, packed)
        whole_rows = jnp.concatenate(pieces + [packed], axis=1).astype(jnp.bfloat16)
        sent[peer + Y_HI * upper] = whole_rows[:HALF]
        sent[Y_HI - 1 - peer + Y_HI * (1 - upper)] = whole_rows[HALF:]


def combine_kernel(base, got, out):
    for half in range(2):
        upper = base[2] if half == 0 else 1 - base[2]
        parts = [got[peer + Y_HI * upper].astype(jnp.float32) for peer in range(Y_HI)]
        for head in range(2):
            at = 2 * HEAD_SIZE + 3 * head
            logs = [
                part[:, at : at + 1] + part[:, at + 1 : at + 2] + part[:, at + 2 : at + 3]
                for part in parts
            ]
            top = jnp.maximum(jnp.maximum(logs[0], logs[1]), jnp.maximum(logs[2], logs[3]))
            cols = slice(head * HEAD_SIZE, (head + 1) * HEAD_SIZE)
            mixed = jnp.zeros((HALF, HEAD_SIZE), jnp.float32)
            total = jnp.zeros((HALF, 1), jnp.float32)
            for part, log in zip(parts, logs):
                weight = jnp.exp(log - top)
                mixed = mixed + weight * part[:, cols]
                total = total + weight
            out[half * HALF : (half + 1) * HALF, cols] = (mixed / total).astype(jnp.bfloat16)


def exchange_heads(value):
    return lax.all_to_all(value, "heads", 0, 0, tiled=True)


def exchange_y(value):
    return lax.all_to_all(value, "ctx", 0, 0, tiled=True, axis_index_groups=Y_GROUPS)


def ctx_shift(value, steps):
    return lax.ppermute(value, "ctx", [(i, (i + steps) % N_CTX) for i in range(N_CTX)])


def shards(
    resid_in,
    first_layer_queries,
    first_layer_keys,
    first_layer_values,
    out_one,
    post_gain,
    pre_gain,
    proj_query,
    key_projection,
    value_projection,
    window,
    positions,
):
    ctx_place = lax.axis_index("ctx").astype(jnp.int32)
    place_z, place_y = ctx_place // Y_HI, ctx_place % Y_HI
    bf16, f32 = jnp.bfloat16, jnp.float32
    params = partial(pltpu.CompilerParams, vmem_limit_bytes=VMEM_LIMIT)
    first_params = pltpu.CompilerParams(vmem_limit_bytes=FIRST_LIMIT)
    norm_params = pltpu.CompilerParams(vmem_limit_bytes=NORM_LIMIT)
    project_params = pltpu.CompilerParams(vmem_limit_bytes=PROJECT_LIMIT)

    own, spread = pl.pallas_call(
        prepare_kernel,
        out_shape=(
            jax.ShapeDtypeStruct((TOK, 2 * HEAD_SIZE), bf16),
            jax.ShapeDtypeStruct((Y_HI, proj_query.shape[0], 4 * HEAD_SIZE), bf16),
        ),
        in_specs=[whole(pltpu.HBM)] * 5,
        out_specs=(whole(), whole(pltpu.HBM)),
        scratch_shapes=[
            pltpu.VMEM((proj_query.shape[0], 4 * HEAD_SIZE), bf16),
            pltpu.SemaphoreType.DMA((5,)),
            pltpu.SemaphoreType.DMA((Y_HI,)),
        ],
        name="prepare",
    )(first_layer_keys, first_layer_values, proj_query, key_projection, value_projection)
    back_one = ctx_shift(own, Y_HI)
    back_two = ctx_shift(own, 2 * Y_HI)
    weights = exchange_y(spread).reshape(-1, 4 * HEAD_SIZE)
    bases = jnp.stack([place_z, place_y, place_z // (Z // 2)])
    pieces = [weights]
    for count, sign in ((Z // 2, 1), (Z // 2 - 1, -1)):
        piece = weights
        for _ in range(1, count + 1):
            piece = ctx_shift(piece, sign * Y_HI)
            pieces.append(piece)

    later = jnp.concatenate([own, back_one], axis=0)
    earlier = jnp.concatenate([back_one, back_two], axis=0)
    peers = jnp.arange(Y_HI, dtype=jnp.int32)[:, None, None]
    window_blocks = jnp.where(peers >= place_y, later[None], earlier[None])
    blocks = exchange_y(window_blocks)

    start = ctx_place * TOK
    tokens = start + jnp.arange(TOK, dtype=jnp.int32)
    local_pos = lax.dynamic_slice_in_dim(positions, start, TOK, 0)
    low_one = jnp.maximum((tokens - local_pos)[None, :], tokens[None, :] - window[:, None] + 1)
    low_one = jnp.broadcast_to(low_one.reshape(2 * TOK, 1), (2 * TOK, 128))
    sent = pl.pallas_call(
        first_kernel,
        out_shape=jax.ShapeDtypeStruct((N_HEADS, ROWS, SLAB), bf16),
        in_specs=[whole(pltpu.SMEM)] + [whole()] * 6,
        out_specs=whole(),
        scratch_shapes=[pltpu.VMEM((2 * TOK, 9 * TOK), f32)],
        compiler_params=first_params,
        cost_estimate=pl.CostEstimate(
            flops=600_000_000, bytes_accessed=6_000_000, transcendentals=300_000
        ),
        name="first_layer",
    )(
        bases,
        first_layer_queries,
        blocks,
        back_two,
        low_one,
        out_one,
        resid_in,
    )
    got = exchange_heads(sent)
    sent = pl.pallas_call(
        norm_kernel,
        out_shape=jax.ShapeDtypeStruct((N_HEADS, ROWS, SLAB), bf16),
        in_specs=[whole()] * 3,
        out_specs=whole(),
        scratch_shapes=[pltpu.VMEM((ROWS, WIDTH), f32)] * 2,
        compiler_params=norm_params,
        name="norms",
    )(got, post_gain[None, :], pre_gain[None, :])
    got = exchange_heads(sent)
    resid_out = got[:, :, WIDTH : WIDTH + COLS].reshape(TOK, COLS)

    speeds = THETA ** (-(jnp.arange(HALF, dtype=f32) * 2.0 / HEAD_SIZE))
    angles = (local_pos.astype(f32) * POSITION_FACTOR)[:, None] * speeds[None, :]
    cosine, sine = jnp.cos(angles), jnp.sin(angles)
    turn_cos = jnp.concatenate([cosine, cosine], axis=1)
    turn_sin = jnp.concatenate([-sine, sine], axis=1)
    query, pair = pl.pallas_call(
        project_kernel,
        out_shape=(
            jax.ShapeDtypeStruct((TOK, 2 * HEAD_SIZE), bf16),
            jax.ShapeDtypeStruct((Z, TOK, 2 * HEAD_SIZE), bf16),
        ),
        in_specs=[whole(pltpu.SMEM)] + [whole(pltpu.HBM)] * (Z + 1) + [whole(), whole()],
        out_specs=(whole(), whole(pltpu.HBM)),
        scratch_shapes=[
            pltpu.VMEM((WIDTH, 4 * HEAD_SIZE), bf16),
            pltpu.VMEM((N_HEADS, ROWS, WIDTH), bf16),
            pltpu.VMEM((TOK, 2 * HEAD_SIZE), bf16),
            pltpu.SemaphoreType.DMA((Z,)),
            pltpu.SemaphoreType.DMA((PARTS,)),
            pltpu.SemaphoreType.DMA((Z,)),
        ],
        compiler_params=project_params,
        name="project",
    )(bases, got, *pieces, turn_cos, turn_sin)

    pairs = lax.all_to_all(pair, "ctx", 0, 0, tiled=True, axis_index_groups=Z_GROUPS)
    pairs = pairs.reshape(Z * TOK, 2 * HEAD_SIZE)
    queries = lax.all_gather(
        query, "ctx", axis=0, tiled=True, axis_index_groups=Y_GROUPS
    )

    level = Y_HI * TOK
    first = place_z * level
    low_two = first + jnp.arange(level, dtype=jnp.int32)
    low_two = low_two - lax.dynamic_slice_in_dim(positions, first, level, 0)
    low_two = jnp.broadcast_to(low_two[:, None], (level, 128))
    sent = pl.pallas_call(
        second_kernel,
        out_shape=jax.ShapeDtypeStruct((2 * Y_HI, HALF, 3 * HEAD_SIZE), bf16),
        in_specs=[whole(pltpu.SMEM)] + [whole()] * 3,
        out_specs=whole(),
        scratch_shapes=[pltpu.VMEM((2 * TOK, Z * TOK), f32)],
        compiler_params=params(),
        name="second_layer",
    )(bases, queries, pairs, low_two)
    got = lax.all_to_all(sent, "ctx", 0, 0, tiled=True, axis_index_groups=LEVEL_PAIRS)
    attended = pl.pallas_call(
        combine_kernel,
        out_shape=jax.ShapeDtypeStruct((TOK, 2 * HEAD_SIZE), bf16),
        in_specs=[whole(pltpu.SMEM), whole()],
        out_specs=whole(),
        compiler_params=params(),
        name="combine",
    )(bases, got)
    return (resid_out, attended)


def solution(mesh):
    placed = (
        P("ctx", "heads"),
        P("ctx", "heads"),
        P("ctx", "heads"),
        P("ctx", "heads"),
        P("heads", None),
        P(),
        P(),
        P("ctx", "heads"),
        P("ctx", "heads"),
        P("ctx", "heads"),
        P("heads"),
        P(),
    )
    return jax.shard_map(
        shards,
        mesh=mesh,
        in_specs=placed,
        out_specs=(P("ctx", "heads"), P("ctx", "heads")),
        check_vma=False,
    )
```

```python
from functools import partial

import jax
import jax.numpy as jnp
from jax import lax
from jax.experimental import pallas as pl
from jax.experimental.pallas import tpu as pltpu
from jax.sharding import PartitionSpec as P


HEAD_SIZE = 128
SCALE = 168.0 ** (-0.5)
EPS = 1e-06
THETA = 1000000.0
POSITION_FACTOR = 0.125
N_CTX = 32
N_HEADS = 16
Y_HI = 4
Z = 8
TOK = 128
HALF = 64
WIDTH = 5376
COLS = WIDTH // N_HEADS
SLAB = 5760
ROWS = TOK // N_HEADS
NEG = -1e30
Y_GROUPS = [[z * Y_HI + y for y in range(Y_HI)] for z in range(Z)]
LEVEL_PAIRS = [
    [z * Y_HI + y for y in range(Y_HI)] + [(Z - 1 - z) * Y_HI + y for y in range(Y_HI)]
    for z in range(Z // 2)
]
Z_GROUPS = [[z * Y_HI + y for z in range(Z)] for y in range(Y_HI)]
VMEM_LIMIT = 24 * 1024 * 1024
FIRST_LIMIT = 24 * 1024 * 1024
NORM_LIMIT = 24 * 1024 * 1024
PROJECT_LIMIT = 56 * 1024 * 1024


def whole(memory_space=pltpu.VMEM):
    return pl.BlockSpec(memory_space=memory_space)


def fold_max(peak, part):
    for lane in range(0, part.shape[1], 128):
        peak = jnp.maximum(peak, part[:, lane : lane + 128])
    return peak


def fold_sum(total, part):
    for lane in range(0, part.shape[1], 128):
        total = total + part[:, lane : lane + 128]
    return total


def softmax_rows(query, chunks, low, high, scores):
    rows = query.shape[0]
    peak = jnp.full((rows, 128), NEG, jnp.float32)
    offset = 0
    for load, tokens in chunks:
        keys, _ = load()
        part = (
            lax.dot_general(
                query, keys, (((1,), (1,)), ((), ())), preferred_element_type=jnp.float32
            )
            * SCALE
        )
        width = part.shape[1]
        seen = (tokens >= low) & (tokens <= high)
        part = jnp.where(seen, part, NEG)
        scores[:, offset : offset + width] = part
        peak = fold_max(peak, part)
        offset += width
    top = jnp.max(peak, axis=1, keepdims=True)
    total = jnp.zeros((rows, 128), jnp.float32)
    mixed = jnp.zeros((rows, HEAD_SIZE), jnp.float32)
    offset = 0
    for load, tokens in chunks:
        _, values = load()
        width = values.shape[0]
        lifted = jnp.exp(scores[:, offset : offset + width] - top)
        total = fold_sum(total, lifted)
        mixed = mixed + jnp.dot(
            lifted.astype(jnp.bfloat16), values, preferred_element_type=jnp.float32
        )
        offset += width
    total = jnp.sum(total, axis=1, keepdims=True)
    return mixed / total, top + jnp.log(total)


def first_kernel(base, query, blocks, last, low, out_one, resid, sent, scores):
    place_z, place_y = base[0], base[1]
    start = (place_z * Y_HI + place_y) * TOK
    stacked = jnp.concatenate([query[:, :HEAD_SIZE], query[:, HEAD_SIZE:]], axis=0)
    lowest = low[...][:, :1]
    row = lax.broadcasted_iota(jnp.int32, (2 * TOK, 1), 0)
    high = start + lax.rem(row, TOK)
    lane = lax.broadcasted_iota(jnp.int32, (1, 2 * TOK), 1)
    pair = jnp.where(lane < TOK, lane, lane - (TOK + Y_HI * TOK))
    chunks = []
    for peer in range(Y_HI):
        newer = (place_z - jnp.where(peer > place_y, 1, 0)) * (Y_HI * TOK) + peer * TOK
        chunks.append(
            (
                lambda peer=peer: (
                    blocks[peer, :, :HEAD_SIZE],
                    blocks[peer, :, HEAD_SIZE:],
                ),
                newer + pair,
            )
        )
    chunks.append(
        (
            lambda: (last[:, :HEAD_SIZE], last[:, HEAD_SIZE:]),
            start - 2 * Y_HI * TOK + lane[:, :TOK],
        )
    )
    mixed, _ = softmax_rows(stacked, chunks, lowest, high, scores)
    mixed = mixed.astype(jnp.bfloat16)
    attend = jnp.concatenate([mixed[:TOK], mixed[TOK:]], axis=1)
    step = 768
    for col in range(0, WIDTH, step):
        part = jnp.dot(attend, out_one[:, col : col + step], preferred_element_type=jnp.float32)
        sent[:, :, col : col + step] = part.reshape(N_HEADS, ROWS, step).astype(jnp.bfloat16)
    own = resid[...].astype(jnp.float32).reshape(N_HEADS, ROWS, COLS)
    sent[:, :, WIDTH : WIDTH + COLS] = own.astype(jnp.bfloat16)
    sent[:, :, WIDTH + COLS :] = jnp.zeros((N_HEADS, ROWS, SLAB - WIDTH - COLS), jnp.bfloat16)


def norm_kernel(got, post_gain, pre_gain, sent, rows, wide):
    combined = got[0, :, :WIDTH].astype(jnp.float32)
    for peer in range(1, N_HEADS):
        combined = combined + got[peer, :, :WIDTH].astype(jnp.float32)
    for peer in range(N_HEADS):
        rows[:, peer * COLS : (peer + 1) * COLS] = got[peer, :, WIDTH : WIDTH + COLS].astype(
            jnp.float32
        )
    scale = lax.rsqrt(jnp.mean(combined * combined, axis=1, keepdims=True) + EPS)
    resid = (rows[...] + post_gain[...] * (combined * scale)).astype(jnp.bfloat16)
    widened = resid.astype(jnp.float32)
    scale = lax.rsqrt(jnp.mean(widened * widened, axis=1, keepdims=True) + EPS)
    normed = (pre_gain[...] * widened * scale).astype(jnp.bfloat16)
    wide[...] = widened
    for peer in range(N_HEADS):
        sent[peer, :, :WIDTH] = normed
        sent[peer, :, WIDTH : WIDTH + COLS] = wide[:, peer * COLS : (peer + 1) * COLS].astype(
            jnp.bfloat16
        )
        sent[peer, :, WIDTH + COLS :] = jnp.zeros((ROWS, SLAB - WIDTH - COLS), jnp.bfloat16)


def prepare_kernel(
    keys, values, proj_query, key_projection, value_projection, own, spread, joined, in_sem, out_sem
):
    width = HEAD_SIZE
    moves = [
        pltpu.make_async_copy(source, target, in_sem.at[index])
        for index, (source, target) in enumerate(
            (
                (proj_query, joined.at[:, : 2 * width]),
                (key_projection, joined.at[:, 2 * width : 3 * width]),
                (value_projection, joined.at[:, 3 * width :]),
                (keys, own.at[:, :width]),
                (values, own.at[:, width:]),
            )
        )
    ]
    for move in moves:
        move.start()
    for move in moves[:3]:
        move.wait()
    copies = [
        pltpu.make_async_copy(joined, spread.at[peer], out_sem.at[peer]) for peer in range(Y_HI)
    ]
    for move in copies:
        move.start()
    for move in moves[3:] + copies:
        move.wait()


def project_kernel(base, got, *refs):
    pieces, refs = refs[: Z + 1], refs[Z + 1 :]
    turn_cos, turn_sin, query, pair, held, normed, block, in_sem, row_sem, out_sem = refs
    level_rows = WIDTH // Z
    depth = WIDTH // PARTS
    offsets = [0, -1, 1, -2, 2, -3, 3, 4, 4]
    for index, (piece, offset) in enumerate(zip(pieces, offsets)):
        level = lax.rem(base[0] + (offset + Z), Z)
        at = level * level_rows + (level_rows // 2 if index == Z else 0)
        target = held.at[pl.ds(pl.multiple_of(at, 16), piece.shape[0])]
        pltpu.make_async_copy(piece, target, in_sem.at[level]).start()

    def row_move(part):
        span = pl.ds(part * depth, depth)
        return pltpu.make_async_copy(got.at[:, :, span], normed.at[:, :, span], row_sem.at[part])

    for part in range(PARTS):
        row_move(part).start()
    total = jnp.zeros((TOK, 4 * HEAD_SIZE), jnp.float32)
    arrived = 0
    for part in range(PARTS):
        span = slice(part * depth, (part + 1) * depth)
        row_move(part).wait()
        rows = normed[:, :, span].astype(jnp.float32).reshape(TOK, depth).astype(jnp.bfloat16)
        while arrived * level_rows < (part + 1) * depth:
            rows_of = slice(arrived * level_rows, (arrived + 1) * level_rows)
            pltpu.make_async_copy(pieces[0], held.at[rows_of], in_sem.at[arrived]).wait()
            arrived += 1
        total = total + jnp.dot(rows, held[span, :], preferred_element_type=jnp.float32)
    for head in range(4):
        values = total[:, head * HEAD_SIZE : (head + 1) * HEAD_SIZE]
        if head < 3:
            values = values * turn_cos[...] + pltpu.roll(values, HALF, 1) * turn_sin[...]
        values = values.astype(jnp.bfloat16)
        if head < 2:
            query[:, head * HEAD_SIZE : (head + 1) * HEAD_SIZE] = values
        else:
            block[:, (head - 2) * HEAD_SIZE : (head - 1) * HEAD_SIZE] = values
    moves = [pltpu.make_async_copy(block, pair.at[member], out_sem.at[member]) for member in range(Z)]
    for move in moves:
        move.start()
    for move in moves:
        move.wait()


CHUNK = 256
PARTS = 7


def three_terms(values):
    terms = []
    for _ in range(3):
        term = values.astype(jnp.bfloat16).astype(jnp.float32)
        terms.append(term)
        values = values - term
    return terms


def second_kernel(base, queries, pair, low, sent, scores):
    place_z, place_y, upper = base[0], base[1], base[2]
    lane = lax.broadcasted_iota(jnp.int32, (1, CHUNK), 1)
    lane = jnp.where(lane < TOK, lane, lane + (Y_HI - 1) * TOK)
    row = lax.broadcasted_iota(jnp.int32, (2 * TOK, 1), 0)
    slot = lax.broadcasted_iota(jnp.int32, (TOK, HEAD_SIZE), 1)
    chunks = []
    for at in range(0, Z * TOK, CHUNK):
        chunks.append(
            (
                lambda at=at: (pair[at : at + CHUNK, :HEAD_SIZE], pair[at : at + CHUNK, HEAD_SIZE:]),
                at * Y_HI + place_y * TOK + lane,
            )
        )
    for peer in range(Y_HI):
        block = queries[peer * TOK : (peer + 1) * TOK, :]
        stacked = jnp.concatenate([block[:, :HEAD_SIZE], block[:, HEAD_SIZE:]], axis=0)
        lowest = low[peer * TOK : (peer + 1) * TOK, :1]
        lowest = jnp.concatenate([lowest, lowest], axis=0)
        high = (place_z * Y_HI + peer) * TOK + lax.rem(row, TOK)
        mixed, logs = softmax_rows(stacked, chunks, lowest, high, scores)
        packed = jnp.zeros((TOK, HEAD_SIZE), jnp.float32)
        pieces = []
        for head in range(2):
            rows = slice(head * TOK, (head + 1) * TOK)
            pieces.append(mixed[rows])
            for place, term in enumerate(three_terms(logs[rows])):
                packed = jnp.where(slot == 3 * head + place, term, packed)
        whole_rows = jnp.concatenate(pieces + [packed], axis=1).astype(jnp.bfloat16)
        sent[peer + Y_HI * upper] = whole_rows[:HALF]
        sent[Y_HI - 1 - peer + Y_HI * (1 - upper)] = whole_rows[HALF:]


def combine_kernel(base, got, out):
    for half in range(2):
        upper = base[2] if half == 0 else 1 - base[2]
        parts = [got[peer + Y_HI * upper].astype(jnp.float32) for peer in range(Y_HI)]
        for head in range(2):
            at = 2 * HEAD_SIZE + 3 * head
            logs = [
                part[:, at : at + 1] + part[:, at + 1 : at + 2] + part[:, at + 2 : at + 3]
                for part in parts
            ]
            top = jnp.maximum(jnp.maximum(logs[0], logs[1]), jnp.maximum(logs[2], logs[3]))
            cols = slice(head * HEAD_SIZE, (head + 1) * HEAD_SIZE)
            mixed = jnp.zeros((HALF, HEAD_SIZE), jnp.float32)
            total = jnp.zeros((HALF, 1), jnp.float32)
            for part, log in zip(parts, logs):
                weight = jnp.exp(log - top)
                mixed = mixed + weight * part[:, cols]
                total = total + weight
            out[half * HALF : (half + 1) * HALF, cols] = (mixed / total).astype(jnp.bfloat16)


def exchange_heads(value):
    return lax.all_to_all(value, "heads", 0, 0, tiled=True)


def exchange_y(value):
    return lax.all_to_all(value, "ctx", 0, 0, tiled=True, axis_index_groups=Y_GROUPS)


def ctx_shift(value, steps):
    return lax.ppermute(value, "ctx", [(i, (i + steps) % N_CTX) for i in range(N_CTX)])


def shards(
    resid_in,
    first_layer_queries,
    first_layer_keys,
    first_layer_values,
    out_one,
    post_gain,
    pre_gain,
    proj_query,
    key_projection,
    value_projection,
    window,
    positions,
):
    ctx_place = lax.axis_index("ctx").astype(jnp.int32)
    place_z, place_y = ctx_place // Y_HI, ctx_place % Y_HI
    bf16, f32 = jnp.bfloat16, jnp.float32
    params = partial(pltpu.CompilerParams, vmem_limit_bytes=VMEM_LIMIT)
    first_params = pltpu.CompilerParams(vmem_limit_bytes=FIRST_LIMIT)
    norm_params = pltpu.CompilerParams(vmem_limit_bytes=NORM_LIMIT)
    project_params = pltpu.CompilerParams(vmem_limit_bytes=PROJECT_LIMIT)

    own, spread = pl.pallas_call(
        prepare_kernel,
        out_shape=(
            jax.ShapeDtypeStruct((TOK, 2 * HEAD_SIZE), bf16),
            jax.ShapeDtypeStruct((Y_HI, proj_query.shape[0], 4 * HEAD_SIZE), bf16),
        ),
        in_specs=[whole(pltpu.HBM)] * 5,
        out_specs=(whole(), whole(pltpu.HBM)),
        scratch_shapes=[
            pltpu.VMEM((proj_query.shape[0], 4 * HEAD_SIZE), bf16),
            pltpu.SemaphoreType.DMA((5,)),
            pltpu.SemaphoreType.DMA((Y_HI,)),
        ],
        name="prepare",
    )(first_layer_keys, first_layer_values, proj_query, key_projection, value_projection)
    back_one = ctx_shift(own, Y_HI)
    back_two = ctx_shift(own, 2 * Y_HI)
    weights = exchange_y(spread).reshape(-1, 4 * HEAD_SIZE)
    bases = jnp.stack([place_z, place_y, place_z // (Z // 2)])
    pieces = [weights]
    upward, downward = weights, weights
    for _ in range(1, Z // 2):
        upward = ctx_shift(upward, Y_HI)
        downward = ctx_shift(downward, -Y_HI)
        pieces += [upward, downward]
    half_rows = weights.shape[0] // 2
    upward, downward = upward[:half_rows], downward[half_rows:]
    upward = ctx_shift(upward, Y_HI)
    downward = ctx_shift(downward, -Y_HI)
    pieces += [upward, downward]

    later = jnp.concatenate([own, back_one], axis=0)
    earlier = jnp.concatenate([back_one, back_two], axis=0)
    peers = jnp.arange(Y_HI, dtype=jnp.int32)[:, None, None]
    window_blocks = jnp.where(peers >= place_y, later[None], earlier[None])
    blocks = exchange_y(window_blocks)

    start = ctx_place * TOK
    tokens = start + jnp.arange(TOK, dtype=jnp.int32)
    local_pos = lax.dynamic_slice_in_dim(positions, start, TOK, 0)
    low_one = jnp.maximum((tokens - local_pos)[None, :], tokens[None, :] - window[:, None] + 1)
    low_one = jnp.broadcast_to(low_one.reshape(2 * TOK, 1), (2 * TOK, 128))
    sent = pl.pallas_call(
        first_kernel,
        out_shape=jax.ShapeDtypeStruct((N_HEADS, ROWS, SLAB), bf16),
        in_specs=[whole(pltpu.SMEM)] + [whole()] * 6,
        out_specs=whole(),
        scratch_shapes=[pltpu.VMEM((2 * TOK, 9 * TOK), f32)],
        compiler_params=first_params,
        cost_estimate=pl.CostEstimate(
            flops=600_000_000, bytes_accessed=6_000_000, transcendentals=300_000
        ),
        name="first_layer",
    )(
        bases,
        first_layer_queries,
        blocks,
        back_two,
        low_one,
        out_one,
        resid_in,
    )
    got = exchange_heads(sent)
    sent = pl.pallas_call(
        norm_kernel,
        out_shape=jax.ShapeDtypeStruct((N_HEADS, ROWS, SLAB), bf16),
        in_specs=[whole()] * 3,
        out_specs=whole(),
        scratch_shapes=[pltpu.VMEM((ROWS, WIDTH), f32)] * 2,
        compiler_params=norm_params,
        name="norms",
    )(got, post_gain[None, :], pre_gain[None, :])
    got = exchange_heads(sent)
    resid_out = got[:, :, WIDTH : WIDTH + COLS].reshape(TOK, COLS)

    speeds = THETA ** (-(jnp.arange(HALF, dtype=f32) * 2.0 / HEAD_SIZE))
    angles = (local_pos.astype(f32) * POSITION_FACTOR)[:, None] * speeds[None, :]
    cosine, sine = jnp.cos(angles), jnp.sin(angles)
    turn_cos = jnp.concatenate([cosine, cosine], axis=1)
    turn_sin = jnp.concatenate([-sine, sine], axis=1)
    query, pair = pl.pallas_call(
        project_kernel,
        out_shape=(
            jax.ShapeDtypeStruct((TOK, 2 * HEAD_SIZE), bf16),
            jax.ShapeDtypeStruct((Z, TOK, 2 * HEAD_SIZE), bf16),
        ),
        in_specs=[whole(pltpu.SMEM)] + [whole(pltpu.HBM)] * (Z + 2) + [whole(), whole()],
        out_specs=(whole(), whole(pltpu.HBM)),
        scratch_shapes=[
            pltpu.VMEM((WIDTH, 4 * HEAD_SIZE), bf16),
            pltpu.VMEM((N_HEADS, ROWS, WIDTH), bf16),
            pltpu.VMEM((TOK, 2 * HEAD_SIZE), bf16),
            pltpu.SemaphoreType.DMA((Z,)),
            pltpu.SemaphoreType.DMA((PARTS,)),
            pltpu.SemaphoreType.DMA((Z,)),
        ],
        compiler_params=project_params,
        name="project",
    )(bases, got, *pieces, turn_cos, turn_sin)

    pairs = lax.all_to_all(pair, "ctx", 0, 0, tiled=True, axis_index_groups=Z_GROUPS)
    pairs = pairs.reshape(Z * TOK, 2 * HEAD_SIZE)
    queries = lax.all_gather(
        query, "ctx", axis=0, tiled=True, axis_index_groups=Y_GROUPS
    )

    level = Y_HI * TOK
    first = place_z * level
    low_two = first + jnp.arange(level, dtype=jnp.int32)
    low_two = low_two - lax.dynamic_slice_in_dim(positions, first, level, 0)
    low_two = jnp.broadcast_to(low_two[:, None], (level, 128))
    sent = pl.pallas_call(
        second_kernel,
        out_shape=jax.ShapeDtypeStruct((2 * Y_HI, HALF, 3 * HEAD_SIZE), bf16),
        in_specs=[whole(pltpu.SMEM)] + [whole()] * 3,
        out_specs=whole(),
        scratch_shapes=[pltpu.VMEM((2 * TOK, Z * TOK), f32)],
        compiler_params=params(),
        name="second_layer",
    )(bases, queries, pairs, low_two)
    got = lax.all_to_all(sent, "ctx", 0, 0, tiled=True, axis_index_groups=LEVEL_PAIRS)
    attended = pl.pallas_call(
        combine_kernel,
        out_shape=jax.ShapeDtypeStruct((TOK, 2 * HEAD_SIZE), bf16),
        in_specs=[whole(pltpu.SMEM), whole()],
        out_specs=whole(),
        compiler_params=params(),
        name="combine",
    )(bases, got)
    return (resid_out, attended)


def solution(mesh):
    placed = (
        P("ctx", "heads"),
        P("ctx", "heads"),
        P("ctx", "heads"),
        P("ctx", "heads"),
        P("heads", None),
        P(),
        P(),
        P("ctx", "heads"),
        P("ctx", "heads"),
        P("ctx", "heads"),
        P("heads"),
        P(),
    )
    return jax.shard_map(
        shards,
        mesh=mesh,
        in_specs=placed,
        out_specs=(P("ctx", "heads"), P("ctx", "heads")),
        check_vma=False,
    )
```

```python
from functools import partial

import jax
import jax.numpy as jnp
from jax import lax
from jax.experimental import pallas as pl
from jax.experimental.pallas import tpu as pltpu
from jax.sharding import PartitionSpec as P


HEAD_SIZE = 128
SCALE = 168.0 ** (-0.5)
EPS = 1e-06
THETA = 1000000.0
POSITION_FACTOR = 0.125
N_CTX = 32
N_HEADS = 16
Y_HI = 4
Z = 8
TOK = 128
HALF = 64
WIDTH = 5376
COLS = WIDTH // N_HEADS
SLAB = 5760
ROWS = TOK // N_HEADS
NEG = -1e30
Y_GROUPS = [[z * Y_HI + y for y in range(Y_HI)] for z in range(Z)]
LEVEL_PAIRS = [
    [z * Y_HI + y for y in range(Y_HI)] + [(Z - 1 - z) * Y_HI + y for y in range(Y_HI)]
    for z in range(Z // 2)
]
Z_GROUPS = [[z * Y_HI + y for z in range(Z)] for y in range(Y_HI)]
VMEM_LIMIT = 24 * 1024 * 1024
FIRST_LIMIT = 24 * 1024 * 1024
NORM_LIMIT = 24 * 1024 * 1024
PROJECT_LIMIT = 50 * 1024 * 1024


def whole(memory_space=pltpu.VMEM):
    return pl.BlockSpec(memory_space=memory_space)


def fold_max(peak, part):
    for lane in range(0, part.shape[1], 128):
        peak = jnp.maximum(peak, part[:, lane : lane + 128])
    return peak


def fold_sum(total, part):
    for lane in range(0, part.shape[1], 128):
        total = total + part[:, lane : lane + 128]
    return total


def softmax_rows(query, chunks, low, high, scores):
    rows = query.shape[0]
    peak = jnp.full((rows, 128), NEG, jnp.float32)
    offset = 0
    for load, tokens in chunks:
        keys, _ = load()
        part = (
            lax.dot_general(
                query, keys, (((1,), (1,)), ((), ())), preferred_element_type=jnp.float32
            )
            * SCALE
        )
        width = part.shape[1]
        seen = (tokens >= low) & (tokens <= high)
        part = jnp.where(seen, part, NEG)
        scores[:, offset : offset + width] = part
        peak = fold_max(peak, part)
        offset += width
    top = jnp.max(peak, axis=1, keepdims=True)
    total = jnp.zeros((rows, 128), jnp.float32)
    mixed = jnp.zeros((rows, HEAD_SIZE), jnp.float32)
    offset = 0
    for load, tokens in chunks:
        _, values = load()
        width = values.shape[0]
        lifted = jnp.exp(scores[:, offset : offset + width] - top)
        total = fold_sum(total, lifted)
        mixed = mixed + jnp.dot(
            lifted.astype(jnp.bfloat16), values, preferred_element_type=jnp.float32
        )
        offset += width
    total = jnp.sum(total, axis=1, keepdims=True)
    return mixed / total, top + jnp.log(total)


def first_kernel(base, query, blocks, last, low, out_one, resid, sent, scores):
    place_z, place_y = base[0], base[1]
    start = (place_z * Y_HI + place_y) * TOK
    stacked = jnp.concatenate([query[:, :HEAD_SIZE], query[:, HEAD_SIZE:]], axis=0)
    lowest = low[...][:, :1]
    row = lax.broadcasted_iota(jnp.int32, (2 * TOK, 1), 0)
    high = start + lax.rem(row, TOK)
    lane = lax.broadcasted_iota(jnp.int32, (1, 2 * TOK), 1)
    pair = jnp.where(lane < TOK, lane, lane - (TOK + Y_HI * TOK))
    chunks = []
    for peer in range(Y_HI):
        newer = (place_z - jnp.where(peer > place_y, 1, 0)) * (Y_HI * TOK) + peer * TOK
        chunks.append(
            (
                lambda peer=peer: (
                    blocks[peer, :, :HEAD_SIZE],
                    blocks[peer, :, HEAD_SIZE:],
                ),
                newer + pair,
            )
        )
    chunks.append(
        (
            lambda: (last[:, :HEAD_SIZE], last[:, HEAD_SIZE:]),
            start - 2 * Y_HI * TOK + lane[:, :TOK],
        )
    )
    mixed, _ = softmax_rows(stacked, chunks, lowest, high, scores)
    mixed = mixed.astype(jnp.bfloat16)
    attend = jnp.concatenate([mixed[:TOK], mixed[TOK:]], axis=1)
    step = 768
    for col in range(0, WIDTH, step):
        part = jnp.dot(attend, out_one[:, col : col + step], preferred_element_type=jnp.float32)
        sent[:, :, col : col + step] = part.reshape(N_HEADS, ROWS, step).astype(jnp.bfloat16)
    own = resid[...].astype(jnp.float32).reshape(N_HEADS, ROWS, COLS)
    sent[:, :, WIDTH : WIDTH + COLS] = own.astype(jnp.bfloat16)
    sent[:, :, WIDTH + COLS :] = jnp.zeros((N_HEADS, ROWS, SLAB - WIDTH - COLS), jnp.bfloat16)


def norm_kernel(got, post_gain, pre_gain, sent, rows, wide):
    combined = got[0, :, :WIDTH].astype(jnp.float32)
    for peer in range(1, N_HEADS):
        combined = combined + got[peer, :, :WIDTH].astype(jnp.float32)
    for peer in range(N_HEADS):
        rows[:, peer * COLS : (peer + 1) * COLS] = got[peer, :, WIDTH : WIDTH + COLS].astype(
            jnp.float32
        )
    scale = lax.rsqrt(jnp.mean(combined * combined, axis=1, keepdims=True) + EPS)
    resid = (rows[...] + post_gain[...] * (combined * scale)).astype(jnp.bfloat16)
    widened = resid.astype(jnp.float32)
    scale = lax.rsqrt(jnp.mean(widened * widened, axis=1, keepdims=True) + EPS)
    normed = (pre_gain[...] * widened * scale).astype(jnp.bfloat16)
    wide[...] = widened
    for peer in range(N_HEADS):
        sent[peer, :, :WIDTH] = normed
        sent[peer, :, WIDTH : WIDTH + COLS] = wide[:, peer * COLS : (peer + 1) * COLS].astype(
            jnp.bfloat16
        )
        sent[peer, :, WIDTH + COLS :] = jnp.zeros((ROWS, SLAB - WIDTH - COLS), jnp.bfloat16)


def prepare_kernel(
    keys, values, proj_query, key_projection, value_projection, own, spread, joined, in_sem, out_sem
):
    width = HEAD_SIZE
    moves = [
        pltpu.make_async_copy(source, target, in_sem.at[index])
        for index, (source, target) in enumerate(
            (
                (proj_query, joined.at[:, : 2 * width]),
                (key_projection, joined.at[:, 2 * width : 3 * width]),
                (value_projection, joined.at[:, 3 * width :]),
                (keys, own.at[:, :width]),
                (values, own.at[:, width:]),
            )
        )
    ]
    for move in moves:
        move.start()
    for move in moves[:3]:
        move.wait()
    copies = [
        pltpu.make_async_copy(joined, spread.at[peer], out_sem.at[peer]) for peer in range(Y_HI)
    ]
    for move in copies:
        move.start()
    for move in moves[3:] + copies:
        move.wait()


def project_kernel(base, got, *refs):
    pieces, refs = refs[:Z], refs[Z:]
    turn_cos, turn_sin, query, pair, held, block, in_sem, out_sem = refs
    level_rows = WIDTH // Z
    depth = WIDTH // PARTS
    offsets = [0, -1, -2, -3, -4, 1, 2, 3]

    piece_of = {offset % Z: piece for piece, offset in zip(pieces, offsets)}
    for place in range(Z):

        @pl.when(base[0] == place)
        def _(place=place):
            for level in range(Z):
                target = held.at[level * level_rows : (level + 1) * level_rows]
                piece = piece_of[(level - place) % Z]
                pltpu.make_async_copy(piece, target, in_sem.at[level]).start()

    total = jnp.zeros((TOK, 4 * HEAD_SIZE), jnp.float32)
    arrived = 0
    for part in range(PARTS):
        span = slice(part * depth, (part + 1) * depth)
        rows = got[:, :, span].astype(jnp.float32).reshape(TOK, depth).astype(jnp.bfloat16)
        while arrived * level_rows < (part + 1) * depth:
            rows_of = slice(arrived * level_rows, (arrived + 1) * level_rows)
            pltpu.make_async_copy(pieces[0], held.at[rows_of], in_sem.at[arrived]).wait()
            arrived += 1
        total = total + jnp.dot(rows, held[span, :], preferred_element_type=jnp.float32)
    for head in range(4):
        values = total[:, head * HEAD_SIZE : (head + 1) * HEAD_SIZE]
        if head < 3:
            values = values * turn_cos[...] + pltpu.roll(values, HALF, 1) * turn_sin[...]
        values = values.astype(jnp.bfloat16)
        if head < 2:
            query[:, head * HEAD_SIZE : (head + 1) * HEAD_SIZE] = values
        else:
            block[:, (head - 2) * HEAD_SIZE : (head - 1) * HEAD_SIZE] = values
    moves = [pltpu.make_async_copy(block, pair.at[member], out_sem.at[member]) for member in range(Z)]
    for move in moves:
        move.start()
    for move in moves:
        move.wait()


CHUNK = 256
PARTS = 7


def three_terms(values):
    terms = []
    for _ in range(3):
        term = values.astype(jnp.bfloat16).astype(jnp.float32)
        terms.append(term)
        values = values - term
    return terms


def second_kernel(base, queries, pair, low, sent, scores):
    place_z, place_y, upper = base[0], base[1], base[2]
    lane = lax.broadcasted_iota(jnp.int32, (1, CHUNK), 1)
    lane = jnp.where(lane < TOK, lane, lane + (Y_HI - 1) * TOK)
    row = lax.broadcasted_iota(jnp.int32, (2 * TOK, 1), 0)
    slot = lax.broadcasted_iota(jnp.int32, (TOK, HEAD_SIZE), 1)
    chunks = []
    for at in range(0, Z * TOK, CHUNK):
        chunks.append(
            (
                lambda at=at: (pair[at : at + CHUNK, :HEAD_SIZE], pair[at : at + CHUNK, HEAD_SIZE:]),
                at * Y_HI + place_y * TOK + lane,
            )
        )
    for peer in range(Y_HI):
        block = queries[peer * TOK : (peer + 1) * TOK, :]
        stacked = jnp.concatenate([block[:, :HEAD_SIZE], block[:, HEAD_SIZE:]], axis=0)
        lowest = low[peer * TOK : (peer + 1) * TOK, :1]
        lowest = jnp.concatenate([lowest, lowest], axis=0)
        high = (place_z * Y_HI + peer) * TOK + lax.rem(row, TOK)
        mixed, logs = softmax_rows(stacked, chunks, lowest, high, scores)
        packed = jnp.zeros((TOK, HEAD_SIZE), jnp.float32)
        pieces = []
        for head in range(2):
            rows = slice(head * TOK, (head + 1) * TOK)
            pieces.append(mixed[rows])
            for place, term in enumerate(three_terms(logs[rows])):
                packed = jnp.where(slot == 3 * head + place, term, packed)
        whole_rows = jnp.concatenate(pieces + [packed], axis=1).astype(jnp.bfloat16)
        sent[peer + Y_HI * upper] = whole_rows[:HALF]
        sent[Y_HI - 1 - peer + Y_HI * (1 - upper)] = whole_rows[HALF:]


def combine_kernel(base, got, out):
    for half in range(2):
        upper = base[2] if half == 0 else 1 - base[2]
        parts = [got[peer + Y_HI * upper].astype(jnp.float32) for peer in range(Y_HI)]
        for head in range(2):
            at = 2 * HEAD_SIZE + 3 * head
            logs = [
                part[:, at : at + 1] + part[:, at + 1 : at + 2] + part[:, at + 2 : at + 3]
                for part in parts
            ]
            top = jnp.maximum(jnp.maximum(logs[0], logs[1]), jnp.maximum(logs[2], logs[3]))
            cols = slice(head * HEAD_SIZE, (head + 1) * HEAD_SIZE)
            mixed = jnp.zeros((HALF, HEAD_SIZE), jnp.float32)
            total = jnp.zeros((HALF, 1), jnp.float32)
            for part, log in zip(parts, logs):
                weight = jnp.exp(log - top)
                mixed = mixed + weight * part[:, cols]
                total = total + weight
            out[half * HALF : (half + 1) * HALF, cols] = (mixed / total).astype(jnp.bfloat16)


def exchange_heads(value):
    return lax.all_to_all(value, "heads", 0, 0, tiled=True)


def exchange_y(value):
    return lax.all_to_all(value, "ctx", 0, 0, tiled=True, axis_index_groups=Y_GROUPS)


def ctx_shift(value, steps):
    return lax.ppermute(value, "ctx", [(i, (i + steps) % N_CTX) for i in range(N_CTX)])


def shards(
    resid_in,
    first_layer_queries,
    first_layer_keys,
    first_layer_values,
    out_one,
    post_gain,
    pre_gain,
    proj_query,
    key_projection,
    value_projection,
    window,
    positions,
):
    ctx_place = lax.axis_index("ctx").astype(jnp.int32)
    place_z, place_y = ctx_place // Y_HI, ctx_place % Y_HI
    bf16, f32 = jnp.bfloat16, jnp.float32
    params = partial(pltpu.CompilerParams, vmem_limit_bytes=VMEM_LIMIT)
    first_params = pltpu.CompilerParams(vmem_limit_bytes=FIRST_LIMIT)
    norm_params = pltpu.CompilerParams(vmem_limit_bytes=NORM_LIMIT)
    project_params = pltpu.CompilerParams(vmem_limit_bytes=PROJECT_LIMIT)

    own, spread = pl.pallas_call(
        prepare_kernel,
        out_shape=(
            jax.ShapeDtypeStruct((TOK, 2 * HEAD_SIZE), bf16),
            jax.ShapeDtypeStruct((Y_HI, proj_query.shape[0], 4 * HEAD_SIZE), bf16),
        ),
        in_specs=[whole(pltpu.HBM)] * 5,
        out_specs=(whole(), whole(pltpu.HBM)),
        scratch_shapes=[
            pltpu.VMEM((proj_query.shape[0], 4 * HEAD_SIZE), bf16),
            pltpu.SemaphoreType.DMA((5,)),
            pltpu.SemaphoreType.DMA((Y_HI,)),
        ],
        name="prepare",
    )(first_layer_keys, first_layer_values, proj_query, key_projection, value_projection)
    back_one = ctx_shift(own, Y_HI)
    back_two = ctx_shift(own, 2 * Y_HI)
    weights = exchange_y(spread).reshape(-1, 4 * HEAD_SIZE)
    bases = jnp.stack([place_z, place_y, place_z // (Z // 2)])
    pieces = [weights]
    for count, sign in ((Z // 2, 1), (Z // 2 - 1, -1)):
        piece = weights
        for _ in range(1, count + 1):
            piece = ctx_shift(piece, sign * Y_HI)
            pieces.append(piece)
    pieces = [pltpu.with_memory_space_constraint(piece, pltpu.HBM) for piece in pieces]

    later = jnp.concatenate([own, back_one], axis=0)
    earlier = jnp.concatenate([back_one, back_two], axis=0)
    peers = jnp.arange(Y_HI, dtype=jnp.int32)[:, None, None]
    window_blocks = jnp.where(peers >= place_y, later[None], earlier[None])
    blocks = exchange_y(window_blocks)

    start = ctx_place * TOK
    tokens = start + jnp.arange(TOK, dtype=jnp.int32)
    local_pos = lax.dynamic_slice_in_dim(positions, start, TOK, 0)
    low_one = jnp.maximum((tokens - local_pos)[None, :], tokens[None, :] - window[:, None] + 1)
    low_one = jnp.broadcast_to(low_one.reshape(2 * TOK, 1), (2 * TOK, 128))
    sent = pl.pallas_call(
        first_kernel,
        out_shape=jax.ShapeDtypeStruct((N_HEADS, ROWS, SLAB), bf16),
        in_specs=[whole(pltpu.SMEM)] + [whole()] * 6,
        out_specs=whole(),
        scratch_shapes=[pltpu.VMEM((2 * TOK, 9 * TOK), f32)],
        compiler_params=first_params,
        cost_estimate=pl.CostEstimate(
            flops=600_000_000, bytes_accessed=6_000_000, transcendentals=300_000
        ),
        name="first_layer",
    )(
        bases,
        first_layer_queries,
        blocks,
        back_two,
        low_one,
        out_one,
        resid_in,
    )
    got = exchange_heads(sent)
    sent = pl.pallas_call(
        norm_kernel,
        out_shape=jax.ShapeDtypeStruct((N_HEADS, ROWS, SLAB), bf16),
        in_specs=[whole()] * 3,
        out_specs=whole(),
        scratch_shapes=[pltpu.VMEM((ROWS, WIDTH), f32)] * 2,
        compiler_params=norm_params,
        name="norms",
    )(got, post_gain[None, :], pre_gain[None, :])
    got = exchange_heads(sent)
    resid_out = got[:, :, WIDTH : WIDTH + COLS].reshape(TOK, COLS)

    speeds = THETA ** (-(jnp.arange(HALF, dtype=f32) * 2.0 / HEAD_SIZE))
    angles = (local_pos.astype(f32) * POSITION_FACTOR)[:, None] * speeds[None, :]
    cosine, sine = jnp.cos(angles), jnp.sin(angles)
    turn_cos = jnp.concatenate([cosine, cosine], axis=1)
    turn_sin = jnp.concatenate([-sine, sine], axis=1)
    query, pair = pl.pallas_call(
        project_kernel,
        out_shape=(
            jax.ShapeDtypeStruct((TOK, 2 * HEAD_SIZE), bf16),
            jax.ShapeDtypeStruct((Z, TOK, 2 * HEAD_SIZE), bf16),
        ),
        in_specs=[whole(pltpu.SMEM), whole()] + [whole(pltpu.HBM)] * Z + [whole(), whole()],
        out_specs=(whole(), whole(pltpu.HBM)),
        scratch_shapes=[
            pltpu.VMEM((WIDTH, 4 * HEAD_SIZE), bf16),
            pltpu.VMEM((TOK, 2 * HEAD_SIZE), bf16),
            pltpu.SemaphoreType.DMA((Z,)),
            pltpu.SemaphoreType.DMA((Z,)),
        ],
        compiler_params=project_params,
        name="project",
    )(bases, got, *pieces, turn_cos, turn_sin)

    pairs = lax.all_to_all(pair, "ctx", 0, 0, tiled=True, axis_index_groups=Z_GROUPS)
    pairs = pairs.reshape(Z * TOK, 2 * HEAD_SIZE)
    queries = lax.all_gather(
        query, "ctx", axis=0, tiled=True, axis_index_groups=Y_GROUPS
    )

    level = Y_HI * TOK
    first = place_z * level
    low_two = first + jnp.arange(level, dtype=jnp.int32)
    low_two = low_two - lax.dynamic_slice_in_dim(positions, first, level, 0)
    low_two = jnp.broadcast_to(low_two[:, None], (level, 128))
    sent = pl.pallas_call(
        second_kernel,
        out_shape=jax.ShapeDtypeStruct((2 * Y_HI, HALF, 3 * HEAD_SIZE), bf16),
        in_specs=[whole(pltpu.SMEM)] + [whole()] * 3,
        out_specs=whole(),
        scratch_shapes=[pltpu.VMEM((2 * TOK, Z * TOK), f32)],
        compiler_params=params(),
        name="second_layer",
    )(bases, queries, pairs, low_two)
    got = lax.all_to_all(sent, "ctx", 0, 0, tiled=True, axis_index_groups=LEVEL_PAIRS)
    attended = pl.pallas_call(
        combine_kernel,
        out_shape=jax.ShapeDtypeStruct((TOK, 2 * HEAD_SIZE), bf16),
        in_specs=[whole(pltpu.SMEM), whole()],
        out_specs=whole(),
        compiler_params=params(),
        name="combine",
    )(bases, got)
    return (resid_out, attended)


def solution(mesh):
    placed = (
        P("ctx", "heads"),
        P("ctx", "heads"),
        P("ctx", "heads"),
        P("ctx", "heads"),
        P("heads", None),
        P(),
        P(),
        P("ctx", "heads"),
        P("ctx", "heads"),
        P("ctx", "heads"),
        P("heads"),
        P(),
    )
    return jax.shard_map(
        shards,
        mesh=mesh,
        in_specs=placed,
        out_specs=(P("ctx", "heads"), P("ctx", "heads")),
        check_vma=False,
    )
```
